32 devices in a mesh: fsdp: 8 (over z, x), tp: 4 (over y, core).
Axes of the slice: x: 2, y: 2, z: 4, core: 2. Of those that a mesh axis runs over, the one named last changes fastest.
Arguments:
- tokens: bfloat16 [8, 2048, 768], P('fsdp', 'tp'), may hold values from -6 to 6
- lengths: int32 [8, 4], P('fsdp'), may hold values from 288 to 1024, as said below
- pictures: int32 [8, 2048], P('fsdp'), may hold values from 0 to 3, as said below
- w_query: bfloat16 [768, 768], P('fsdp', 'tp'), may hold values from -0.21875 to 0.21875
- w_key: bfloat16 [768, 768], P('fsdp', 'tp'), may hold values from -0.21875 to 0.21875
- w_value: bfloat16 [768, 768], P('fsdp', 'tp'), may hold values from -0.21875 to 0.21875
- w_out: bfloat16 [768, 768], P('tp', 'fsdp'), may hold values from -0.875 to 0.875
- w_up: bfloat16 [768, 3072], P('fsdp', 'tp'), may hold values from -0.21875 to 0.21875
- w_down: bfloat16 [3072, 768], P('tp', 'fsdp'), may hold values from -0.15625 to 0.15625
- norm1_gain: float32 [768], P(('fsdp', 'tp')), may hold values from 0.5 to 1.5
- norm1_shift: float32 [768], P(('fsdp', 'tp')), may hold values from -1.75 to 1.75
- norm2_gain: float32 [768], P(('fsdp', 'tp')), may hold values from 0.5 to 1.5
- norm2_shift: float32 [768], P(('fsdp', 'tp')), may hold values from -1.75 to 1.75
- query_gain: float32 [768], P(('fsdp', 'tp')), may hold values from 1 to 2
- key_gain: float32 [768], P(('fsdp', 'tp')), may hold values from 1 to 2
- cotangent: bfloat16 [8, 2048, 768], P('fsdp', 'tp'), may hold values from -6 to 6
Outputs:
- layer_out: bfloat16 [8, 2048, 768], P('fsdp', 'tp')
- input_grad: float32 [8, 2048, 768], P('fsdp', 'tp')
- grad_query: float32 [768, 768], P('fsdp', 'tp')
- grad_key: float32 [768, 768], P('fsdp', 'tp')
- grad_value: float32 [768, 768], P('fsdp', 'tp')
- grad_output_proj: float32 [768, 768], P('tp', 'fsdp')
- grad_up: float32 [768, 3072], P('fsdp', 'tp')
- grad_down: float32 [3072, 768], P('tp', 'fsdp')
- grad_norm1_gain: float32 [768], P(('fsdp', 'tp'))
- grad_norm1_shift: float32 [768], P(('fsdp', 'tp'))
- grad_norm2_gain: float32 [768], P(('fsdp', 'tp'))
- grad_norm2_shift: float32 [768], P(('fsdp', 'tp'))
- grad_query_gain: float32 [768], P(('fsdp', 'tp'))
- grad_key_gain: float32 [768], P(('fsdp', 'tp'))
- statistics: float32 [4], replicated
The draws below stay inside these ranges and needn't reach their ends.
Inputs may be any that keep to these rules, and one draw needn't show every extreme that they name: The lengths of a row sum to at most 2048; one picture of every row has exactly 1024 patches. Slots of a row carry the pictures in order, each picture covering as many slots as its length; slots after the row's total length repeat the last picture's number.
All inputs are finite; a program needn't handle non-finite values.
Results may differ from the reference program's by a relative error of at most 0.018.
Values may be sent and summed in bfloat16 or wider, within the bound.
A program may use at most 192 MiB of HBM per device.

```python
import jax
import jax.numpy as jnp
from jax import lax

D = 768
H = 12
HD = 64
FF = 3072
L = 2048
PICS = 4
ROWS = 8


def picture_layout(key):
    base = jax.random.fold_in(key, 11)
    other_key = jax.random.fold_in(base, 1)
    place_key = jax.random.fold_in(base, 2)
    others = jax.random.randint(other_key, (ROWS, PICS), L * 9 // 64, L // 6 + 1)
    largest = jax.random.randint(place_key, (ROWS, 1), 0, PICS)
    slots = jnp.arange(PICS, dtype=jnp.int32)[None, :]
    lengths = jnp.where(slots == largest, L // 2, others).astype(jnp.int32)
    ends = jnp.cumsum(lengths, axis=1)
    positions = jnp.arange(L, dtype=jnp.int32)
    covered = jnp.sum((positions[None, :, None] >= ends[:, None, :]).astype(jnp.int32), axis=2)
    pictures = jnp.minimum(covered, PICS - 1).astype(jnp.int32)
    return (lengths, pictures)


def draw_lengths(key, part):
    return picture_layout(key)[0]


def draw_pictures(key, part):
    return picture_layout(key)[1]


def draw_tokens(key, part):
    scales = 0.5 + jnp.arange(ROWS, dtype=jnp.float32) / max(ROWS - 1, 1)
    sampled = jnp.clip(jax.random.normal(key, (ROWS, L, D), jnp.float32), -4.0, 4.0)
    return (sampled * scales[:, None, None]).astype(jnp.bfloat16)


def levels(stream_key, shape, split, smallest, top_value):
    gain = 1.0
    for dim, shards_of in split:
        draws = jax.random.uniform(jax.random.fold_in(jax.random.fold_in(stream_key, 6), dim), (shards_of,), jnp.float32, smallest / len(split), top_value / len(split))
        gain = gain * jnp.repeat(jnp.exp(draws), shape[dim] // shards_of).reshape((-1,) + (1,) * (len(shape) - 1 - dim))
    return gain


def noise(own_key, shape, scale, limit, pieces=(), kind=jnp.bfloat16):
    drawn = scale * jax.random.normal(own_key, shape, jnp.float32)
    if pieces:
        drawn = drawn * levels(own_key, shape, pieces, -0.22, 0.18)
    return jnp.clip(drawn, -limit, limit).astype(kind)


def setup_inputs(seed: int = 0) -> dict:
    streams_of = jax.random.split(jax.random.key(seed), 17)
    tokens = draw_tokens(jax.random.fold_in(streams_of[16], 71), 0)
    lengths = draw_lengths(jax.random.fold_in(streams_of[16], 71), 0)
    pictures = draw_pictures(jax.random.fold_in(streams_of[16], 71), 0)
    w_query = noise(streams_of[3], (D, D), D ** -0.5, 0.21875, ((0, 8), (1, 4)))
    w_key = noise(streams_of[4], (D, D), D ** -0.5, 0.21875, ((0, 8), (1, 4)))
    w_value = noise(streams_of[5], (D, D), D ** -0.5, 0.21875, ((0, 8), (1, 4)))
    w_out = noise(streams_of[6], (D, D), (D // 16) ** -0.5, 0.875, ((0, 4), (1, 8)))
    w_up = noise(streams_of[7], (D, FF), D ** -0.5, 0.21875, ((0, 8), (1, 4)))
    w_down = noise(streams_of[8], (FF, D), (FF // 2) ** -0.5, 0.15625, ((0, 4), (1, 8)))
    norm1_gain = jnp.clip(1.0 + 0.1 * jax.random.normal(streams_of[9], (D,), jnp.float32), 0.5, 1.5)
    norm1_shift = noise(streams_of[10], (D,), 0.3, 1.75, ((0, 32),), jnp.float32)
    norm2_gain = jnp.clip(1.0 + 0.1 * jax.random.normal(streams_of[11], (D,), jnp.float32), 0.5, 1.5)
    norm2_shift = noise(streams_of[12], (D,), 0.3, 1.75, ((0, 32),), jnp.float32)
    query_gain = jnp.clip(1.0 + 1.0 * jax.random.uniform(streams_of[13], (D,), jnp.float32) ** levels(streams_of[13], (D,), ((0, 32),), -0.2, 0.2), 1.0, 2.0)
    key_gain = jnp.clip(1.0 + 1.0 * jax.random.uniform(streams_of[14], (D,), jnp.float32) ** levels(streams_of[14], (D,), ((0, 32),), -0.2, 0.2), 1.0, 2.0)
    cotangent = noise(streams_of[15], (ROWS, L, D), 1.0, 6.0, ((0, 8), (1, 4)))
    return dict(tokens=tokens, lengths=lengths, pictures=pictures, w_query=w_query, w_key=w_key, w_value=w_value, w_out=w_out, w_up=w_up, w_down=w_down, norm1_gain=norm1_gain, norm1_shift=norm1_shift, norm2_gain=norm2_gain, norm2_shift=norm2_shift, query_gain=query_gain, key_gain=key_gain, cotangent=cotangent)


EPS = 1e-06

@jax.custom_vjp
def low(v):
    return lax.optimization_barrier(v.astype(jnp.bfloat16)).astype(jnp.float32)

@jax.custom_vjp
def low_back(v):
    return v

def low_keep(v):
    return (low(v), None)

def low_pass(kept, grad):
    return (grad,)

def back_keep(v):
    return (v, None)

def back_low(kept, grad):
    return (low(grad),)
low.defvjp(low_keep, low_pass)
low_back.defvjp(back_keep, back_low)

def matmul(left, right):
    return jnp.dot(left, right, precision=lax.Precision.HIGHEST)

def layer_norm(values, scaling, offset):
    centre = lax.optimization_barrier(jnp.mean(values, axis=-1, keepdims=True))
    centred = values - centre
    spread = lax.optimization_barrier(jnp.mean(centred * centred, axis=-1, keepdims=True))
    return centred * lax.rsqrt(spread + EPS) * scaling + offset

def attend(query, keyed, valued, allowed):
    raw_scores = matmul(query, keyed.T)
    scores = low_back(raw_scores * HD ** (-0.5))
    scores = jnp.where(allowed, scores, -1e+30)
    probability = low(jax.nn.softmax(scores, axis=-1))
    return matmul(probability, valued)

def row_layer(inputs, lengths_row, pictures_row, params):
    w_query, w_key, w_value, w_out, w_up, w_down, norm1_gain, norm1_shift, norm2_gain, norm2_shift, query_gain, key_gain = params
    valid_mask = (jnp.arange(L, dtype=jnp.int32) < jnp.sum(lengths_row)).astype(jnp.float32)[:, None]
    hidden = low(layer_norm(inputs, norm1_gain, norm1_shift))
    query = low_back(matmul(hidden, w_query))
    keyed = low_back(matmul(hidden, w_key))
    valued = low(low_back(matmul(hidden, w_value)))
    query_heads = low(layer_norm(query.reshape(L, H, HD), query_gain.reshape(H, HD), 0.0))
    key_heads = low(layer_norm(keyed.reshape(L, H, HD), key_gain.reshape(H, HD), 0.0))
    value_heads = valued.reshape(L, H, HD)
    allowed = (pictures_row[:, None] == pictures_row[None, :]) & (valid_mask[:, 0][None, :] > 0)

    def one_head(packed):
        return jax.checkpoint(attend)(packed[0], packed[1], packed[2], allowed)
    mixture = lax.map(one_head, (jnp.transpose(query_heads, (1, 0, 2)), jnp.transpose(key_heads, (1, 0, 2)), jnp.transpose(value_heads, (1, 0, 2))))
    mixture = jnp.transpose(mixture, (1, 0, 2)).reshape(L, D)
    mixture = low(low_back(mixture))
    attn_branch = valid_mask * low_back(matmul(mixture, w_out))
    middle = inputs + attn_branch
    hidden_two = low(layer_norm(middle, norm2_gain, norm2_shift))
    up_value = low_back(matmul(hidden_two, w_up))
    activated = low(jax.nn.gelu(up_value, approximate=False))
    mlp_branch = valid_mask * low_back(matmul(activated, w_down))
    output = middle + mlp_branch
    square_sums = jnp.stack([jnp.sum(valid_mask * inputs * inputs), jnp.sum(attn_branch * attn_branch), jnp.sum(valid_mask * middle * middle), jnp.sum(mlp_branch * mlp_branch)])
    return (output, square_sums)

def reference(tokens, lengths, pictures, w_query, w_key, w_value, w_out, w_up, w_down, norm1_gain, norm1_shift, norm2_gain, norm2_shift, query_gain, key_gain, cotangent):
    inputs = tokens.astype(jnp.float32)
    params = (w_query.astype(jnp.float32), w_key.astype(jnp.float32), w_value.astype(jnp.float32), w_out.astype(jnp.float32), w_up.astype(jnp.float32), w_down.astype(jnp.float32), norm1_gain.astype(jnp.float32), norm1_shift.astype(jnp.float32), norm2_gain.astype(jnp.float32), norm2_shift.astype(jnp.float32), query_gain.astype(jnp.float32), key_gain.astype(jnp.float32))

    def forward(inputs_all, params_all):

        def step(running, packed):
            row_out, row_sums = jax.checkpoint(row_layer)(packed[0], packed[1], packed[2], params_all)
            return (running, (row_out, row_sums))
        final, stacked = lax.scan(step, jnp.zeros((), jnp.float32), (inputs_all, lengths, pictures))
        return (stacked[0], stacked[1])
    outputs, vjp_fn, square_sums = jax.vjp(forward, inputs, params, has_aux=True)
    valid_full = (jnp.arange(L, dtype=jnp.int32)[None, :] < lax.optimization_barrier(jnp.sum(lengths, axis=1))[:, None]).astype(jnp.float32)
    grad_inputs, grad_params = vjp_fn(cotangent.astype(jnp.float32) * valid_full[:, :, None])
    counted = jnp.sum(lengths).astype(jnp.float32)
    statistics = jnp.sqrt(lax.optimization_barrier(jnp.sum(square_sums, axis=0)) / (counted * D))
    return (outputs.astype(jnp.bfloat16), grad_inputs, grad_params[0], grad_params[1], grad_params[2], grad_params[3], grad_params[4], grad_params[5], grad_params[6], grad_params[7], grad_params[8], grad_params[9], grad_params[10], grad_params[11], statistics)
```

```python
import functools

import jax
import jax.numpy as jnp
from jax import lax
from jax.experimental import pallas as pl
from jax.experimental.pallas import tpu as pltpu
from jax.sharding import PartitionSpec as P

HD = 64
BIG = 1024
SMALL = 448
LP = BIG + 3 * SMALL
MARGIN = 128
EXP_SCALE = 0.125 * 1.4426950408889634
MESH = pl.DeviceIdType.MESH
BF = jnp.bfloat16
F32 = jnp.float32


def dot_nn(a, b):
    return lax.dot_general(a, b, (((1,), (0,)), ((), ())), preferred_element_type=F32)


def dot_nt(a, b):
    return lax.dot_general(a, b, (((1,), (1,)), ((), ())), preferred_element_type=F32)


def dot_tn(a, b):
    return lax.dot_general(a, b, (((0,), (0,)), ((), ())), preferred_element_type=F32)


def iota(shape, dim):
    return lax.broadcasted_iota(jnp.int32, shape, dim)


def head_mask(rows, width, h):
    lane = iota((rows, width), 1)
    return (lane >= h * HD) & (lane < (h + 1) * HD)


def segment_matrix(width):
    r = iota((width, width), 0) // HD
    c = iota((width, width), 1) // HD
    return jnp.where(r == c, 1.0 / HD, 0.0).astype(BF)


def segment_mean(x, seg):
    hi = x.astype(BF)
    lo = (x - hi.astype(F32)).astype(BF)
    return dot_nn(hi, seg) + dot_nn(lo, seg)


class Place:
    def __init__(self, nf, nt):
        self.nf, self.nt = nf, nt
        self.nx = 2
        self.nz = nf // 2
        f = lax.axis_index("fsdp")
        t = lax.axis_index("tp")
        self.f, self.t = f, t
        self.z, self.x = f // 2, lax.rem(f, 2)
        self.y, self.c = t // 2, lax.rem(t, 2)
        self.me = f * nt + t

    def rel(self, dz=0, dx=0, dy=0, dc=0):
        z = lax.rem(self.z + dz, self.nz) if dz else self.z
        x = 1 - self.x if dx else self.x
        y = 1 - self.y if dy else self.y
        c = 1 - self.c if dc else self.c
        return (z * 2 + x, y * 2 + c)


class Copies:
    def __init__(self):
        self.sent = []

    def start(self, src, dst, send_sem, recv_sem, dev):
        cp = pltpu.make_async_remote_copy(
            src_ref=src,
            dst_ref=dst,
            send_sem=send_sem,
            recv_sem=recv_sem,
            device_id=dev,
            device_id_type=MESH,
        )
        cp.start()
        self.sent.append(cp)

    def finish(self):
        for cp in self.sent:
            cp.wait_send()
        self.sent = []


def wait_recv(dst, send_sem, recv_sem, dev):
    pltpu.make_async_remote_copy(
        src_ref=dst,
        dst_ref=dst,
        send_sem=send_sem,
        recv_sem=recv_sem,
        device_id=dev,
        device_id_type=MESH,
    ).wait_recv()


def barrier_all(pc):
    n = pc.nf * pc.nt
    bar = pltpu.get_barrier_semaphore()

    def body(r, carry):
        p = lax.rem(pc.me + r, n)
        pl.semaphore_signal(
            bar, inc=1, device_id=(p // pc.nt, lax.rem(p, pc.nt)), device_id_type=MESH
        )
        return carry

    lax.fori_loop(1, n, body, 0)
    pl.semaphore_wait(bar, n - 1)


GATHER_ORDERS = {"zxy": ("z", "x", "y"), "zyx": ("z", "y", "x")}


def axis_steps(pc, axis):
    if axis == "z":
        return [dict(dz=i) for i in range(1, pc.nz)]
    return [{"d" + axis: 1}]


def gather_plan(pc, order):
    stages = [[(dict(), 0)]]
    have = [dict()]
    for k, axis in enumerate(order):
        fresh = []
        for step in axis_steps(pc, axis):
            for b in have:
                fresh.append(dict(b, **step))
        stages.append([(b, k + 1) for b in fresh])
        have = have + fresh
    return stages


class Gather:
    def __init__(self, pc, copies, src, dst, send, recv, order, spread_tp=True):
        self.pc, self.copies = pc, copies
        self.src, self.dst, self.send, self.recv = src, dst, send, recv
        self.order = order
        self.spread_tp = spread_tp
        self.stages = gather_plan(pc, order)
        self.count = 0

    def slot(self, place):
        f, t = place
        return self.dst.at[t, f] if self.spread_tp else self.dst.at[f]

    def rsem(self, place):
        f, t = place
        return self.recv.at[t, f] if self.spread_tp else self.recv.at[f]

    def pass_on(self, block, depth):
        pc = self.pc
        place = pc.rel(**block)
        src = self.src if not block else self.slot(place)
        targets = []
        for axis in self.order[depth:]:
            targets += axis_steps(pc, axis)
        if self.spread_tp:
            targets.append(dict(dc=1))
        for step in targets:
            self.copies.start(
                src,
                self.slot(place),
                self.send.at[self.count],
                self.rsem(place),
                pc.rel(**step),
            )
            self.count += 1

    def wait(self, block):
        place = self.pc.rel(**block)
        wait_recv(self.slot(place), self.send.at[0], self.rsem(place), self.pc.rel(dc=1))

    def stage(self, k):
        for block, depth in self.stages[k]:
            if block:
                self.wait(block)
            self.pass_on(block, depth)

    def last(self):
        if self.spread_tp:
            for stage in self.stages:
                for block, depth in stage:
                    self.wait(dict(block, dc=1))


def sends_of(nz, order, spread_tp):
    n = {"z": nz - 1, "x": 1, "y": 1}
    total, have = 0, 1
    for axis in order:
        total += have * n[axis]
        have *= n[axis] + 1
    return total + (have if spread_tp else 0)


def slots_of(lens_ref):
    lens = [lens_ref[0, p] for p in range(4)]
    starts = [0]
    for p in range(3):
        starts.append(starts[-1] + lens[p])
    big = 0
    for p in range(1, 4):
        big = jnp.where(lens[p] == BIG, p, big)
    sb = 0
    for p in range(1, 4):
        sb = jnp.where(big == p, starts[p], sb)
    out = [(sb, BIG)]
    for k in range(3):
        s = jnp.where(big <= k, starts[k + 1], starts[k])
        n = jnp.where(big <= k, lens[k + 1], lens[k])
        out.append((s, n))
    return out


BASES = (0, BIG, BIG + SMALL, BIG + 2 * SMALL)


def shift_matrix(rows, cols, r):
    return jnp.where(iota((rows, cols), 1) == iota((rows, cols), 0) + r, 1.0, 0.0).astype(BF)


def load_rows(src, first, count):
    return jnp.concatenate([src[first + m] for m in range(count)], axis=0)


def pack_rows(src, dst, lens):
    def big(j, carry):
        s = slots_of(lens)[0][0]
        r = lax.rem(s, 16)
        d = shift_matrix(128, 144, r)
        out = dot_nn(d, load_rows(src, s // 16 + j * 8, 9)).astype(BF)
        dst[pl.ds(pl.multiple_of(j * 128, 128), 128), :] = out
        return carry

    lax.fori_loop(0, BIG // 128, big, 0)

    for k in range(3):

        def small(j, carry, k=k):
            s = slots_of(lens)[1 + k][0]
            r = lax.rem(s, 16)
            d = shift_matrix(112, 128, r)
            out = dot_nn(d, load_rows(src, s // 16 + j * 7, 8)).astype(BF)
            dst[pl.ds(pl.multiple_of(BASES[1 + k] + j * 112, 16), 112), :] = out
            return carry

        lax.fori_loop(0, 4, small, 0)


def unpack_tile(src, i0, lens):
    wa, ea, wb, sb = 0, 0, 0, 4096
    for (s, n), base in zip(slots_of(lens), BASES):
        inside = (s <= i0) & (i0 < s + n)
        begins = (s > i0) & (s <= i0 + 127)
        w = base + i0 - s + MARGIN
        wa = jnp.where(inside, w, wa)
        ea = jnp.where(inside, s + n - i0, ea)
        wb = jnp.where(begins, w, wb)
        sb = jnp.where(begins, s - i0, sb)
    out = None
    row = iota((128, 144), 0)
    col = iota((128, 144), 1)
    for w, ok in ((wa, lambda: row < ea), (wb, lambda: row >= sb)):
        r = lax.rem(w, 16)
        d = jnp.where((col == row + r) & ok(), 1.0, 0.0).astype(BF)
        part = dot_nn(d, load_rows(src, w // 16, 9))
        out = part if out is None else out + part
    return out


def layer_norm_rows(x, g, b):
    mean = jnp.mean(x, axis=-1, keepdims=True)
    xc = x - mean
    var = jnp.mean(xc * xc, axis=-1, keepdims=True)
    inv = lax.rsqrt(var + EPS)
    n = xc * inv
    return n * g + b, n, inv


def own_heads(row, t, nt, width):
    out = row[:, :width]
    for k in range(1, nt):
        out = jnp.where(t == k, row[:, k * width : (k + 1) * width], out)
    return out


def build_gains(prm_all, gains, n, per):
    chunks = n * per // 128
    lane = iota((8, 128), 1)
    acc = [jnp.zeros((8, 128), F32) for _ in range(chunks)]
    for d in range(n):
        j, a = divmod(d * per, 128)
        tile = prm_all[d]
        if a:
            tile = pltpu.roll(tile, a, 1)
        acc[j] = jnp.where((lane >= a) & (lane < a + per), tile, acc[j])
        if a + per > 128:
            acc[j + 1] = jnp.where(lane < a + per - 128, tile, acc[j + 1])
    for j in range(chunks):
        gains[:, j * 128 : (j + 1) * 128] = acc[j]


def ka_kernel(
    nf, nt, orders,
    lens, tok, wa, wo, wu, wd, prm,
    h1p, qraw, kraw, qn, kn, va, lse, of, wqkv, wo_all, wu_all, wd_all, gains, o_own,
    tok_all, h1t, wa_all, prm_all, op, osend,
    prm_s, prm_r, tok_s, tok_r, wa_s, wa_r, wo_s, wo_r, wu_s, wu_r, wd_s, wd_r, o_s, o_r, loc,
):
    pc = Place(nf, nt)
    n = nf * nt
    cps = Copies()
    rows, width = tok.shape
    hw = qn.shape[1]
    barrier_all(pc)

    cps.start(tok, tok_all.at[pc.t], tok_s.at[0], tok_r.at[pc.t], pc.rel(dy=1))
    cps.start(tok, tok_all.at[pc.t], tok_s.at[1], tok_r.at[pc.t], pc.rel(dc=1))

    def push_prm(r, carry):
        p = lax.rem(pc.me + r, n)
        pltpu.make_async_remote_copy(
            src_ref=prm, dst_ref=prm_all.at[pc.me], send_sem=prm_s.at[r], recv_sem=prm_r.at[pc.me],
            device_id=(p // nt, lax.rem(p, nt)), device_id_type=MESH,
        ).start()
        return carry

    lax.fori_loop(1, n, push_prm, 0)
    ga = Gather(pc, cps, wa, wa_all, wa_s, wa_r, ("z", "x"), False)
    gw = [
        Gather(pc, cps, wo, wo_all, wo_s, wo_r, orders[0]),
        Gather(pc, cps, wu, wu_all, wu_s, wu_r, orders[1]),
        Gather(pc, cps, wd, wd_all, wd_s, wd_r, orders[2]),
    ]
    ga.stage(0)
    for g in gw:
        g.stage(0)
    local = []
    for src, dst in ((tok, tok_all.at[pc.t]), (wa, wa_all.at[pc.f]), (wo, wo_all.at[pc.t, pc.f]),
                     (wu, wu_all.at[pc.t, pc.f]), (wd, wd_all.at[pc.t, pc.f])):
        cp = pltpu.make_async_copy(src, dst, loc.at[len(local)])
        cp.start()
        local.append(cp)
    prm_all[pc.me] = prm[...]

    h1t[4 * rows // 16 :] = jnp.zeros((h1t.shape[0] - 4 * rows // 16, 16, width), BF)

    def wait_prm(r, carry):
        p = lax.rem(pc.me + r, n)
        wait_recv(prm_all.at[p], prm_s.at[0], prm_r.at[p], (p // nt, lax.rem(p, nt)))
        return carry

    lax.fori_loop(1, n, wait_prm, 0)
    build_gains(prm_all, gains, n, width // n)
    gain_one, shift_one = gains[0:1, :], gains[1:2, :]

    def norm_block(t):
        def body(j, carry):
            at = pl.ds(pl.multiple_of(j * 128, 128), 128)
            out, _, _ = layer_norm_rows(tok_all[t, at, :].astype(F32), gain_one, shift_one)
            h1t[pl.ds(t * (rows // 16) + j * 8, 8)] = out.astype(BF).reshape(8, 16, width)
            return carry

        lax.fori_loop(0, rows // 128, body, 0)

    def wait_tok(t):
        wait_recv(tok_all.at[t], tok_s.at[0], tok_r.at[t], pc.rel(dc=1))

    for cp in local:
        cp.wait()
    norm_block(pc.t)
    t_core, t_y, t_diag = pc.rel(dc=1)[1], pc.rel(dy=1)[1], pc.rel(dy=1, dc=1)[1]
    wait_tok(t_core)
    norm_block(t_core)
    ga.stage(1)
    for g in gw:
        g.stage(1)
    wait_tok(t_y)
    cps.start(tok_all.at[t_y], tok_all.at[t_y], tok_s.at[2], tok_r.at[t_y], pc.rel(dc=1))
    norm_block(t_y)
    ga.stage(2)
    wait_tok(t_diag)
    norm_block(t_diag)

    pack_rows(h1t, h1p, lens)
    seg = segment_matrix(hw)
    gq = own_heads(gains[4:5, :], pc.t, nt, hw)
    gk = own_heads(gains[5:6, :], pc.t, nt, hw)
    w_full = wa_all[...].reshape(width, 3 * hw)
    for i in range(3):
        wqkv[i] = w_full[:, i * hw : (i + 1) * hw]

    qt = LP // 4

    def project(j, carry):
        at = pl.ds(pl.multiple_of(j * qt, 16), qt)
        h = h1p[at, :]
        for i, (raw, normed, g) in enumerate(((qraw, qn, gq), (kraw, kn, gk))):
            q = dot_nn(h, wqkv[i])
            raw[at, :] = q
            qc = q - segment_mean(q, seg)
            inv = lax.rsqrt(segment_mean(qc * qc, seg) + EPS)
            normed[at, :] = (qc * inv * g).astype(BF)
        v = dot_nn(h, wqkv[2]).astype(BF)
        va[at, :hw] = v
        return carry

    lax.fori_loop(0, 4, project, 0)
    va[:, hw:] = jnp.ones((LP, va.shape[1] - hw), BF)
    head, tail = MARGIN // 16, (MARGIN + LP) // 16
    op[:head] = jnp.zeros((head, 16, hw), BF)
    op[tail:] = jnp.zeros((op.shape[0] - tail, 16, hw), BF)

    for g in gw:
        g.stage(2)

    def attend(at, keys, h, limit):
        nrow = at.size
        q = jnp.where(head_mask(nrow, hw, h), qn[at, :], jnp.zeros((), BF))
        s = dot_nt(q, kn[keys, :])
        p = jnp.exp2(s * EXP_SCALE)
        if limit is not None:
            p = jnp.where(iota(p.shape, 1) < limit, p, 0.0)
        oa = dot_nn(p.astype(BF), va[keys, :])
        total = oa[:, hw : hw + 1]
        o = oa[:, :hw] * (1.0 / total)
        l2 = jnp.log2(total)
        lane = iota((nrow, 128), 1)
        if h == 0:
            of[at, :] = o
            lse[at, :] = jnp.broadcast_to(l2, (nrow, 128))
        else:
            of[at, :] = jnp.where(head_mask(nrow, hw, h), o, of[at, :])
            lse[at, :] = jnp.where(lane == h, l2, lse[at, :])

    nh = hw // HD
    for h in range(nh):
        def big(j, carry, h=h):
            attend(pl.ds(pl.multiple_of(j * 512, 512), 512), pl.ds(0, BIG), h, None)
            return carry

        lax.fori_loop(0, BIG // 512, big, 0)

        for k in range(3):
            at = pl.ds(BASES[1 + k], SMALL)
            attend(at, at, h, slots_of(lens)[1 + k][1])
        if h == 0:
            for g in gw:
                g.stage(3)

    op[head:tail] = of[...].astype(BF).reshape(LP // 16, 16, hw)

    def unpack(i, carry):
        out = unpack_tile(op, i * 128, lens)
        osend[i // 4, pl.ds(pl.multiple_of(lax.rem(i, 4) * 128, 128), 128), :] = out.astype(BF)
        return carry

    lax.fori_loop(0, 16, unpack, 0)
    peers = [pc.rel(dy=1), pc.rel(dy=1, dc=1), pc.rel(dc=1)]
    for i, dev in enumerate(peers):
        cps.start(osend.at[dev[1]], o_own.at[pc.t], o_s.at[i], o_r.at[pc.t], dev)
    cp = pltpu.make_async_copy(osend.at[pc.t], o_own.at[pc.t], loc.at[0])
    cp.start()
    cp.wait()
    for g in gw:
        g.last()
    for dev in peers:
        wait_recv(o_own.at[dev[1]], o_s.at[0], o_r.at[dev[1]], dev)

    def wait_prm_sent(r, carry):
        p = lax.rem(pc.me + r, n)
        pltpu.make_async_remote_copy(
            src_ref=prm, dst_ref=prm_all.at[pc.me], send_sem=prm_s.at[r], recv_sem=prm_r.at[pc.me],
            device_id=(p // nt, lax.rem(p, nt)), device_id_type=MESH,
        ).wait_send()
        return carry

    lax.fori_loop(1, n, wait_prm_sent, 0)
    cps.finish()


def call_ka(nf, nt, lens, tok, wa, wo, wu, wd, prm):
    nz = nf // 2
    rows, width = tok.shape
    r = wa.shape[0]
    hw = wa.shape[1] // 3
    cu, cd = wu.shape[1], wd.shape[1]
    orders = (("z", "x", "y"), ("z", "y", "x"), ("z", "x", "y"))
    S = jax.ShapeDtypeStruct
    vm = pl.BlockSpec(memory_space=pltpu.VMEM)
    hb = pl.BlockSpec(memory_space=pl.ANY)
    outs = [
        (S((LP, width), BF), vm), (S((LP, hw), F32), vm), (S((LP, hw), F32), vm),
        (S((LP, hw), BF), vm), (S((LP, hw), BF), vm), (S((LP, 256), BF), vm),
        (S((LP, 128), F32), vm), (S((LP, hw), F32), vm), (S((3, width, hw), BF), vm),
        (S((nt, nf, r, hw), BF), hb), (S((nt, nf, r, cu), BF), hb), (S((nt, nf, r, cd), BF), hb),
        (S((8, width), F32), vm), (S((nt, rows, hw), BF), vm),
    ]
    dma = pltpu.SemaphoreType.DMA
    sends = [sends_of(nz, o, True) for o in orders]
    scratch = [
        pltpu.VMEM((nt, rows, width), BF), pltpu.VMEM(((nt * rows + 192) // 16, 16, width), BF),
        pltpu.VMEM((nf, r, 3 * hw), BF), pltpu.VMEM((nf * nt, 8, 128), F32),
        pltpu.VMEM(((MARGIN + LP + 160) // 16, 16, hw), BF), pltpu.VMEM((nt, rows, hw), BF),
        dma((nf * nt,)), dma((nf * nt,)), dma((3,)), dma((nt,)),
        dma((sends_of(nz, ("z", "x"), False),)), dma((nf,)),
        dma((sends[0],)), dma((nt, nf)), dma((sends[1],)), dma((nt, nf)), dma((sends[2],)), dma((nt, nf)),
        dma((3,)), dma((nt,)), dma((5,)),
    ]
    return pl.pallas_call(
        functools.partial(ka_kernel, nf, nt, orders),
        out_shape=[o[0] for o in outs],
        in_specs=[pl.BlockSpec(memory_space=pltpu.SMEM), vm, vm, hb, hb, hb, vm],
        out_specs=[o[1] for o in outs],
        scratch_shapes=scratch,
        compiler_params=pltpu.CompilerParams(
            collective_id=0, has_side_effects=True, vmem_limit_bytes=56 << 20
        ),
    )(lens, tok, wa, wo, wu, wd, prm)


EPS = 1e-06
ROOT_HALF = 0.7071067811865476
DENSITY = 0.3989422804014327


def normalise(values, scaling, offset):
    centre = jnp.mean(values, axis=-1, keepdims=True)
    centred = values - centre
    spread = jnp.mean(centred * centred, axis=-1, keepdims=True)
    inverse = lax.rsqrt(spread + EPS)
    normed = centred * inverse
    return (normed * scaling + offset, normed, inverse)


def normalise_back(grad_out, normed, inverse, scaling):
    grad_unit = grad_out * scaling
    grad_values = inverse * (
        grad_unit
        - jnp.mean(grad_unit, axis=-1, keepdims=True)
        - normed * jnp.mean(grad_unit * normed, axis=-1, keepdims=True)
    )
    return (grad_values, jnp.sum(grad_out * normed, axis=(0, 1)), jnp.sum(grad_out, axis=(0, 1)))


def gelu_slope(values):
    return (
        0.5 * (1.0 + jax.scipy.special.erf(values * ROOT_HALF))
        + values * jnp.exp(-0.5 * values * values) * DENSITY
    )


def gather_tokens(values):
    return lax.all_gather(values, "tp", axis=1, tiled=True)


def gather_grads(values):
    return lax.all_gather(values, "tp", axis=1, tiled=True)


def reduce_tokens(values):
    return lax.psum_scatter(
        values.astype(jnp.bfloat16), "tp", scatter_dimension=1, tiled=True
    ).astype(jnp.float32)


def reduce_grads(values):
    return lax.psum_scatter(
        values.astype(jnp.bfloat16), "tp", scatter_dimension=1, tiled=True
    ).astype(jnp.float32)


def block_scores(query, keyed, picture_query, picture_key, key_mask):
    raw_scores = jnp.einsum("qhd,khd->hqk", query, keyed, preferred_element_type=jnp.float32)
    allowed = (picture_query[:, None] == picture_key[None, :]) & (key_mask[None, :] > 0)
    return jnp.where(allowed[None], raw_scores * query.shape[-1] ** (-0.5), -1e30)


def forward_row(packed):
    query_row, key_row, value_row, picture_row, mask_row = packed
    full_len = query_row.shape[0]
    block_len = min(512, full_len)
    block_count = full_len // block_len

    def forward_one_block(packed_block):
        query_block, picture_block = packed_block
        scores = block_scores(query_block, key_row, picture_block, picture_row, mask_row)
        highest = jnp.max(scores, axis=-1, keepdims=True)
        logsum = highest + jnp.log(jnp.sum(jnp.exp(scores - highest), axis=-1, keepdims=True))
        probability = jnp.exp(scores - logsum).astype(jnp.bfloat16)
        mixture = jnp.einsum(
            "hqk,khd->qhd", probability, value_row, preferred_element_type=jnp.float32
        )
        return (mixture, logsum)

    query_blocks = query_row.reshape((block_count, block_len) + query_row.shape[1:])
    return lax.map(forward_one_block, (query_blocks, picture_row.reshape(block_count, block_len)))


def backward_row(packed):
    query_row, key_row, value_row, picture_row, mask_row, grad_row, logsum_row = packed
    full_len = query_row.shape[0]
    block_len = min(512, full_len)
    block_count = full_len // block_len
    factor = query_row.shape[-1] ** (-0.5)

    def backward_one_block(running, packed_block):
        grad_key, grad_value = running
        query_block, picture_block, grad_block, logsum_block = packed_block
        scores = block_scores(query_block, key_row, picture_block, picture_row, mask_row)
        probability = jnp.exp(scores - logsum_block)
        prob_low = probability.astype(jnp.bfloat16)
        grad_prob = jnp.einsum(
            "qhd,khd->hqk", grad_block, value_row, preferred_element_type=jnp.float32
        )
        grad_value = grad_value + jnp.einsum(
            "hqk,qhd->khd", prob_low, grad_block, preferred_element_type=jnp.float32
        )
        centre = jnp.sum(probability * grad_prob, axis=-1, keepdims=True)
        grad_scores = (probability * (grad_prob - centre)).astype(jnp.bfloat16)
        grad_query = factor * jnp.einsum(
            "hqk,khd->qhd", grad_scores, key_row, preferred_element_type=jnp.float32
        )
        grad_key = grad_key + factor * jnp.einsum(
            "hqk,qhd->khd", grad_scores, query_block, preferred_element_type=jnp.float32
        )
        return ((grad_key, grad_value), grad_query)

    zero_state = jnp.zeros(key_row.shape, jnp.float32)
    block_shape = (block_count, block_len) + query_row.shape[1:]
    (grad_key, grad_value), grad_query = lax.scan(
        backward_one_block,
        (zero_state, zero_state),
        (
            query_row.reshape(block_shape),
            picture_row.reshape(block_count, block_len),
            grad_row.reshape(block_shape),
            logsum_row,
        ),
    )
    return (grad_query.reshape(key_row.shape), grad_key, grad_value)


def local_layer(
    nf,
    nt,
    tokens,
    lengths,
    pictures,
    w_query,
    w_key,
    w_value,
    w_out,
    w_up,
    w_down,
    norm1_gain,
    norm1_shift,
    norm2_gain,
    norm2_shift,
    query_gain,
    key_gain,
    cotangent,
):
    tp_place = lax.axis_index("tp")
    local_len = tokens.shape[1]
    model_width = tokens.shape[2]
    full_len = pictures.shape[1]
    local_width = w_query.shape[1]
    heads_local = local_width // HD
    gain_one, shift_one, gain_two, shift_two, gain_query, gain_key = (
        lax.all_gather(norm1_gain, ("fsdp", "tp"), axis=0, tiled=True),
        lax.all_gather(norm1_shift, ("fsdp", "tp"), axis=0, tiled=True),
        lax.all_gather(norm2_gain, ("fsdp", "tp"), axis=0, tiled=True),
        lax.all_gather(norm2_shift, ("fsdp", "tp"), axis=0, tiled=True),
        lax.all_gather(query_gain, ("fsdp", "tp"), axis=0, tiled=True),
        lax.all_gather(key_gain, ("fsdp", "tp"), axis=0, tiled=True),
    )
    positions = jnp.arange(full_len, dtype=jnp.int32)
    valid_full = (positions[None, :] < jnp.sum(lengths, axis=1)[:, None]).astype(jnp.float32)
    valid_here = lax.dynamic_slice_in_dim(valid_full, tp_place * local_len, local_len, 1)[
        :, :, None
    ]
    qgain_here = lax.dynamic_slice_in_dim(
        gain_query, tp_place * local_width, local_width, 0
    ).reshape(heads_local, HD)
    kgain_here = lax.dynamic_slice_in_dim(gain_key, tp_place * local_width, local_width, 0).reshape(
        heads_local, HD
    )
    front_query, front_key, front_value, front_out = (
        lax.all_gather(w_query, "fsdp", axis=0, tiled=True),
        lax.all_gather(w_key, "fsdp", axis=0, tiled=True),
        lax.all_gather(w_value, "fsdp", axis=0, tiled=True),
        lax.all_gather(w_out, "fsdp", axis=1, tiled=True),
    )
    fused = nt == 4 and tokens.shape[0] == 1 and w_query.shape[0] % 16 == 0
    if fused:
        smalls = (norm1_gain, norm1_shift, norm2_gain, norm2_shift, query_gain, key_gain)
        per = norm1_gain.shape[0]
        prm = jnp.zeros((8, 128), jnp.float32).at[:6, :per].set(jnp.stack(smalls))
        attn = jnp.concatenate([w_query, w_key, w_value], axis=1)
        ka = call_ka(nf, nt, lengths, tokens[0], attn, w_out.T, w_up, w_down.T, prm)
    inputs = tokens.astype(jnp.float32)
    hidden, normed_one, inverse_one = normalise(inputs, gain_one, shift_one)
    hidden_full = gather_tokens(hidden.astype(jnp.bfloat16))
    row_shape = hidden_full.shape[:2] + (heads_local, HD)
    query = jnp.dot(hidden_full, front_query, preferred_element_type=jnp.float32).reshape(row_shape)
    keyed = jnp.dot(hidden_full, front_key, preferred_element_type=jnp.float32).reshape(row_shape)
    value_low = (
        jnp.dot(hidden_full, front_value, preferred_element_type=jnp.float32)
        .astype(jnp.bfloat16)
        .reshape(row_shape)
    )
    query_norm, query_unit, query_inverse = normalise(query, qgain_here, 0.0)
    key_norm, key_unit, key_inverse = normalise(keyed, kgain_here, 0.0)
    query_low = query_norm.astype(jnp.bfloat16)
    key_low = key_norm.astype(jnp.bfloat16)
    mixture, logsum = lax.map(forward_row, (query_low, key_low, value_low, pictures, valid_full))
    mixture_low = mixture.reshape(hidden_full.shape[:2] + (local_width,)).astype(jnp.bfloat16)
    attn_branch = valid_here * reduce_tokens(
        jnp.dot(mixture_low, front_out, preferred_element_type=jnp.float32)
    )
    if fused:
        mixed = jnp.transpose(ka[13], (1, 0, 2)).reshape(local_len, model_width)
        w_full = jnp.transpose(ka[9], (1, 2, 0, 3)).reshape(model_width, model_width)
        attn_branch = valid_here * dot_nt(mixed, w_full)[None]
    middle = inputs + attn_branch
    hidden_two, normed_two, inverse_two = normalise(middle, gain_two, shift_two)
    hidden_two_full = gather_tokens(hidden_two.astype(jnp.bfloat16))
    front_up, front_down = (
        lax.all_gather(w_up, "fsdp", axis=0, tiled=True),
        lax.all_gather(w_down, "fsdp", axis=1, tiled=True),
    )
    up_value = jnp.dot(hidden_two_full, front_up, preferred_element_type=jnp.float32)
    activated = jax.nn.gelu(up_value, approximate=False).astype(jnp.bfloat16)
    mlp_branch = valid_here * reduce_tokens(
        jnp.dot(activated, front_down, preferred_element_type=jnp.float32)
    )
    result = (middle + mlp_branch).astype(jnp.bfloat16)
    square_sums = jnp.stack(
        [
            jnp.sum(valid_here * inputs * inputs),
            jnp.sum(attn_branch * attn_branch),
            jnp.sum(valid_here * middle * middle),
            jnp.sum(mlp_branch * mlp_branch),
        ]
    )
    valid_count = jnp.sum(valid_here)
    back_up, back_down = (
        lax.all_gather(w_up, "fsdp", axis=0, tiled=True),
        lax.all_gather(w_down, "fsdp", axis=1, tiled=True),
    )
    back_query, back_key, back_value, back_out = (
        lax.all_gather(w_query, "fsdp", axis=0, tiled=True),
        lax.all_gather(w_key, "fsdp", axis=0, tiled=True),
        lax.all_gather(w_value, "fsdp", axis=0, tiled=True),
        lax.all_gather(w_out, "fsdp", axis=1, tiled=True),
    )
    grad_y = cotangent.astype(jnp.float32) * valid_here
    grad_y_full = gather_grads(grad_y.astype(jnp.bfloat16))
    grad_down = jnp.einsum(
        "rlf,rld->fd", activated, grad_y_full, preferred_element_type=jnp.float32
    )
    grad_act = jnp.dot(grad_y_full, back_down.T, preferred_element_type=jnp.float32)
    grad_pre = (grad_act * gelu_slope(up_value)).astype(jnp.bfloat16)
    grad_up = jnp.einsum(
        "rld,rlf->df", hidden_two_full, grad_pre, preferred_element_type=jnp.float32
    )
    grad_hidden_two = reduce_grads(jnp.dot(grad_pre, back_up.T, preferred_element_type=jnp.float32))
    mlp_grads = (
        lax.psum_scatter(grad_up, "fsdp", scatter_dimension=0, tiled=True),
        lax.psum_scatter(grad_down, "fsdp", scatter_dimension=1, tiled=True),
    )
    grad_mid_norm, grad_gain_two, grad_shift_two = normalise_back(
        grad_hidden_two, normed_two, inverse_two, gain_two
    )
    grad_middle = grad_y + grad_mid_norm
    grad_branch_here = (valid_here * grad_middle).astype(jnp.bfloat16)
    grad_branch_full = gather_grads(grad_branch_here)
    grad_out_proj = jnp.einsum(
        "rlh,rld->hd", mixture_low, grad_branch_full, preferred_element_type=jnp.float32
    )
    grad_mixture = jnp.dot(grad_branch_full, back_out.T, preferred_element_type=jnp.float32).astype(
        jnp.bfloat16
    )
    grad_qnorm, grad_knorm, grad_value_full = lax.map(
        backward_row,
        (
            query_low,
            key_low,
            value_low,
            pictures,
            valid_full,
            grad_mixture.reshape(row_shape),
            logsum,
        ),
    )
    grad_query_pre, grad_qgain, unused_one = normalise_back(
        grad_qnorm, query_unit, query_inverse, qgain_here
    )
    grad_key_pre, grad_kgain, unused_two = normalise_back(
        grad_knorm, key_unit, key_inverse, kgain_here
    )
    flat_shape = hidden_full.shape[:2] + (local_width,)
    grad_query_low = grad_query_pre.reshape(flat_shape).astype(jnp.bfloat16)
    grad_key_low = grad_key_pre.reshape(flat_shape).astype(jnp.bfloat16)
    grad_value_low = grad_value_full.reshape(flat_shape).astype(jnp.bfloat16)
    grad_wquery = jnp.einsum(
        "rld,rlh->dh", hidden_full, grad_query_low, preferred_element_type=jnp.float32
    )
    grad_wkey = jnp.einsum(
        "rld,rlh->dh", hidden_full, grad_key_low, preferred_element_type=jnp.float32
    )
    grad_wvalue = jnp.einsum(
        "rld,rlh->dh", hidden_full, grad_value_low, preferred_element_type=jnp.float32
    )
    grad_hidden_part = (
        jnp.dot(grad_query_low, back_query.T, preferred_element_type=jnp.float32)
        + jnp.dot(grad_key_low, back_key.T, preferred_element_type=jnp.float32)
        + jnp.dot(grad_value_low, back_value.T, preferred_element_type=jnp.float32)
    )
    grad_hidden = reduce_grads(grad_hidden_part)
    attn_grads = (
        lax.psum_scatter(grad_wquery, "fsdp", scatter_dimension=0, tiled=True),
        lax.psum_scatter(grad_wkey, "fsdp", scatter_dimension=0, tiled=True),
        lax.psum_scatter(grad_wvalue, "fsdp", scatter_dimension=0, tiled=True),
        lax.psum_scatter(grad_out_proj, "fsdp", scatter_dimension=1, tiled=True),
    )
    grad_in_norm, grad_gain_one, grad_shift_one = normalise_back(
        grad_hidden, normed_one, inverse_one, gain_one
    )
    grad_inputs = grad_middle + grad_in_norm
    zero_width = jnp.zeros((model_width,), jnp.float32)
    grad_qgain_full = lax.dynamic_update_slice_in_dim(
        zero_width, grad_qgain.reshape(local_width), tp_place * local_width, 0
    )
    grad_kgain_full = lax.dynamic_update_slice_in_dim(
        zero_width, grad_kgain.reshape(local_width), tp_place * local_width, 0
    )
    small_shards = (
        lax.psum_scatter(grad_gain_one, ("fsdp", "tp"), scatter_dimension=0, tiled=True),
        lax.psum_scatter(grad_shift_one, ("fsdp", "tp"), scatter_dimension=0, tiled=True),
        lax.psum_scatter(grad_gain_two, ("fsdp", "tp"), scatter_dimension=0, tiled=True),
        lax.psum_scatter(grad_shift_two, ("fsdp", "tp"), scatter_dimension=0, tiled=True),
        lax.psum_scatter(grad_qgain_full, ("fsdp", "tp"), scatter_dimension=0, tiled=True),
        lax.psum_scatter(grad_kgain_full, ("fsdp", "tp"), scatter_dimension=0, tiled=True),
    )
    totals, counted = lax.psum((square_sums, valid_count), ("fsdp", "tp"))
    statistics = jnp.sqrt(totals / (counted * model_width))
    return (
        result,
        grad_inputs,
        attn_grads[0],
        attn_grads[1],
        attn_grads[2],
        attn_grads[3],
        mlp_grads[0],
        mlp_grads[1],
        small_shards[0],
        small_shards[1],
        small_shards[2],
        small_shards[3],
        small_shards[4],
        small_shards[5],
        statistics,
    )


def solution(mesh):
    nf, nt = mesh.shape["fsdp"], mesh.shape["tp"]
    local = functools.partial(local_layer, nf, nt)

    in_specs = (
        P("fsdp", "tp", None),
        P("fsdp", None),
        P("fsdp", None),
        P("fsdp", "tp"),
        P("fsdp", "tp"),
        P("fsdp", "tp"),
        P("tp", "fsdp"),
        P("fsdp", "tp"),
        P("tp", "fsdp"),
        P(("fsdp", "tp")),
        P(("fsdp", "tp")),
        P(("fsdp", "tp")),
        P(("fsdp", "tp")),
        P(("fsdp", "tp")),
        P(("fsdp", "tp")),
        P("fsdp", "tp", None),
    )
    out_specs = (
        P("fsdp", "tp", None),
        P("fsdp", "tp", None),
        P("fsdp", "tp"),
        P("fsdp", "tp"),
        P("fsdp", "tp"),
        P("tp", "fsdp"),
        P("fsdp", "tp"),
        P("tp", "fsdp"),
        P(("fsdp", "tp")),
        P(("fsdp", "tp")),
        P(("fsdp", "tp")),
        P(("fsdp", "tp")),
        P(("fsdp", "tp")),
        P(("fsdp", "tp")),
        P(),
    )
    return jax.shard_map(local, mesh=mesh, in_specs=in_specs, out_specs=out_specs, check_vma=False)
```

```python
import functools

import jax
import jax.numpy as jnp
from jax import lax
from jax.experimental import pallas as pl
from jax.experimental.pallas import tpu as pltpu
from jax.sharding import PartitionSpec as P

HD = 64


EPS = 1e-06
ROOT_HALF = 0.7071067811865476
DENSITY = 0.3989422804014327


def normalise(values, scaling, offset):
    centre = jnp.mean(values, axis=-1, keepdims=True)
    centred = values - centre
    spread = jnp.mean(centred * centred, axis=-1, keepdims=True)
    inverse = lax.rsqrt(spread + EPS)
    normed = centred * inverse
    return (normed * scaling + offset, normed, inverse)


def normalise_back(grad_out, normed, inverse, scaling):
    grad_unit = grad_out * scaling
    grad_values = inverse * (
        grad_unit
        - jnp.mean(grad_unit, axis=-1, keepdims=True)
        - normed * jnp.mean(grad_unit * normed, axis=-1, keepdims=True)
    )
    return (grad_values, jnp.sum(grad_out * normed, axis=(0, 1)), jnp.sum(grad_out, axis=(0, 1)))


def gelu_slope(values):
    return (
        0.5 * (1.0 + jax.scipy.special.erf(values * ROOT_HALF))
        + values * jnp.exp(-0.5 * values * values) * DENSITY
    )


def gather_tokens(values):
    return lax.all_gather(values, "tp", axis=1, tiled=True)


def gather_grads(values):
    return lax.all_gather(values, "tp", axis=1, tiled=True)


def reduce_tokens(values):
    return lax.psum_scatter(
        values.astype(jnp.bfloat16), "tp", scatter_dimension=1, tiled=True
    ).astype(jnp.float32)


def reduce_grads(values):
    return lax.psum_scatter(
        values.astype(jnp.bfloat16), "tp", scatter_dimension=1, tiled=True
    ).astype(jnp.float32)


def block_scores(query, keyed, picture_query, picture_key, key_mask):
    raw_scores = jnp.einsum("qhd,khd->hqk", query, keyed, preferred_element_type=jnp.float32)
    allowed = (picture_query[:, None] == picture_key[None, :]) & (key_mask[None, :] > 0)
    return jnp.where(allowed[None], raw_scores * query.shape[-1] ** (-0.5), -1e30)


def forward_row(packed):
    query_row, key_row, value_row, picture_row, mask_row = packed
    full_len = query_row.shape[0]
    block_len = min(512, full_len)
    block_count = full_len // block_len

    def forward_one_block(packed_block):
        query_block, picture_block = packed_block
        scores = block_scores(query_block, key_row, picture_block, picture_row, mask_row)
        highest = jnp.max(scores, axis=-1, keepdims=True)
        logsum = highest + jnp.log(jnp.sum(jnp.exp(scores - highest), axis=-1, keepdims=True))
        probability = jnp.exp(scores - logsum).astype(jnp.bfloat16)
        mixture = jnp.einsum(
            "hqk,khd->qhd", probability, value_row, preferred_element_type=jnp.float32
        )
        return (mixture, logsum)

    query_blocks = query_row.reshape((block_count, block_len) + query_row.shape[1:])
    return lax.map(forward_one_block, (query_blocks, picture_row.reshape(block_count, block_len)))


def backward_row(packed):
    query_row, key_row, value_row, picture_row, mask_row, grad_row, logsum_row = packed
    full_len = query_row.shape[0]
    block_len = min(512, full_len)
    block_count = full_len // block_len
    factor = query_row.shape[-1] ** (-0.5)

    def backward_one_block(running, packed_block):
        grad_key, grad_value = running
        query_block, picture_block, grad_block, logsum_block = packed_block
        scores = block_scores(query_block, key_row, picture_block, picture_row, mask_row)
        probability = jnp.exp(scores - logsum_block)
        prob_low = probability.astype(jnp.bfloat16)
        grad_prob = jnp.einsum(
            "qhd,khd->hqk", grad_block, value_row, preferred_element_type=jnp.float32
        )
        grad_value = grad_value + jnp.einsum(
            "hqk,qhd->khd", prob_low, grad_block, preferred_element_type=jnp.float32
        )
        centre = jnp.sum(probability * grad_prob, axis=-1, keepdims=True)
        grad_scores = (probability * (grad_prob - centre)).astype(jnp.bfloat16)
        grad_query = factor * jnp.einsum(
            "hqk,khd->qhd", grad_scores, key_row, preferred_element_type=jnp.float32
        )
        grad_key = grad_key + factor * jnp.einsum(
            "hqk,qhd->khd", grad_scores, query_block, preferred_element_type=jnp.float32
        )
        return ((grad_key, grad_value), grad_query)

    zero_state = jnp.zeros(key_row.shape, jnp.float32)
    block_shape = (block_count, block_len) + query_row.shape[1:]
    (grad_key, grad_value), grad_query = lax.scan(
        backward_one_block,
        (zero_state, zero_state),
        (
            query_row.reshape(block_shape),
            picture_row.reshape(block_count, block_len),
            grad_row.reshape(block_shape),
            logsum_row,
        ),
    )
    return (grad_query.reshape(key_row.shape), grad_key, grad_value)


def local_plain(
    tokens,
    lengths,
    pictures,
    w_query,
    w_key,
    w_value,
    w_out,
    w_up,
    w_down,
    norm1_gain,
    norm1_shift,
    norm2_gain,
    norm2_shift,
    query_gain,
    key_gain,
    cotangent,
):
    tp_place = lax.axis_index("tp")
    local_len = tokens.shape[1]
    model_width = tokens.shape[2]
    full_len = pictures.shape[1]
    local_width = w_query.shape[1]
    heads_local = local_width // HD
    gain_one, shift_one, gain_two, shift_two, gain_query, gain_key = (
        lax.all_gather(norm1_gain, ("fsdp", "tp"), axis=0, tiled=True),
        lax.all_gather(norm1_shift, ("fsdp", "tp"), axis=0, tiled=True),
        lax.all_gather(norm2_gain, ("fsdp", "tp"), axis=0, tiled=True),
        lax.all_gather(norm2_shift, ("fsdp", "tp"), axis=0, tiled=True),
        lax.all_gather(query_gain, ("fsdp", "tp"), axis=0, tiled=True),
        lax.all_gather(key_gain, ("fsdp", "tp"), axis=0, tiled=True),
    )
    positions = jnp.arange(full_len, dtype=jnp.int32)
    valid_full = (positions[None, :] < jnp.sum(lengths, axis=1)[:, None]).astype(jnp.float32)
    valid_here = lax.dynamic_slice_in_dim(valid_full, tp_place * local_len, local_len, 1)[
        :, :, None
    ]
    qgain_here = lax.dynamic_slice_in_dim(
        gain_query, tp_place * local_width, local_width, 0
    ).reshape(heads_local, HD)
    kgain_here = lax.dynamic_slice_in_dim(gain_key, tp_place * local_width, local_width, 0).reshape(
        heads_local, HD
    )
    front_query, front_key, front_value, front_out = (
        lax.all_gather(w_query, "fsdp", axis=0, tiled=True),
        lax.all_gather(w_key, "fsdp", axis=0, tiled=True),
        lax.all_gather(w_value, "fsdp", axis=0, tiled=True),
        lax.all_gather(w_out, "fsdp", axis=1, tiled=True),
    )
    inputs = tokens.astype(jnp.float32)
    hidden, normed_one, inverse_one = normalise(inputs, gain_one, shift_one)
    hidden_full = gather_tokens(hidden.astype(jnp.bfloat16))
    row_shape = hidden_full.shape[:2] + (heads_local, HD)
    query = jnp.dot(hidden_full, front_query, preferred_element_type=jnp.float32).reshape(row_shape)
    keyed = jnp.dot(hidden_full, front_key, preferred_element_type=jnp.float32).reshape(row_shape)
    value_low = (
        jnp.dot(hidden_full, front_value, preferred_element_type=jnp.float32)
        .astype(jnp.bfloat16)
        .reshape(row_shape)
    )
    query_norm, query_unit, query_inverse = normalise(query, qgain_here, 0.0)
    key_norm, key_unit, key_inverse = normalise(keyed, kgain_here, 0.0)
    query_low = query_norm.astype(jnp.bfloat16)
    key_low = key_norm.astype(jnp.bfloat16)
    mixture, logsum = lax.map(forward_row, (query_low, key_low, value_low, pictures, valid_full))
    mixture_low = mixture.reshape(hidden_full.shape[:2] + (local_width,)).astype(jnp.bfloat16)
    attn_branch = valid_here * reduce_tokens(
        jnp.dot(mixture_low, front_out, preferred_element_type=jnp.float32)
    )
    middle = inputs + attn_branch
    hidden_two, normed_two, inverse_two = normalise(middle, gain_two, shift_two)
    hidden_two_full = gather_tokens(hidden_two.astype(jnp.bfloat16))
    front_up, front_down = (
        lax.all_gather(w_up, "fsdp", axis=0, tiled=True),
        lax.all_gather(w_down, "fsdp", axis=1, tiled=True),
    )
    up_value = jnp.dot(hidden_two_full, front_up, preferred_element_type=jnp.float32)
    activated = jax.nn.gelu(up_value, approximate=False).astype(jnp.bfloat16)
    mlp_branch = valid_here * reduce_tokens(
        jnp.dot(activated, front_down, preferred_element_type=jnp.float32)
    )
    result = (middle + mlp_branch).astype(jnp.bfloat16)
    square_sums = jnp.stack(
        [
            jnp.sum(valid_here * inputs * inputs),
            jnp.sum(attn_branch * attn_branch),
            jnp.sum(valid_here * middle * middle),
            jnp.sum(mlp_branch * mlp_branch),
        ]
    )
    valid_count = jnp.sum(valid_here)
    back_up, back_down = (
        lax.all_gather(w_up, "fsdp", axis=0, tiled=True),
        lax.all_gather(w_down, "fsdp", axis=1, tiled=True),
    )
    back_query, back_key, back_value, back_out = (
        lax.all_gather(w_query, "fsdp", axis=0, tiled=True),
        lax.all_gather(w_key, "fsdp", axis=0, tiled=True),
        lax.all_gather(w_value, "fsdp", axis=0, tiled=True),
        lax.all_gather(w_out, "fsdp", axis=1, tiled=True),
    )
    grad_y = cotangent.astype(jnp.float32) * valid_here
    grad_y_full = gather_grads(grad_y.astype(jnp.bfloat16))
    grad_down = jnp.einsum(
        "rlf,rld->fd", activated, grad_y_full, preferred_element_type=jnp.float32
    )
    grad_act = jnp.dot(grad_y_full, back_down.T, preferred_element_type=jnp.float32)
    grad_pre = (grad_act * gelu_slope(up_value)).astype(jnp.bfloat16)
    grad_up = jnp.einsum(
        "rld,rlf->df", hidden_two_full, grad_pre, preferred_element_type=jnp.float32
    )
    grad_hidden_two = reduce_grads(jnp.dot(grad_pre, back_up.T, preferred_element_type=jnp.float32))
    mlp_grads = (
        lax.psum_scatter(grad_up, "fsdp", scatter_dimension=0, tiled=True),
        lax.psum_scatter(grad_down, "fsdp", scatter_dimension=1, tiled=True),
    )
    grad_mid_norm, grad_gain_two, grad_shift_two = normalise_back(
        grad_hidden_two, normed_two, inverse_two, gain_two
    )
    grad_middle = grad_y + grad_mid_norm
    grad_branch_here = (valid_here * grad_middle).astype(jnp.bfloat16)
    grad_branch_full = gather_grads(grad_branch_here)
    grad_out_proj = jnp.einsum(
        "rlh,rld->hd", mixture_low, grad_branch_full, preferred_element_type=jnp.float32
    )
    grad_mixture = jnp.dot(grad_branch_full, back_out.T, preferred_element_type=jnp.float32).astype(
        jnp.bfloat16
    )
    grad_qnorm, grad_knorm, grad_value_full = lax.map(
        backward_row,
        (
            query_low,
            key_low,
            value_low,
            pictures,
            valid_full,
            grad_mixture.reshape(row_shape),
            logsum,
        ),
    )
    grad_query_pre, grad_qgain, unused_one = normalise_back(
        grad_qnorm, query_unit, query_inverse, qgain_here
    )
    grad_key_pre, grad_kgain, unused_two = normalise_back(
        grad_knorm, key_unit, key_inverse, kgain_here
    )
    flat_shape = hidden_full.shape[:2] + (local_width,)
    grad_query_low = grad_query_pre.reshape(flat_shape).astype(jnp.bfloat16)
    grad_key_low = grad_key_pre.reshape(flat_shape).astype(jnp.bfloat16)
    grad_value_low = grad_value_full.reshape(flat_shape).astype(jnp.bfloat16)
    grad_wquery = jnp.einsum(
        "rld,rlh->dh", hidden_full, grad_query_low, preferred_element_type=jnp.float32
    )
    grad_wkey = jnp.einsum(
        "rld,rlh->dh", hidden_full, grad_key_low, preferred_element_type=jnp.float32
    )
    grad_wvalue = jnp.einsum(
        "rld,rlh->dh", hidden_full, grad_value_low, preferred_element_type=jnp.float32
    )
    grad_hidden_part = (
        jnp.dot(grad_query_low, back_query.T, preferred_element_type=jnp.float32)
        + jnp.dot(grad_key_low, back_key.T, preferred_element_type=jnp.float32)
        + jnp.dot(grad_value_low, back_value.T, preferred_element_type=jnp.float32)
    )
    grad_hidden = reduce_grads(grad_hidden_part)
    attn_grads = (
        lax.psum_scatter(grad_wquery, "fsdp", scatter_dimension=0, tiled=True),
        lax.psum_scatter(grad_wkey, "fsdp", scatter_dimension=0, tiled=True),
        lax.psum_scatter(grad_wvalue, "fsdp", scatter_dimension=0, tiled=True),
        lax.psum_scatter(grad_out_proj, "fsdp", scatter_dimension=1, tiled=True),
    )
    grad_in_norm, grad_gain_one, grad_shift_one = normalise_back(
        grad_hidden, normed_one, inverse_one, gain_one
    )
    grad_inputs = grad_middle + grad_in_norm
    zero_width = jnp.zeros((model_width,), jnp.float32)
    grad_qgain_full = lax.dynamic_update_slice_in_dim(
        zero_width, grad_qgain.reshape(local_width), tp_place * local_width, 0
    )
    grad_kgain_full = lax.dynamic_update_slice_in_dim(
        zero_width, grad_kgain.reshape(local_width), tp_place * local_width, 0
    )
    small_shards = (
        lax.psum_scatter(grad_gain_one, ("fsdp", "tp"), scatter_dimension=0, tiled=True),
        lax.psum_scatter(grad_shift_one, ("fsdp", "tp"), scatter_dimension=0, tiled=True),
        lax.psum_scatter(grad_gain_two, ("fsdp", "tp"), scatter_dimension=0, tiled=True),
        lax.psum_scatter(grad_shift_two, ("fsdp", "tp"), scatter_dimension=0, tiled=True),
        lax.psum_scatter(grad_qgain_full, ("fsdp", "tp"), scatter_dimension=0, tiled=True),
        lax.psum_scatter(grad_kgain_full, ("fsdp", "tp"), scatter_dimension=0, tiled=True),
    )
    totals, counted = lax.psum((square_sums, valid_count), ("fsdp", "tp"))
    statistics = jnp.sqrt(totals / (counted * model_width))
    return (
        result,
        grad_inputs,
        attn_grads[0],
        attn_grads[1],
        attn_grads[2],
        attn_grads[3],
        mlp_grads[0],
        mlp_grads[1],
        small_shards[0],
        small_shards[1],
        small_shards[2],
        small_shards[3],
        small_shards[4],
        small_shards[5],
        statistics,
    )


BIG = 1024
SMALL = 448
LP = BIG + 3 * SMALL
MARGIN = 128
EXP_SCALE = 0.125 * 1.4426950408889634
MESH = pl.DeviceIdType.MESH
BF = jnp.bfloat16
F32 = jnp.float32


def dot_nn(a, b):
    return lax.dot_general(a, b, (((1,), (0,)), ((), ())), preferred_element_type=F32)


def dot_nt(a, b):
    return lax.dot_general(a, b, (((1,), (1,)), ((), ())), preferred_element_type=F32)


def dot_tn(a, b):
    return lax.dot_general(a, b, (((0,), (0,)), ((), ())), preferred_element_type=F32)


def iota(shape, dim):
    return lax.broadcasted_iota(jnp.int32, shape, dim)


def head_mask(rows, width, h):
    lane = iota((rows, width), 1)
    return (lane >= h * HD) & (lane < (h + 1) * HD)


def segment_matrix(width):
    r = iota((width, width), 0) // HD
    c = iota((width, width), 1) // HD
    return jnp.where(r == c, 1.0 / HD, 0.0).astype(BF)


def segment_mean(x, seg):
    hi = x.astype(BF)
    lo = (x - hi.astype(F32)).astype(BF)
    return dot_nn(hi, seg) + dot_nn(lo, seg)


class Place:
    def __init__(self, nf, nt):
        self.nf, self.nt = nf, nt
        self.nx = 2
        self.nz = nf // 2
        f = lax.axis_index("fsdp")
        t = lax.axis_index("tp")
        self.f, self.t = f, t
        self.z, self.x = f // 2, lax.rem(f, 2)
        self.y, self.c = t // 2, lax.rem(t, 2)
        self.me = f * nt + t

    def rel(self, dz=0, dx=0, dy=0, dc=0):
        z = lax.rem(self.z + dz, self.nz) if dz else self.z
        x = 1 - self.x if dx else self.x
        y = 1 - self.y if dy else self.y
        c = 1 - self.c if dc else self.c
        return (z * 2 + x, y * 2 + c)


class Copies:
    def __init__(self):
        self.sent = []

    def start(self, src, dst, send_sem, recv_sem, dev):
        cp = pltpu.make_async_remote_copy(
            src_ref=src,
            dst_ref=dst,
            send_sem=send_sem,
            recv_sem=recv_sem,
            device_id=dev,
            device_id_type=MESH,
        )
        cp.start()
        self.sent.append(cp)

    def finish(self):
        for cp in self.sent:
            cp.wait_send()
        self.sent = []


def wait_recv(dst, send_sem, recv_sem, dev):
    pltpu.make_async_remote_copy(
        src_ref=dst,
        dst_ref=dst,
        send_sem=send_sem,
        recv_sem=recv_sem,
        device_id=dev,
        device_id_type=MESH,
    ).wait_recv()


def barrier_all(pc):
    n = pc.nf * pc.nt
    bar = pltpu.get_barrier_semaphore()

    def body(r, carry):
        p = lax.rem(pc.me + r, n)
        pl.semaphore_signal(
            bar, inc=1, device_id=(p // pc.nt, lax.rem(p, pc.nt)), device_id_type=MESH
        )
        return carry

    lax.fori_loop(1, n, body, 0)
    pl.semaphore_wait(bar, n - 1)


GATHER_ORDERS = {"zxy": ("z", "x", "y"), "zyx": ("z", "y", "x")}


def axis_steps(pc, axis):
    if axis == "z":
        return [dict(dz=i) for i in range(1, pc.nz)]
    return [{"d" + axis: 1}]


def gather_plan(pc, order):
    stages = [[(dict(), 0)]]
    have = [dict()]
    for k, axis in enumerate(order):
        fresh = []
        for step in axis_steps(pc, axis):
            for b in have:
                fresh.append(dict(b, **step))
        stages.append([(b, k + 1) for b in fresh])
        have = have + fresh
    return stages


class Gather:
    def __init__(self, pc, copies, src, dst, send, recv, order, spread_tp=True):
        self.pc, self.copies = pc, copies
        self.src, self.dst, self.send, self.recv = src, dst, send, recv
        self.order = order
        self.spread_tp = spread_tp
        self.stages = gather_plan(pc, order)
        self.count = 0

    def slot(self, place):
        f, t = place
        return self.dst.at[t, f] if self.spread_tp else self.dst.at[f]

    def rsem(self, place):
        f, t = place
        return self.recv.at[t, f] if self.spread_tp else self.recv.at[f]

    def pass_on(self, block, depth):
        pc = self.pc
        place = pc.rel(**block)
        src = self.src if not block else self.slot(place)
        targets = []
        for axis in self.order[depth:]:
            targets += axis_steps(pc, axis)
        if self.spread_tp:
            targets.append(dict(dc=1))
        for step in targets:
            self.copies.start(
                src,
                self.slot(place),
                self.send.at[self.count],
                self.rsem(place),
                pc.rel(**step),
            )
            self.count += 1

    def wait(self, block):
        place = self.pc.rel(**block)
        wait_recv(self.slot(place), self.send.at[0], self.rsem(place), self.pc.rel(dc=1))

    def stage(self, k):
        for block, depth in self.stages[k]:
            if block:
                self.wait(block)
            self.pass_on(block, depth)

    def last(self):
        if self.spread_tp:
            for stage in self.stages:
                for block, depth in stage:
                    self.wait(dict(block, dc=1))


def sends_of(nz, order, spread_tp):
    n = {"z": nz - 1, "x": 1, "y": 1}
    total, have = 0, 1
    for axis in order:
        total += have * n[axis]
        have *= n[axis] + 1
    return total + (have if spread_tp else 0)


def slots_of(lens_ref):
    lens = [lens_ref[0, p] for p in range(4)]
    starts = [0]
    for p in range(3):
        starts.append(starts[-1] + lens[p])
    big = 0
    for p in range(1, 4):
        big = jnp.where(lens[p] == BIG, p, big)
    sb = 0
    for p in range(1, 4):
        sb = jnp.where(big == p, starts[p], sb)
    out = [(sb, BIG)]
    for k in range(3):
        s = jnp.where(big <= k, starts[k + 1], starts[k])
        n = jnp.where(big <= k, lens[k + 1], lens[k])
        out.append((s, n))
    return out


BASES = (0, BIG, BIG + SMALL, BIG + 2 * SMALL)


def shift_matrix(rows, cols, r):
    return jnp.where(iota((rows, cols), 1) == iota((rows, cols), 0) + r, 1.0, 0.0).astype(BF)


def load_rows(src, first, count):
    return jnp.concatenate([src[first + m] for m in range(count)], axis=0)


def pack_rows(src, dst, lens, masked=False):
    def big(j, carry):
        s = slots_of(lens)[0][0]
        r = lax.rem(s, 16)
        d = shift_matrix(128, 144, r)
        out = dot_nn(d, load_rows(src, s // 16 + j * 8, 9)).astype(BF)
        dst[pl.ds(pl.multiple_of(j * 128, 128), 128), :] = out
        return carry

    lax.fori_loop(0, BIG // 128, big, 0)

    for k in range(3):

        def small(j, carry, k=k):
            s, n = slots_of(lens)[1 + k]
            r = lax.rem(s, 16)
            d = shift_matrix(112, 128, r)
            out = dot_nn(d, load_rows(src, s // 16 + j * 7, 8))
            if masked:
                out = jnp.where(iota(out.shape, 0) + j * 112 < n, out, 0.0)
            out = out.astype(BF)
            dst[pl.ds(pl.multiple_of(BASES[1 + k] + j * 112, 16), 112), :] = out
            return carry

        lax.fori_loop(0, 4, small, 0)


def unpack_tile(src, i0, lens):
    wa, ea, wb, sb = 0, 0, 0, 4096
    for (s, n), base in zip(slots_of(lens), BASES):
        inside = (s <= i0) & (i0 < s + n)
        begins = (s > i0) & (s <= i0 + 127)
        w = base + i0 - s + MARGIN
        wa = jnp.where(inside, w, wa)
        ea = jnp.where(inside, s + n - i0, ea)
        wb = jnp.where(begins, w, wb)
        sb = jnp.where(begins, s - i0, sb)
    out = None
    row = iota((128, 144), 0)
    col = iota((128, 144), 1)
    for w, ok in ((wa, lambda: row < ea), (wb, lambda: row >= sb)):
        r = lax.rem(w, 16)
        d = jnp.where((col == row + r) & ok(), 1.0, 0.0).astype(BF)
        part = dot_nn(d, load_rows(src, w // 16, 9))
        out = part if out is None else out + part
    return out


def layer_norm_rows(x, g, b):
    mean = jnp.mean(x, axis=-1, keepdims=True)
    xc = x - mean
    var = jnp.mean(xc * xc, axis=-1, keepdims=True)
    inv = lax.rsqrt(var + EPS)
    n = xc * inv
    return n * g + b, n, inv


def own_heads(row, t, nt, width):
    out = row[:, :width]
    for k in range(1, nt):
        out = jnp.where(t == k, row[:, k * width : (k + 1) * width], out)
    return out


def build_gains(prm_all, gains, n, per):
    chunks = n * per // 128
    lane = iota((8, 128), 1)
    acc = [jnp.zeros((8, 128), F32) for _ in range(chunks)]
    for d in range(n):
        j, a = divmod(d * per, 128)
        tile = prm_all[d]
        if a:
            tile = pltpu.roll(tile, a, 1)
        acc[j] = jnp.where((lane >= a) & (lane < a + per), tile, acc[j])
        if a + per > 128:
            acc[j + 1] = jnp.where(lane < a + per - 128, tile, acc[j + 1])
    for j in range(chunks):
        gains[:, j * 128 : (j + 1) * 128] = acc[j]


def ka_kernel(
    nf, nt, orders,
    lens, tok, wa, wo, wu, wd, prm,
    h1p, qraw, kraw, qn, kn, va, lse, ob, wqkv, wo_all, wu_all, wd_all, gains, o_own,
    tok_all, h1t, wa_all, prm_all, of, op, osend,
    prm_s, prm_r, tok_s, tok_r, wa_s, wa_r, wo_s, wo_r, wu_s, wu_r, wd_s, wd_r, o_s, o_r, loc,
):
    pc = Place(nf, nt)
    n = nf * nt
    cps = Copies()
    rows, width = tok.shape
    hw = qn.shape[1]
    barrier_all(pc)

    cps.start(tok, tok_all.at[pc.t], tok_s.at[0], tok_r.at[pc.t], pc.rel(dy=1))
    cps.start(tok, tok_all.at[pc.t], tok_s.at[1], tok_r.at[pc.t], pc.rel(dc=1))

    def push_prm(r, carry):
        p = lax.rem(pc.me + r, n)
        pltpu.make_async_remote_copy(
            src_ref=prm, dst_ref=prm_all.at[pc.me], send_sem=prm_s.at[r], recv_sem=prm_r.at[pc.me],
            device_id=(p // nt, lax.rem(p, nt)), device_id_type=MESH,
        ).start()
        return carry

    lax.fori_loop(1, n, push_prm, 0)
    ga = Gather(pc, cps, wa, wa_all, wa_s, wa_r, ("z", "x"), False)
    gw = [
        Gather(pc, cps, wo, wo_all, wo_s, wo_r, orders[0]),
        Gather(pc, cps, wu, wu_all, wu_s, wu_r, orders[1]),
        Gather(pc, cps, wd, wd_all, wd_s, wd_r, orders[2]),
    ]
    ga.stage(0)
    for g in gw:
        g.stage(0)
    local = []
    for src, dst in ((tok, tok_all.at[pc.t]), (wa, wa_all.at[pc.f]), (wo, wo_all.at[pc.t, pc.f]),
                     (wu, wu_all.at[pc.t, pc.f]), (wd, wd_all.at[pc.t, pc.f])):
        cp = pltpu.make_async_copy(src, dst, loc.at[len(local)])
        cp.start()
        local.append(cp)
    prm_all[pc.me] = prm[...]

    h1t[4 * rows // 16 :] = jnp.zeros((h1t.shape[0] - 4 * rows // 16, 16, width), BF)

    def wait_prm(r, carry):
        p = lax.rem(pc.me + r, n)
        wait_recv(prm_all.at[p], prm_s.at[0], prm_r.at[p], (p // nt, lax.rem(p, nt)))
        return carry

    lax.fori_loop(1, n, wait_prm, 0)
    build_gains(prm_all, gains, n, width // n)
    gain_one, shift_one = gains[0:1, :], gains[1:2, :]

    def norm_block(t):
        def body(j, carry):
            at = pl.ds(pl.multiple_of(j * 128, 128), 128)
            out, _, _ = layer_norm_rows(tok_all[t, at, :].astype(F32), gain_one, shift_one)
            h1t[pl.ds(t * (rows // 16) + j * 8, 8)] = out.astype(BF).reshape(8, 16, width)
            return carry

        lax.fori_loop(0, rows // 128, body, 0)

    def wait_tok(t):
        wait_recv(tok_all.at[t], tok_s.at[0], tok_r.at[t], pc.rel(dc=1))

    for cp in local:
        cp.wait()
    norm_block(pc.t)
    t_core, t_y, t_diag = pc.rel(dc=1)[1], pc.rel(dy=1)[1], pc.rel(dy=1, dc=1)[1]
    wait_tok(t_core)
    norm_block(t_core)
    ga.stage(1)
    for g in gw:
        g.stage(1)
    wait_tok(t_y)
    cps.start(tok_all.at[t_y], tok_all.at[t_y], tok_s.at[2], tok_r.at[t_y], pc.rel(dc=1))
    norm_block(t_y)
    ga.stage(2)
    wait_tok(t_diag)
    norm_block(t_diag)

    pack_rows(h1t, h1p, lens)
    seg = segment_matrix(hw)
    gq = own_heads(gains[4:5, :], pc.t, nt, hw)
    gk = own_heads(gains[5:6, :], pc.t, nt, hw)
    w_full = wa_all[...].reshape(width, 3 * hw)
    for i in range(3):
        wqkv[i] = w_full[:, i * hw : (i + 1) * hw]

    qt = LP // 4

    def project(j, carry):
        at = pl.ds(pl.multiple_of(j * qt, 16), qt)
        h = h1p[at, :]
        for i, (raw, normed, g) in enumerate(((qraw, qn, gq), (kraw, kn, gk))):
            q = dot_nn(h, wqkv[i])
            raw[at, :] = q
            qc = q - segment_mean(q, seg)
            inv = lax.rsqrt(segment_mean(qc * qc, seg) + EPS)
            normed[at, :] = (qc * inv * g).astype(BF)
        v = dot_nn(h, wqkv[2]).astype(BF)
        va[at, :hw] = v
        return carry

    lax.fori_loop(0, 4, project, 0)
    va[:, hw:] = jnp.ones((LP, va.shape[1] - hw), BF)
    head, tail = MARGIN // 16, (MARGIN + LP) // 16
    op[:head] = jnp.zeros((head, 16, hw), BF)
    op[tail:] = jnp.zeros((op.shape[0] - tail, 16, hw), BF)

    for g in gw:
        g.stage(2)

    def attend(at, keys, h, limit):
        nrow = at.size
        q = jnp.where(head_mask(nrow, hw, h), qn[at, :], jnp.zeros((), BF))
        s = dot_nt(q, kn[keys, :])
        p = jnp.exp2(s * EXP_SCALE)
        if limit is not None:
            p = jnp.where(iota(p.shape, 1) < limit, p, 0.0)
        oa = dot_nn(p.astype(BF), va[keys, :])
        total = oa[:, hw : hw + 1]
        o = oa[:, :hw] * (1.0 / total)
        l2 = jnp.log2(total)
        lane = iota((nrow, 128), 1)
        if h == 0:
            of[at, :] = o
            lse[at, :] = jnp.broadcast_to(l2, (nrow, 128))
        else:
            of[at, :] = jnp.where(head_mask(nrow, hw, h), o, of[at, :])
            lse[at, :] = jnp.where(lane == h, l2, lse[at, :])

    nh = hw // HD
    for h in range(nh):
        def big(j, carry, h=h):
            attend(pl.ds(pl.multiple_of(j * 512, 512), 512), pl.ds(0, BIG), h, None)
            return carry

        lax.fori_loop(0, BIG // 512, big, 0)

        for k in range(3):
            at = pl.ds(BASES[1 + k], SMALL)
            attend(at, at, h, slots_of(lens)[1 + k][1])
        if h == 0:
            for g in gw:
                g.stage(3)

    ob[...] = of[...].astype(BF)
    op[head:tail] = ob[...].reshape(LP // 16, 16, hw)

    def unpack(i, carry):
        out = unpack_tile(op, i * 128, lens)
        osend[i // 4, pl.ds(pl.multiple_of(lax.rem(i, 4) * 128, 128), 128), :] = out.astype(BF)
        return carry

    lax.fori_loop(0, 16, unpack, 0)
    peers = [pc.rel(dy=1), pc.rel(dy=1, dc=1), pc.rel(dc=1)]
    for i, dev in enumerate(peers):
        cps.start(osend.at[dev[1]], o_own.at[pc.t], o_s.at[i], o_r.at[pc.t], dev)
    cp = pltpu.make_async_copy(osend.at[pc.t], o_own.at[pc.t], loc.at[0])
    cp.start()
    cp.wait()
    for g in gw:
        g.last()
    for dev in peers:
        wait_recv(o_own.at[dev[1]], o_s.at[0], o_r.at[dev[1]], dev)

    def wait_prm_sent(r, carry):
        p = lax.rem(pc.me + r, n)
        pltpu.make_async_remote_copy(
            src_ref=prm, dst_ref=prm_all.at[pc.me], send_sem=prm_s.at[r], recv_sem=prm_r.at[pc.me],
            device_id=(p // nt, lax.rem(p, nt)), device_id_type=MESH,
        ).wait_send()
        return carry

    lax.fori_loop(1, n, wait_prm_sent, 0)
    cps.finish()


def call_ka(nf, nt, lens, tok, wa, wo, wu, wd, prm):
    nz = nf // 2
    rows, width = tok.shape
    r = wa.shape[0]
    hw = wa.shape[1] // 3
    cu, cd = wu.shape[1], wd.shape[1]
    orders = (("z", "x", "y"), ("z", "y", "x"), ("z", "x", "y"))
    S = jax.ShapeDtypeStruct
    vm = pl.BlockSpec(memory_space=pltpu.VMEM)
    hb = pl.BlockSpec(memory_space=pl.ANY)
    outs = [
        (S((LP, width), BF), vm), (S((LP, hw), F32), vm), (S((LP, hw), F32), vm),
        (S((LP, hw), BF), vm), (S((LP, hw), BF), vm), (S((LP, 256), BF), vm),
        (S((LP, 128), F32), vm), (S((LP, hw), BF), vm), (S((3, width, hw), BF), vm),
        (S((nt, nf, r, hw), BF), hb), (S((nt, nf, r, cu), BF), hb), (S((nt, nf, r, cd), BF), hb),
        (S((8, width), F32), vm), (S((nt, rows, hw), BF), vm),
    ]
    dma = pltpu.SemaphoreType.DMA
    sends = [sends_of(nz, o, True) for o in orders]
    scratch = [
        pltpu.VMEM((nt, rows, width), BF), pltpu.VMEM(((nt * rows + 192) // 16, 16, width), BF),
        pltpu.VMEM((nf, r, 3 * hw), BF), pltpu.VMEM((nf * nt, 8, 128), F32),
        pltpu.VMEM((LP, hw), F32), pltpu.VMEM(((MARGIN + LP + 160) // 16, 16, hw), BF), pltpu.VMEM((nt, rows, hw), BF),
        dma((nf * nt,)), dma((nf * nt,)), dma((3,)), dma((nt,)),
        dma((sends_of(nz, ("z", "x"), False),)), dma((nf,)),
        dma((sends[0],)), dma((nt, nf)), dma((sends[1],)), dma((nt, nf)), dma((sends[2],)), dma((nt, nf)),
        dma((3,)), dma((nt,)), dma((5,)),
    ]
    return pl.pallas_call(
        functools.partial(ka_kernel, nf, nt, orders),
        out_shape=[o[0] for o in outs],
        in_specs=[pl.BlockSpec(memory_space=pltpu.SMEM), vm, vm, hb, hb, hb, vm],
        out_specs=[o[1] for o in outs],
        scratch_shapes=scratch,
        compiler_params=pltpu.CompilerParams(
            collective_id=0, has_side_effects=True, vmem_limit_bytes=56 << 20
        ),
    )(lens, tok, wa, wo, wu, wd, prm)


def scatter_names(order):
    return order


class Scatter:
    def __init__(self, pc, copies, part, own, rc, ra, rb, rz, send, recv, order, loc):
        self.pc, self.copies = pc, copies
        self.part, self.own, self.rc, self.ra, self.rb, self.rz = part, own, rc, ra, rb, rz
        self.send, self.recv, self.order, self.loc = send, recv, order, loc
        self.count = 0
        self.got = 0
        self.waits = []
        self.local = []

    def put(self, src, dst, step):
        k = self.count
        self.copies.start(src, dst, self.send.at[k], self.recv.at[k], self.pc.rel(**step))
        self.waits.append((dst, k, self.pc.rel(**step)))
        self.count += 1

    def arrive(self):
        for dst, k, dev in self.waits:
            wait_recv(dst, self.send.at[k], self.recv.at[k], dev)
        self.waits = []

    def add(self, dst, src):
        rows = dst.shape[0]

        def body(j, carry):
            at = pl.ds(pl.multiple_of(j * 32, 32), 32)
            dst[at, :] = (dst[at, :].astype(F32) + src[at, :].astype(F32)).astype(BF)
            return carry

        lax.fori_loop(0, rows // 32, body, 0)

    def start(self):
        pc = self.pc
        for y in range(2):
            self.put(self.part.at[y * 2 + 1 - pc.c], self.rc.at[y], dict(dc=1))
        for y in range(2):
            cp = pltpu.make_async_copy(self.part.at[y * 2 + pc.c], self.own.at[y], self.loc.at[y])
            cp.start()
            self.local.append(cp)

    def block(self, y, z, x):
        return self.own.at[y, z * 2 + x]

    def stage_a(self):
        pc = self.pc
        self.arrive()
        for cp in self.local:
            cp.wait()
        first = self.order[0]

        def add_core(i, carry):
            self.add(self.own.at[i // pc.nf, lax.rem(i, pc.nf)], self.rc.at[i // pc.nf, lax.rem(i, pc.nf)])
            return carry

        lax.fori_loop(0, 2 * pc.nf, add_core, 0)
        if first == "y":
            for z in range(pc.nz):
                for x in range(2):
                    self.put(self.block(1 - pc.y, z, x), self.ra.at[z * 2 + x], dict(dy=1))
        else:
            for z in range(pc.nz):
                for y in range(2):
                    self.put(self.block(y, z, 1 - pc.x), self.ra.at[z * 2 + y], dict(dx=1))

    def stage_b(self):
        pc = self.pc
        self.arrive()
        first = self.order[0]

        def add_a(i, carry):
            z, o = i // 2, lax.rem(i, 2)
            dst = self.block(pc.y, z, o) if first == "y" else self.block(o, z, pc.x)
            self.add(dst, self.ra.at[i])
            return carry

        lax.fori_loop(0, 2 * pc.nz, add_a, 0)
        for z in range(pc.nz):
            if first == "y":
                self.put(self.block(pc.y, z, 1 - pc.x), self.rb.at[z], dict(dx=1))
            else:
                self.put(self.block(1 - pc.y, z, pc.x), self.rb.at[z], dict(dy=1))

    def stage_c(self):
        pc = self.pc
        self.arrive()

        def add_b(z, carry):
            self.add(self.block(pc.y, z, pc.x), self.rb.at[z])
            return carry

        lax.fori_loop(0, pc.nz, add_b, 0)
        self.to_z(lambda z: self.block(pc.y, z, pc.x))

    def to_z(self, block):
        pc = self.pc
        for dz in range(1, pc.nz):
            z = lax.rem(pc.z + dz, pc.nz)
            self.put(block(z), self.rz.at[dz], dict(dz=dz))

    def finish(self, out, block):
        self.arrive()
        rows = out.shape[0]

        def body(j, carry):
            at = pl.ds(pl.multiple_of(j * 32, 32), 32)
            total = block[at, :].astype(F32)
            for dz in range(1, self.pc.nz):
                total = total + self.rz[dz, at, :].astype(F32)
            out[at, :] = total
            return carry

        lax.fori_loop(0, rows // 32, body, 0)


def kc_kernel(
    nf, nt,
    lens, dos, h1p, qraw, kraw, qn, kn, va, lse, ob, wqkv, gains, gwo, gwu, gwd, tok, dm, part,
    dx_out, gqkv_out, gwo_out, gwu_out, gwd_out, small_out,
    dot_all, dop, delta, dq, dk, dv, dqkv, dhp, dhs, dhr, dhy, gq_own, gq_x, gq_z, sm_t, sm_f, sm_sum,
    o_own, o_rc, o_ra, o_rb, o_rz, u_own, u_rc, u_ra, u_rb, u_rz, d_own, d_rc, d_ra, d_rb, d_rz,
    do_s, do_r, o_s, o_r, u_s, u_r, d_s, d_r, dh_s, dh_r, gq_s, gq_r, st_s, st_r, sf_s, sf_r, loc,
):
    pc = Place(nf, nt)
    cps = Copies()
    rows, width = tok.shape
    hw = qn.shape[1]
    nh = hw // HD
    groups = rows // 16
    barrier_all(pc)

    peers = [pc.rel(dy=1), pc.rel(dy=1, dc=1), pc.rel(dc=1)]
    own_groups = pl.ds(pc.t * groups, groups)
    for i, dev in enumerate(peers):
        cps.start(dos.at[dev[1]], dot_all.at[own_groups], do_s.at[i], do_r.at[pc.t], dev)
    cp = pltpu.make_async_copy(dos.at[pc.t], dot_all.at[own_groups], loc.at[6])
    cp.start()
    sc = [
        Scatter(pc, cps, gwd, d_own, d_rc, d_ra, d_rb, d_rz, d_s, d_r, ("y", "x"), loc.at[0:2]),
        Scatter(pc, cps, gwu, u_own, u_rc, u_ra, u_rb, u_rz, u_s, u_r, ("x", "y"), loc.at[2:4]),
        Scatter(pc, cps, gwo, o_own, o_rc, o_ra, o_rb, o_rz, o_s, o_r, ("y", "x"), loc.at[4:6]),
    ]
    for s in sc:
        s.start()
    tail = 4 * groups
    dot_all[tail:] = jnp.zeros((dot_all.shape[0] - tail, 16, hw), BF)
    for acc in (dq, dk, dv):
        acc[...] = jnp.zeros(acc.shape, F32)
    cp.wait()
    for dev in peers:
        wait_recv(dot_all.at[pl.ds(dev[1] * groups, groups)], do_s.at[0], do_r.at[dev[1]], dev)
    pack_rows(dot_all, dop, lens, True)

    dlt = LP // 4

    def deltas(j, carry):
        at = pl.ds(pl.multiple_of(j * dlt, 16), dlt)
        prod = dop[at, :].astype(F32) * ob[at, :].astype(F32)
        lane = iota((dlt, 128), 1)
        out = jnp.zeros((dlt, 128), F32)
        for h in range(nh):
            part_h = jnp.where(head_mask(dlt, hw, h), prod, 0.0)
            out = jnp.where(lane == h, jnp.sum(part_h, axis=-1, keepdims=True), out)
        delta[at, :] = out
        return carry

    lax.fori_loop(0, 4, deltas, 0)

    def back(at, keys, h, limit):
        nrow, nkey = at.size, keys.size
        zero = jnp.zeros((), BF)
        hm = head_mask(nrow, hw, h)
        q = jnp.where(hm, qn[at, :], zero)
        s = dot_nt(q, kn[keys, :])
        p = jnp.exp2(s * EXP_SCALE - lse[at, h : h + 1])
        if limit is not None:
            p = jnp.where(iota(p.shape, 1) < limit, p, 0.0)
        g = jnp.where(hm, dop[at, :], zero)
        dp = dot_nt(g, va[keys, :hw])
        ds = (p * (dp - delta[at, h : h + 1])).astype(BF)
        dv[keys, :] += dot_tn(p.astype(BF), g)
        dk[keys, :] += dot_tn(ds, q)
        km = jnp.where(head_mask(nkey, hw, h), kn[keys, :], zero)
        dq[at, :] += dot_nn(ds, km)

    for h in range(nh):
        def big(j, carry, h=h):
            back(pl.ds(pl.multiple_of(j * 256, 256), 256), pl.ds(0, BIG), h, None)
            return carry

        lax.fori_loop(0, BIG // 256, big, 0)
        for k in range(3):
            at = pl.ds(BASES[1 + k], SMALL)
            back(at, at, h, slots_of(lens)[1 + k][1])
        for s in sc:
            if h == 0:
                s.stage_a()
            elif h == 1:
                s.stage_b()

    head, mid = MARGIN // 16, (MARGIN + LP) // 16
    h1_copy = pltpu.make_async_copy(h1p, dhp.at[head:mid], loc.at[7])
    h1_copy.start()
    seg = segment_matrix(hw)
    gq = own_heads(gains[4:5, :], pc.t, nt, hw)
    gk = own_heads(gains[5:6, :], pc.t, nt, hw)
    small_out[...] = jnp.zeros(small_out.shape, F32)

    def norms(j, carry):
        at = pl.ds(pl.multiple_of(j * dlt, 16), dlt)
        sums = []
        for i, (raw, grad, g) in enumerate(((qraw, dq, gq), (kraw, dk, gk))):
            q = raw[at, :]
            qc = q - segment_mean(q, seg)
            inv = lax.rsqrt(segment_mean(qc * qc, seg) + EPS)
            n = qc * inv
            e = grad[at, :] * 0.125
            c = e * g
            out = inv * (c - segment_mean(c, seg) - n * segment_mean(c * n, seg))
            dqkv[i, at, :] = out.astype(BF)
            sums.append(jnp.sum(e * n, axis=0, keepdims=True))
        dqkv[2, at, :] = dv[at, :].astype(BF)
        return (carry[0] + sums[0], carry[1] + sums[1])

    none = jnp.zeros((1, hw), F32)
    sum_q, sum_k = lax.fori_loop(0, 4, norms, (none, none))
    small_out[4:5, :hw] = sum_q
    small_out[5:6, :hw] = sum_k
    placed = pltpu.roll(small_out[...], pc.t * hw, 1)
    small_out[...] = placed + part[...]

    dhp[:head] = jnp.zeros((head, 16, width), BF)
    dhp[mid:] = jnp.zeros((dhp.shape[0] - mid, 16, width), BF)

    r = width // nf
    h1_copy.wait()
    for i in range(3):
        g = dot_tn(dhp[head:mid].reshape(LP, width), dqkv[i]).astype(BF)
        gq_own[i] = g.reshape(nf, r, hw)
    nq = 0
    waits = []
    for i in range(3):
        for z in range(pc.nz):
            cps.start(gq_own.at[i, z * 2 + 1 - pc.x], gq_x.at[i, z], gq_s.at[nq], gq_r.at[nq], pc.rel(dx=1))
            waits.append((gq_x.at[i, z], nq, pc.rel(dx=1)))
            nq += 1

    def project(j, carry):
        at = pl.ds(pl.multiple_of(j * dlt, 16), dlt)
        total = dot_nt(dqkv[0, at, :], wqkv[0])
        total += dot_nt(dqkv[1, at, :], wqkv[1])
        total += dot_nt(dqkv[2, at, :], wqkv[2])
        dhp[pl.ds(head + j * (dlt // 16), dlt // 16)] = total.astype(BF).reshape(dlt // 16, 16, width)
        return carry

    lax.fori_loop(0, 4, project, 0)

    def unpack(i, carry):
        out = unpack_tile(dhp, i * 128, lens)
        dhs[i // 4, pl.ds(pl.multiple_of(lax.rem(i, 4) * 128, 128), 128), :] = out.astype(BF)
        return carry

    lax.fori_loop(0, 16, unpack, 0)
    for y in range(2):
        src = (1 - pc.y if y == 0 else pc.y) * 2 + 1 - pc.c
        cps.start(dhs.at[src], dhr.at[y], dh_s.at[y], dh_r.at[y], pc.rel(dc=1))

    for s in sc:
        s.stage_c()

    def add_rows(dst, src):
        def body(j, carry):
            at = pl.ds(pl.multiple_of(j * 64, 64), 64)
            dst[at, :] = (dst[at, :].astype(F32) + src[at, :].astype(F32)).astype(BF)
            return carry

        lax.fori_loop(0, rows // 64, body, 0)

    t_far, t_own = (1 - pc.y) * 2 + pc.c, pc.t
    wait_recv(dhr.at[0], dh_s.at[0], dh_r.at[0], pc.rel(dc=1))
    add_rows(dhs.at[t_far], dhr.at[0])
    cps.start(dhs.at[t_far], dhy, dh_s.at[2], dh_r.at[2], pc.rel(dy=1))

    def add_block(dst, src):
        dst[...] = (dst[...].astype(F32) + src[...].astype(F32)).astype(BF)

    for dst, k, dev in waits:
        wait_recv(dst, gq_s.at[k], gq_r.at[k], dev)
    waits = []
    for i in range(3):
        for z in range(pc.nz):
            add_block(gq_own.at[i, z * 2 + pc.x], gq_x.at[i, z])
        for dz in range(1, pc.nz):
            z = lax.rem(pc.z + dz, pc.nz)
            cps.start(gq_own.at[i, z * 2 + pc.x], gq_z.at[i, dz], gq_s.at[nq], gq_r.at[nq], pc.rel(dz=dz))
            waits.append((gq_z.at[i, dz], nq, pc.rel(dz=dz)))
            nq += 1

    wait_recv(dhr.at[1], dh_s.at[1], dh_r.at[1], pc.rel(dc=1))
    add_rows(dhs.at[t_own], dhr.at[1])
    wait_recv(dhy, dh_s.at[2], dh_r.at[2], pc.rel(dy=1))
    gain_one = gains[0:1, :]

    def last(j, carry):
        at = pl.ds(pl.multiple_of(j * 128, 128), 128)
        e = dhs[t_own, at, :].astype(F32) + dhy[at, :].astype(F32)
        x = tok[at, :].astype(F32)
        _, n, inv = layer_norm_rows(x, gain_one, 0.0)
        c = e * gain_one
        grad = inv * (
            c - jnp.mean(c, axis=-1, keepdims=True) - n * jnp.mean(c * n, axis=-1, keepdims=True)
        )
        dx_out[at, :] = dm[at, :] + grad
        return (carry[0] + jnp.sum(e * n, axis=0, keepdims=True), carry[1] + jnp.sum(e, axis=0, keepdims=True))

    none = jnp.zeros((1, width), F32)
    g1, b1 = lax.fori_loop(0, rows // 128, last, (none, none))
    small_out[0:1, :] += g1
    small_out[1:2, :] += b1

    sm_sum[...] = small_out[...]
    for i, dev in enumerate(peers):
        cps.start(sm_sum, sm_t.at[pc.t], st_s.at[i], st_r.at[pc.t], dev)
    total = small_out[...]
    for dev in peers:
        wait_recv(sm_t.at[dev[1]], st_s.at[0], st_r.at[dev[1]], dev)
        total = total + sm_t[dev[1]]
    small_out[...] = total
    far = [(lax.rem(pc.f + i, nf), pc.t) for i in range(1, nf)]
    sm_f[0] = total
    for i, dev in enumerate(far):
        cps.start(sm_f.at[0], sm_f.at[1 + i], sf_s.at[i], sf_r.at[i], dev)

    for dst, k, dev in waits:
        wait_recv(dst, gq_s.at[k], gq_r.at[k], dev)
    for i in range(3):
        out = gq_own[i, pc.f].astype(F32)
        for dz in range(1, pc.nz):
            out = out + gq_z[i, dz].astype(F32)
        gqkv_out[i] = out
    for s, out in zip(sc, (gwd_out, gwu_out, gwo_out)):
        s.finish(out, s.own.at[pc.y, pc.f])
    for i, dev in enumerate(far):
        wait_recv(sm_f.at[1 + i], sf_s.at[i], sf_r.at[i], dev)
        total = total + sm_f[1 + i]
    small_out[...] = total
    cps.finish()


def call_kc(nf, nt, lens, dos, h1p, qraw, kraw, qn, kn, va, lse, ob, wqkv, gains, gwo, gwu, gwd, tok, dm, part):
    nz = nf // 2
    rows, width = tok.shape
    hw = qn.shape[1]
    r = width // nf
    S = jax.ShapeDtypeStruct
    vm = pl.BlockSpec(memory_space=pltpu.VMEM)
    hb = pl.BlockSpec(memory_space=pl.ANY)
    dma = pltpu.SemaphoreType.DMA
    V = pltpu.VMEM
    outs = [S((rows, width), F32), S((3, r, hw), F32)] + [S((r, g.shape[3]), F32) for g in (gwo, gwu, gwd)] + [S((8, width), F32)]
    scratch = [
        V(((nt * rows + 192) // 16, 16, hw), BF), V((LP, hw), BF), V((LP, 128), F32),
        V((LP, hw), F32), V((LP, hw), F32), V((LP, hw), F32), V((3, LP, hw), BF),
        V(((MARGIN + LP + 160) // 16, 16, width), BF), V((nt, rows, width), BF), V((2, rows, width), BF),
        V((rows, width), BF), V((3, nf, r, hw), BF), V((3, nz, r, hw), BF), V((3, nz, r, hw), BF),
        V((nt, 8, width), F32), V((nf, 8, width), F32), V((8, width), F32),
    ]
    for g in (gwo, gwu, gwd):
        c = g.shape[3]
        scratch += [V((2, nf, r, c), BF), V((2, nf, r, c), BF), V((nf, r, c), BF), V((nz, r, c), BF), V((nz, r, c), BF)]
    ns = 2 + 2 * nz + nz + nz
    scratch += [
        dma((3,)), dma((nt,)), dma((ns,)), dma((ns,)), dma((ns,)), dma((ns,)), dma((ns,)), dma((ns,)),
        dma((3,)), dma((3,)), dma((6 * nz,)), dma((6 * nz,)), dma((3,)), dma((nt,)), dma((nf,)), dma((nf,)), dma((8,)),
    ]
    return pl.pallas_call(
        functools.partial(kc_kernel, nf, nt),
        out_shape=outs,
        in_specs=[pl.BlockSpec(memory_space=pltpu.SMEM)] + [vm, hb] + [vm] * 9 + [hb] * 3 + [vm] * 3,
        out_specs=[vm] * 6,
        scratch_shapes=scratch,
        compiler_params=pltpu.CompilerParams(
            collective_id=1, has_side_effects=True, vmem_limit_bytes=63 << 20
        ),
    )(lens, dos, h1p, qraw, kraw, qn, kn, va, lse, ob, wqkv, gains, gwo, gwu, gwd, tok, dm, part)


def middle(o_own, inputs, valid, w_out, w_up, w_down, gain, shift, cotangent):
    f32 = dict(preferred_element_type=jnp.float32)
    branch = valid * jnp.einsum("tlh,tdh->ld", o_own, w_out, **f32)
    mid = inputs + branch
    hidden, normed, inverse = normalise(mid, gain, shift)
    hidden = hidden.astype(jnp.bfloat16)
    up = jnp.einsum("ld,tdf->tlf", hidden, w_up, **f32)
    act = jax.nn.gelu(up, approximate=False).astype(jnp.bfloat16)
    mlp = valid * jnp.einsum("tlf,tdf->ld", act, w_down, **f32)
    result = (mid + mlp).astype(jnp.bfloat16)
    grad_y = cotangent.astype(jnp.float32) * valid
    grad_low = grad_y.astype(jnp.bfloat16)
    grad_down = jnp.einsum("ld,tlf->tdf", grad_low, act, **f32).astype(jnp.bfloat16)
    grad_act = jnp.einsum("ld,tdf->tlf", grad_low, w_down, **f32)
    grad_pre = (grad_act * gelu_slope(up)).astype(jnp.bfloat16)
    grad_up = jnp.einsum("ld,tlf->tdf", hidden, grad_pre, **f32).astype(jnp.bfloat16)
    grad_hidden = jnp.einsum("tlf,tdf->ld", grad_pre, w_up, **f32)
    unit = grad_hidden * gain
    grad_mid = grad_y + inverse * (
        unit
        - jnp.mean(unit, axis=-1, keepdims=True)
        - normed * jnp.mean(unit * normed, axis=-1, keepdims=True)
    )
    grad_z = (valid * grad_mid).astype(jnp.bfloat16)
    grad_out = jnp.einsum("ld,tlh->tdh", grad_z, o_own, **f32).astype(jnp.bfloat16)
    grad_mix = jnp.einsum("ld,tdh->tlh", grad_z, w_out, **f32).astype(jnp.bfloat16)
    sums = jnp.stack(
        [
            jnp.sum(valid * inputs * inputs),
            jnp.sum(branch * branch),
            jnp.sum(valid * mid * mid),
            jnp.sum(mlp * mlp),
            jnp.sum(valid),
        ]
    )
    width = inputs.shape[1]
    part = jnp.zeros((8, width), jnp.float32)
    part = part.at[2].set(jnp.sum(grad_hidden * normed, axis=0))
    part = part.at[3].set(jnp.sum(grad_hidden, axis=0))
    part = part.at[6, :5].set(sums)
    return result, grad_mid, grad_mix, grad_out, grad_up, grad_down, part


def local_fused(nf, nt, args):
    (tokens, lengths, pictures, w_query, w_key, w_value, w_out, w_up, w_down) = args[:9]
    smalls, cotangent = args[9:15], args[15]
    rows, width = tokens.shape[1:]
    hw = w_query.shape[1]
    per = smalls[0].shape[0]
    place = lax.axis_index("fsdp") * nt + lax.axis_index("tp")
    prm = jnp.zeros((8, 128), jnp.float32).at[:6, :per].set(jnp.stack(smalls))
    attn = jnp.concatenate([w_query, w_key, w_value], axis=1)
    (h1p, qraw, kraw, qn, kn, va, lse, ob, wqkv, wo_all, wu_all, wd_all, gains, o_own) = call_ka(
        nf, nt, lengths, tokens[0], attn, w_out.T, w_up, w_down.T, prm
    )
    slots = lax.axis_index("tp") * rows + jnp.arange(rows, dtype=jnp.int32)
    valid = (slots < jnp.sum(lengths)).astype(jnp.float32)[:, None]
    full = lambda w: w.reshape(nt, width, w.shape[3])
    result, grad_mid, grad_mix, grad_out, grad_up, grad_down, part = middle(
        o_own, tokens[0].astype(jnp.float32), valid, full(wo_all), full(wu_all), full(wd_all),
        gains[2], gains[3], cotangent[0],
    )
    split = lambda g: g.reshape(nt, nf, width // nf, g.shape[2])
    grad_in, gqkv, gwo, gwu, gwd, small = call_kc(
        nf, nt, lengths, grad_mix.reshape(nt, rows // 16, 16, hw), h1p.reshape(LP // 16, 16, width),
        qraw, kraw, qn, kn, va, lse, ob, wqkv, gains, split(grad_out), split(grad_up), split(grad_down),
        tokens[0], grad_mid, part,
    )
    own = lax.dynamic_slice_in_dim(small, place * per, per, 1)
    statistics = jnp.sqrt(small[6, :4] / (small[6, 4] * width))
    return (
        result[None], grad_in[None], gqkv[0], gqkv[1], gqkv[2], gwo.T, gwu, gwd.T,
        own[0], own[1], own[2], own[3], own[4], own[5], statistics,
    )


def solution(mesh):
    nf, nt = mesh.shape["fsdp"], mesh.shape["tp"]

    def local(*args):
        tokens, w_query = args[0], args[3]
        if nt == 4 and tokens.shape[0] == 1 and tokens.shape[1] == 512 and w_query.shape[0] % 32 == 0:
            return local_fused(nf, nt, args)
        return local_plain(*args)

    in_specs = (
        P("fsdp", "tp", None),
        P("fsdp", None),
        P("fsdp", None),
        P("fsdp", "tp"),
        P("fsdp", "tp"),
        P("fsdp", "tp"),
        P("tp", "fsdp"),
        P("fsdp", "tp"),
        P("tp", "fsdp"),
        P(("fsdp", "tp")),
        P(("fsdp", "tp")),
        P(("fsdp", "tp")),
        P(("fsdp", "tp")),
        P(("fsdp", "tp")),
        P(("fsdp", "tp")),
        P("fsdp", "tp", None),
    )
    out_specs = (
        P("fsdp", "tp", None),
        P("fsdp", "tp", None),
        P("fsdp", "tp"),
        P("fsdp", "tp"),
        P("fsdp", "tp"),
        P("tp", "fsdp"),
        P("fsdp", "tp"),
        P("tp", "fsdp"),
        P(("fsdp", "tp")),
        P(("fsdp", "tp")),
        P(("fsdp", "tp")),
        P(("fsdp", "tp")),
        P(("fsdp", "tp")),
        P(("fsdp", "tp")),
        P(),
    )
    return jax.shard_map(local, mesh=mesh, in_specs=in_specs, out_specs=out_specs, check_vma=False)
```

```python
import functools

import jax
import jax.numpy as jnp
from jax import lax
from jax.experimental import pallas as pl
from jax.experimental.pallas import tpu as pltpu
from jax.sharding import PartitionSpec as P

HD = 64


EPS = 1e-06
ROOT_HALF = 0.7071067811865476
DENSITY = 0.3989422804014327


def normalise(values, scaling, offset):
    centre = jnp.mean(values, axis=-1, keepdims=True)
    centred = values - centre
    spread = jnp.mean(centred * centred, axis=-1, keepdims=True)
    inverse = lax.rsqrt(spread + EPS)
    normed = centred * inverse
    return (normed * scaling + offset, normed, inverse)


def normalise_back(grad_out, normed, inverse, scaling):
    grad_unit = grad_out * scaling
    grad_values = inverse * (
        grad_unit
        - jnp.mean(grad_unit, axis=-1, keepdims=True)
        - normed * jnp.mean(grad_unit * normed, axis=-1, keepdims=True)
    )
    return (grad_values, jnp.sum(grad_out * normed, axis=(0, 1)), jnp.sum(grad_out, axis=(0, 1)))


def gelu_slope(values):
    return (
        0.5 * (1.0 + jax.scipy.special.erf(values * ROOT_HALF))
        + values * jnp.exp(-0.5 * values * values) * DENSITY
    )


def gather_tokens(values):
    return lax.all_gather(values, "tp", axis=1, tiled=True)


def gather_grads(values):
    return lax.all_gather(values, "tp", axis=1, tiled=True)


def reduce_tokens(values):
    return lax.psum_scatter(
        values.astype(jnp.bfloat16), "tp", scatter_dimension=1, tiled=True
    ).astype(jnp.float32)


def reduce_grads(values):
    return lax.psum_scatter(
        values.astype(jnp.bfloat16), "tp", scatter_dimension=1, tiled=True
    ).astype(jnp.float32)


def block_scores(query, keyed, picture_query, picture_key, key_mask):
    raw_scores = jnp.einsum("qhd,khd->hqk", query, keyed, preferred_element_type=jnp.float32)
    allowed = (picture_query[:, None] == picture_key[None, :]) & (key_mask[None, :] > 0)
    return jnp.where(allowed[None], raw_scores * query.shape[-1] ** (-0.5), -1e30)


def forward_row(packed):
    query_row, key_row, value_row, picture_row, mask_row = packed
    full_len = query_row.shape[0]
    block_len = min(512, full_len)
    block_count = full_len // block_len

    def forward_one_block(packed_block):
        query_block, picture_block = packed_block
        scores = block_scores(query_block, key_row, picture_block, picture_row, mask_row)
        highest = jnp.max(scores, axis=-1, keepdims=True)
        logsum = highest + jnp.log(jnp.sum(jnp.exp(scores - highest), axis=-1, keepdims=True))
        probability = jnp.exp(scores - logsum).astype(jnp.bfloat16)
        mixture = jnp.einsum(
            "hqk,khd->qhd", probability, value_row, preferred_element_type=jnp.float32
        )
        return (mixture, logsum)

    query_blocks = query_row.reshape((block_count, block_len) + query_row.shape[1:])
    return lax.map(forward_one_block, (query_blocks, picture_row.reshape(block_count, block_len)))


def backward_row(packed):
    query_row, key_row, value_row, picture_row, mask_row, grad_row, logsum_row = packed
    full_len = query_row.shape[0]
    block_len = min(512, full_len)
    block_count = full_len // block_len
    factor = query_row.shape[-1] ** (-0.5)

    def backward_one_block(running, packed_block):
        grad_key, grad_value = running
        query_block, picture_block, grad_block, logsum_block = packed_block
        scores = block_scores(query_block, key_row, picture_block, picture_row, mask_row)
        probability = jnp.exp(scores - logsum_block)
        prob_low = probability.astype(jnp.bfloat16)
        grad_prob = jnp.einsum(
            "qhd,khd->hqk", grad_block, value_row, preferred_element_type=jnp.float32
        )
        grad_value = grad_value + jnp.einsum(
            "hqk,qhd->khd", prob_low, grad_block, preferred_element_type=jnp.float32
        )
        centre = jnp.sum(probability * grad_prob, axis=-1, keepdims=True)
        grad_scores = (probability * (grad_prob - centre)).astype(jnp.bfloat16)
        grad_query = factor * jnp.einsum(
            "hqk,khd->qhd", grad_scores, key_row, preferred_element_type=jnp.float32
        )
        grad_key = grad_key + factor * jnp.einsum(
            "hqk,qhd->khd", grad_scores, query_block, preferred_element_type=jnp.float32
        )
        return ((grad_key, grad_value), grad_query)

    zero_state = jnp.zeros(key_row.shape, jnp.float32)
    block_shape = (block_count, block_len) + query_row.shape[1:]
    (grad_key, grad_value), grad_query = lax.scan(
        backward_one_block,
        (zero_state, zero_state),
        (
            query_row.reshape(block_shape),
            picture_row.reshape(block_count, block_len),
            grad_row.reshape(block_shape),
            logsum_row,
        ),
    )
    return (grad_query.reshape(key_row.shape), grad_key, grad_value)


def local_plain(
    tokens,
    lengths,
    pictures,
    w_query,
    w_key,
    w_value,
    w_out,
    w_up,
    w_down,
    norm1_gain,
    norm1_shift,
    norm2_gain,
    norm2_shift,
    query_gain,
    key_gain,
    cotangent,
):
    tp_place = lax.axis_index("tp")
    local_len = tokens.shape[1]
    model_width = tokens.shape[2]
    full_len = pictures.shape[1]
    local_width = w_query.shape[1]
    heads_local = local_width // HD
    gain_one, shift_one, gain_two, shift_two, gain_query, gain_key = (
        lax.all_gather(norm1_gain, ("fsdp", "tp"), axis=0, tiled=True),
        lax.all_gather(norm1_shift, ("fsdp", "tp"), axis=0, tiled=True),
        lax.all_gather(norm2_gain, ("fsdp", "tp"), axis=0, tiled=True),
        lax.all_gather(norm2_shift, ("fsdp", "tp"), axis=0, tiled=True),
        lax.all_gather(query_gain, ("fsdp", "tp"), axis=0, tiled=True),
        lax.all_gather(key_gain, ("fsdp", "tp"), axis=0, tiled=True),
    )
    positions = jnp.arange(full_len, dtype=jnp.int32)
    valid_full = (positions[None, :] < jnp.sum(lengths, axis=1)[:, None]).astype(jnp.float32)
    valid_here = lax.dynamic_slice_in_dim(valid_full, tp_place * local_len, local_len, 1)[
        :, :, None
    ]
    qgain_here = lax.dynamic_slice_in_dim(
        gain_query, tp_place * local_width, local_width, 0
    ).reshape(heads_local, HD)
    kgain_here = lax.dynamic_slice_in_dim(gain_key, tp_place * local_width, local_width, 0).reshape(
        heads_local, HD
    )
    front_query, front_key, front_value, front_out = (
        lax.all_gather(w_query, "fsdp", axis=0, tiled=True),
        lax.all_gather(w_key, "fsdp", axis=0, tiled=True),
        lax.all_gather(w_value, "fsdp", axis=0, tiled=True),
        lax.all_gather(w_out, "fsdp", axis=1, tiled=True),
    )
    inputs = tokens.astype(jnp.float32)
    hidden, normed_one, inverse_one = normalise(inputs, gain_one, shift_one)
    hidden_full = gather_tokens(hidden.astype(jnp.bfloat16))
    row_shape = hidden_full.shape[:2] + (heads_local, HD)
    query = jnp.dot(hidden_full, front_query, preferred_element_type=jnp.float32).reshape(row_shape)
    keyed = jnp.dot(hidden_full, front_key, preferred_element_type=jnp.float32).reshape(row_shape)
    value_low = (
        jnp.dot(hidden_full, front_value, preferred_element_type=jnp.float32)
        .astype(jnp.bfloat16)
        .reshape(row_shape)
    )
    query_norm, query_unit, query_inverse = normalise(query, qgain_here, 0.0)
    key_norm, key_unit, key_inverse = normalise(keyed, kgain_here, 0.0)
    query_low = query_norm.astype(jnp.bfloat16)
    key_low = key_norm.astype(jnp.bfloat16)
    mixture, logsum = lax.map(forward_row, (query_low, key_low, value_low, pictures, valid_full))
    mixture_low = mixture.reshape(hidden_full.shape[:2] + (local_width,)).astype(jnp.bfloat16)
    attn_branch = valid_here * reduce_tokens(
        jnp.dot(mixture_low, front_out, preferred_element_type=jnp.float32)
    )
    middle = inputs + attn_branch
    hidden_two, normed_two, inverse_two = normalise(middle, gain_two, shift_two)
    hidden_two_full = gather_tokens(hidden_two.astype(jnp.bfloat16))
    front_up, front_down = (
        lax.all_gather(w_up, "fsdp", axis=0, tiled=True),
        lax.all_gather(w_down, "fsdp", axis=1, tiled=True),
    )
    up_value = jnp.dot(hidden_two_full, front_up, preferred_element_type=jnp.float32)
    activated = jax.nn.gelu(up_value, approximate=False).astype(jnp.bfloat16)
    mlp_branch = valid_here * reduce_tokens(
        jnp.dot(activated, front_down, preferred_element_type=jnp.float32)
    )
    result = (middle + mlp_branch).astype(jnp.bfloat16)
    square_sums = jnp.stack(
        [
            jnp.sum(valid_here * inputs * inputs),
            jnp.sum(attn_branch * attn_branch),
            jnp.sum(valid_here * middle * middle),
            jnp.sum(mlp_branch * mlp_branch),
        ]
    )
    valid_count = jnp.sum(valid_here)
    back_up, back_down = (
        lax.all_gather(w_up, "fsdp", axis=0, tiled=True),
        lax.all_gather(w_down, "fsdp", axis=1, tiled=True),
    )
    back_query, back_key, back_value, back_out = (
        lax.all_gather(w_query, "fsdp", axis=0, tiled=True),
        lax.all_gather(w_key, "fsdp", axis=0, tiled=True),
        lax.all_gather(w_value, "fsdp", axis=0, tiled=True),
        lax.all_gather(w_out, "fsdp", axis=1, tiled=True),
    )
    grad_y = cotangent.astype(jnp.float32) * valid_here
    grad_y_full = gather_grads(grad_y.astype(jnp.bfloat16))
    grad_down = jnp.einsum(
        "rlf,rld->fd", activated, grad_y_full, preferred_element_type=jnp.float32
    )
    grad_act = jnp.dot(grad_y_full, back_down.T, preferred_element_type=jnp.float32)
    grad_pre = (grad_act * gelu_slope(up_value)).astype(jnp.bfloat16)
    grad_up = jnp.einsum(
        "rld,rlf->df", hidden_two_full, grad_pre, preferred_element_type=jnp.float32
    )
    grad_hidden_two = reduce_grads(jnp.dot(grad_pre, back_up.T, preferred_element_type=jnp.float32))
    mlp_grads = (
        lax.psum_scatter(grad_up, "fsdp", scatter_dimension=0, tiled=True),
        lax.psum_scatter(grad_down, "fsdp", scatter_dimension=1, tiled=True),
    )
    grad_mid_norm, grad_gain_two, grad_shift_two = normalise_back(
        grad_hidden_two, normed_two, inverse_two, gain_two
    )
    grad_middle = grad_y + grad_mid_norm
    grad_branch_here = (valid_here * grad_middle).astype(jnp.bfloat16)
    grad_branch_full = gather_grads(grad_branch_here)
    grad_out_proj = jnp.einsum(
        "rlh,rld->hd", mixture_low, grad_branch_full, preferred_element_type=jnp.float32
    )
    grad_mixture = jnp.dot(grad_branch_full, back_out.T, preferred_element_type=jnp.float32).astype(
        jnp.bfloat16
    )
    grad_qnorm, grad_knorm, grad_value_full = lax.map(
        backward_row,
        (
            query_low,
            key_low,
            value_low,
            pictures,
            valid_full,
            grad_mixture.reshape(row_shape),
            logsum,
        ),
    )
    grad_query_pre, grad_qgain, unused_one = normalise_back(
        grad_qnorm, query_unit, query_inverse, qgain_here
    )
    grad_key_pre, grad_kgain, unused_two = normalise_back(
        grad_knorm, key_unit, key_inverse, kgain_here
    )
    flat_shape = hidden_full.shape[:2] + (local_width,)
    grad_query_low = grad_query_pre.reshape(flat_shape).astype(jnp.bfloat16)
    grad_key_low = grad_key_pre.reshape(flat_shape).astype(jnp.bfloat16)
    grad_value_low = grad_value_full.reshape(flat_shape).astype(jnp.bfloat16)
    grad_wquery = jnp.einsum(
        "rld,rlh->dh", hidden_full, grad_query_low, preferred_element_type=jnp.float32
    )
    grad_wkey = jnp.einsum(
        "rld,rlh->dh", hidden_full, grad_key_low, preferred_element_type=jnp.float32
    )
    grad_wvalue = jnp.einsum(
        "rld,rlh->dh", hidden_full, grad_value_low, preferred_element_type=jnp.float32
    )
    grad_hidden_part = (
        jnp.dot(grad_query_low, back_query.T, preferred_element_type=jnp.float32)
        + jnp.dot(grad_key_low, back_key.T, preferred_element_type=jnp.float32)
        + jnp.dot(grad_value_low, back_value.T, preferred_element_type=jnp.float32)
    )
    grad_hidden = reduce_grads(grad_hidden_part)
    attn_grads = (
        lax.psum_scatter(grad_wquery, "fsdp", scatter_dimension=0, tiled=True),
        lax.psum_scatter(grad_wkey, "fsdp", scatter_dimension=0, tiled=True),
        lax.psum_scatter(grad_wvalue, "fsdp", scatter_dimension=0, tiled=True),
        lax.psum_scatter(grad_out_proj, "fsdp", scatter_dimension=1, tiled=True),
    )
    grad_in_norm, grad_gain_one, grad_shift_one = normalise_back(
        grad_hidden, normed_one, inverse_one, gain_one
    )
    grad_inputs = grad_middle + grad_in_norm
    zero_width = jnp.zeros((model_width,), jnp.float32)
    grad_qgain_full = lax.dynamic_update_slice_in_dim(
        zero_width, grad_qgain.reshape(local_width), tp_place * local_width, 0
    )
    grad_kgain_full = lax.dynamic_update_slice_in_dim(
        zero_width, grad_kgain.reshape(local_width), tp_place * local_width, 0
    )
    small_shards = (
        lax.psum_scatter(grad_gain_one, ("fsdp", "tp"), scatter_dimension=0, tiled=True),
        lax.psum_scatter(grad_shift_one, ("fsdp", "tp"), scatter_dimension=0, tiled=True),
        lax.psum_scatter(grad_gain_two, ("fsdp", "tp"), scatter_dimension=0, tiled=True),
        lax.psum_scatter(grad_shift_two, ("fsdp", "tp"), scatter_dimension=0, tiled=True),
        lax.psum_scatter(grad_qgain_full, ("fsdp", "tp"), scatter_dimension=0, tiled=True),
        lax.psum_scatter(grad_kgain_full, ("fsdp", "tp"), scatter_dimension=0, tiled=True),
    )
    totals, counted = lax.psum((square_sums, valid_count), ("fsdp", "tp"))
    statistics = jnp.sqrt(totals / (counted * model_width))
    return (
        result,
        grad_inputs,
        attn_grads[0],
        attn_grads[1],
        attn_grads[2],
        attn_grads[3],
        mlp_grads[0],
        mlp_grads[1],
        small_shards[0],
        small_shards[1],
        small_shards[2],
        small_shards[3],
        small_shards[4],
        small_shards[5],
        statistics,
    )


BIG = 1024
SMALL = 448
LP = BIG + 3 * SMALL
MARGIN = 128
EXP_SCALE = 0.125 * 1.4426950408889634
MESH = pl.DeviceIdType.MESH
BF = jnp.bfloat16
F32 = jnp.float32


def dot_nn(a, b):
    return lax.dot_general(a, b, (((1,), (0,)), ((), ())), preferred_element_type=F32)


def dot_nt(a, b):
    return lax.dot_general(a, b, (((1,), (1,)), ((), ())), preferred_element_type=F32)


def dot_tn(a, b):
    return lax.dot_general(a, b, (((0,), (0,)), ((), ())), preferred_element_type=F32)


def iota(shape, dim):
    return lax.broadcasted_iota(jnp.int32, shape, dim)


def head_mask(rows, width, h):
    lane = iota((rows, width), 1)
    return (lane >= h * HD) & (lane < (h + 1) * HD)


def segment_matrix(width):
    r = iota((width, width), 0) // HD
    c = iota((width, width), 1) // HD
    return jnp.where(r == c, 1.0 / HD, 0.0).astype(BF)


def segment_mean(x, seg):
    hi = x.astype(BF)
    lo = (x - hi.astype(F32)).astype(BF)
    return dot_nn(hi, seg) + dot_nn(lo, seg)


class Place:
    def __init__(self, nf, nt):
        self.nf, self.nt = nf, nt
        self.nx = 2
        self.nz = nf // 2
        f = lax.axis_index("fsdp")
        t = lax.axis_index("tp")
        self.f, self.t = f, t
        self.z, self.x = f // 2, lax.rem(f, 2)
        self.y, self.c = t // 2, lax.rem(t, 2)
        self.me = f * nt + t

    def rel(self, dz=0, dx=0, dy=0, dc=0):
        z = lax.rem(self.z + dz, self.nz) if dz else self.z
        x = 1 - self.x if dx else self.x
        y = 1 - self.y if dy else self.y
        c = 1 - self.c if dc else self.c
        return (z * 2 + x, y * 2 + c)


class Copies:
    def __init__(self):
        self.sent = []

    def start(self, src, dst, send_sem, recv_sem, dev):
        cp = pltpu.make_async_remote_copy(
            src_ref=src,
            dst_ref=dst,
            send_sem=send_sem,
            recv_sem=recv_sem,
            device_id=dev,
            device_id_type=MESH,
        )
        cp.start()
        self.sent.append(cp)

    def finish(self):
        for cp in self.sent:
            cp.wait_send()
        self.sent = []


def wait_recv(dst, send_sem, recv_sem, dev):
    pltpu.make_async_remote_copy(
        src_ref=dst,
        dst_ref=dst,
        send_sem=send_sem,
        recv_sem=recv_sem,
        device_id=dev,
        device_id_type=MESH,
    ).wait_recv()


def barrier_all(pc):
    n = pc.nf * pc.nt
    bar = pltpu.get_barrier_semaphore()

    def body(r, carry):
        p = lax.rem(pc.me + r, n)
        pl.semaphore_signal(
            bar, inc=1, device_id=(p // pc.nt, lax.rem(p, pc.nt)), device_id_type=MESH
        )
        return carry

    lax.fori_loop(1, n, body, 0)
    pl.semaphore_wait(bar, n - 1)


GATHER_ORDERS = {"zxy": ("z", "x", "y"), "zyx": ("z", "y", "x")}


def axis_steps(pc, axis):
    if axis == "z":
        return [dict(dz=i) for i in range(1, pc.nz)]
    return [{"d" + axis: 1}]


def gather_plan(pc, order):
    stages = [[(dict(), 0)]]
    have = [dict()]
    for k, axis in enumerate(order):
        fresh = []
        for step in axis_steps(pc, axis):
            for b in have:
                fresh.append(dict(b, **step))
        stages.append([(b, k + 1) for b in fresh])
        have = have + fresh
    return stages


class Gather:
    def __init__(self, pc, copies, src, dst, send, recv, order, kind):
        self.pc, self.copies = pc, copies
        self.src, self.dst, self.send, self.recv = src, dst, send, recv
        self.order = order
        self.kind = kind
        self.stages = gather_plan(pc, order)
        self.count = 0

    def index(self, place):
        f, t = place
        return {"full": (t, f), "half": (t // 2, f), "row": (f,)}[self.kind]

    def slot(self, place):
        return self.dst.at[self.index(place)]

    def rsem(self, place):
        return self.recv.at[self.index(place)]

    def pass_on(self, block, axes):
        pc = self.pc
        place = pc.rel(**block)
        src = self.src if not block else self.slot(place)
        targets = []
        for axis in axes:
            targets += [dict(dc=1)] if axis == "c" else axis_steps(pc, axis)
        for step in targets:
            self.copies.start(
                src,
                self.slot(place),
                self.send.at[self.count],
                self.rsem(place),
                pc.rel(**step),
            )
            self.count += 1

    def wait(self, block):
        place = self.pc.rel(**block)
        wait_recv(self.slot(place), self.send.at[0], self.rsem(place), self.pc.rel(dc=1))

    def axes_after(self, depth):
        return tuple(self.order[depth:]) + (("c",) if self.kind == "full" else ())

    def stage(self, k, axes=None):
        for block, depth in self.stages[k]:
            if block:
                self.wait(block)
            self.pass_on(block, self.axes_after(depth) if axes is None else axes)

    def last(self):
        if self.kind == "full":
            for stage in self.stages:
                for block, depth in stage:
                    self.wait(dict(block, dc=1))


def sends_of(nz, order, kind):
    n = {"z": nz - 1, "x": 1, "y": 1}
    total, have = 0, 1
    for axis in order:
        total += have * n[axis]
        have *= n[axis] + 1
    return total + (have if kind == "full" else 0)


def slots_of(lens_ref):
    lens = [lens_ref[0, p] for p in range(4)]
    starts = [0]
    for p in range(3):
        starts.append(starts[-1] + lens[p])
    big = 0
    for p in range(1, 4):
        big = jnp.where(lens[p] == BIG, p, big)
    sb = 0
    for p in range(1, 4):
        sb = jnp.where(big == p, starts[p], sb)
    out = [(sb, BIG)]
    for k in range(3):
        s = jnp.where(big <= k, starts[k + 1], starts[k])
        n = jnp.where(big <= k, lens[k + 1], lens[k])
        out.append((s, n))
    return out


BASES = (0, BIG, BIG + SMALL, BIG + 2 * SMALL)


def shift_matrix(rows, cols, r):
    return jnp.where(iota((rows, cols), 1) == iota((rows, cols), 0) + r, 1.0, 0.0).astype(BF)


def load_rows(src, first, count):
    return jnp.concatenate([src[first + m] for m in range(count)], axis=0)


def pack_rows(src, dst, lens, masked=False):
    def big(j, carry):
        s = slots_of(lens)[0][0]
        r = lax.rem(s, 16)
        d = shift_matrix(128, 144, r)
        out = dot_nn(d, load_rows(src, s // 16 + j * 8, 9)).astype(BF)
        dst[pl.ds(pl.multiple_of(j * 128, 128), 128), :] = out
        return carry

    lax.fori_loop(0, BIG // 128, big, 0)

    for k in range(3):

        def small(j, carry, k=k):
            s, n = slots_of(lens)[1 + k]
            r = lax.rem(s, 16)
            d = shift_matrix(112, 128, r)
            out = dot_nn(d, load_rows(src, s // 16 + j * 7, 8))
            if masked:
                out = jnp.where(iota(out.shape, 0) + j * 112 < n, out, 0.0)
            out = out.astype(BF)
            dst[pl.ds(pl.multiple_of(BASES[1 + k] + j * 112, 16), 112), :] = out
            return carry

        lax.fori_loop(0, 4, small, 0)


def unpack_tile(src, i0, lens):
    wa, ea, wb, sb = 0, 0, 0, 4096
    for (s, n), base in zip(slots_of(lens), BASES):
        inside = (s <= i0) & (i0 < s + n)
        begins = (s > i0) & (s <= i0 + 127)
        w = base + i0 - s + MARGIN
        wa = jnp.where(inside, w, wa)
        ea = jnp.where(inside, s + n - i0, ea)
        wb = jnp.where(begins, w, wb)
        sb = jnp.where(begins, s - i0, sb)
    out = None
    row = iota((128, 144), 0)
    col = iota((128, 144), 1)
    for w, ok in ((wa, lambda: row < ea), (wb, lambda: row >= sb)):
        r = lax.rem(w, 16)
        d = jnp.where((col == row + r) & ok(), 1.0, 0.0).astype(BF)
        part = dot_nn(d, load_rows(src, w // 16, 9))
        out = part if out is None else out + part
    return out


def layer_norm_rows(x, g, b):
    mean = jnp.mean(x, axis=-1, keepdims=True)
    xc = x - mean
    var = jnp.mean(xc * xc, axis=-1, keepdims=True)
    inv = lax.rsqrt(var + EPS)
    n = xc * inv
    return n * g + b, n, inv


def own_heads(row, t, nt, width):
    out = row[:, :width]
    for k in range(1, nt):
        out = jnp.where(t == k, row[:, k * width : (k + 1) * width], out)
    return out


def build_gains(prm_all, gains, n, per):
    chunks = n * per // 128
    lane = iota((8, 128), 1)
    acc = [jnp.zeros((8, 128), F32) for _ in range(chunks)]
    for d in range(n):
        j, a = divmod(d * per, 128)
        tile = prm_all[d]
        if a:
            tile = pltpu.roll(tile, a, 1)
        acc[j] = jnp.where((lane >= a) & (lane < a + per), tile, acc[j])
        if a + per > 128:
            acc[j + 1] = jnp.where(lane < a + per - 128, tile, acc[j + 1])
    for j in range(chunks):
        gains[:, j * 128 : (j + 1) * 128] = acc[j]


def ka_kernel(
    nf, nt, orders,
    lens, tok, wa, wo, wu, wd, prm,
    qkv, lse, ob, wqkv, gains, o_own, h1_out, wo_all, wu_all, wd_all,
    tok_all, h1t, h1p, wa_all, prm_all, of, op, osend,
    prm_s, prm_r, tok_s, tok_r, wa_s, wa_r, wo_s, wo_r, wu_s, wu_r, wd_s, wd_r, o_s, o_r, loc,
):
    pc = Place(nf, nt)
    n = nf * nt
    cps = Copies()
    rows, width = tok.shape
    hw = ob.shape[1]
    barrier_all(pc)

    cps.start(tok, tok_all.at[pc.t], tok_s.at[0], tok_r.at[pc.t], pc.rel(dy=1))
    cps.start(tok, tok_all.at[pc.t], tok_s.at[1], tok_r.at[pc.t], pc.rel(dc=1))
    ga = Gather(pc, cps, wa, wa_all, wa_s, wa_r, ("z", "x"), "row")
    go = Gather(pc, cps, wo, wo_all, wo_s, wo_r, orders[0], "full")
    gu = Gather(pc, cps, wu, wu_all, wu_s, wu_r, orders[1], "half")
    gd = Gather(pc, cps, wd, wd_all, wd_s, wd_r, orders[2], "half")
    gw = [go, gu, gd]
    ga.stage(0)

    def push_prm(r, carry):
        p = lax.rem(pc.me + r, n)
        pltpu.make_async_remote_copy(
            src_ref=prm, dst_ref=prm_all.at[pc.me], send_sem=prm_s.at[r], recv_sem=prm_r.at[pc.me],
            device_id=(p // nt, lax.rem(p, nt)), device_id_type=MESH,
        ).start()
        return carry

    lax.fori_loop(1, n, push_prm, 0)
    for g in gw:
        g.stage(0, ("z",))
    local = []
    for src, dst in ((tok, tok_all.at[pc.t]), (wa, wa_all.at[pc.f]), (wo, wo_all.at[pc.t, pc.f]),
                     (wu, wu_all.at[pc.y, pc.f]), (wd, wd_all.at[pc.y, pc.f])):
        cp = pltpu.make_async_copy(src, dst, loc.at[len(local)])
        cp.start()
        local.append(cp)
    prm_all[pc.me] = prm[...]
    h1t[4 * rows // 16 :] = jnp.zeros((h1t.shape[0] - 4 * rows // 16, 16, width), BF)

    def wait_prm(r, carry):
        p = lax.rem(pc.me + r, n)
        wait_recv(prm_all.at[p], prm_s.at[0], prm_r.at[p], (p // nt, lax.rem(p, nt)))
        return carry

    lax.fori_loop(1, n, wait_prm, 0)
    build_gains(prm_all, gains, n, width // n)
    gain_one, shift_one = gains[0:1, :], gains[1:2, :]

    def norm_block(t):
        def body(j, carry):
            at = pl.ds(pl.multiple_of(j * 128, 128), 128)
            out, _, _ = layer_norm_rows(tok_all[t, at, :].astype(F32), gain_one, shift_one)
            h1t[pl.ds(t * (rows // 16) + j * 8, 8)] = out.astype(BF).reshape(8, 16, width)
            return carry

        lax.fori_loop(0, rows // 128, body, 0)

    def wait_tok(t):
        wait_recv(tok_all.at[t], tok_s.at[0], tok_r.at[t], pc.rel(dc=1))

    for cp in local:
        cp.wait()
    norm_block(pc.t)
    t_core, t_y, t_diag = pc.rel(dc=1)[1], pc.rel(dy=1)[1], pc.rel(dy=1, dc=1)[1]
    wait_tok(t_core)
    norm_block(t_core)
    ga.stage(1)
    gu.pass_on({}, ("x",))
    gd.pass_on({}, ("x",))
    go.pass_on({}, ("x", "c"))
    wait_tok(t_y)
    cps.start(tok_all.at[t_y], tok_all.at[t_y], tok_s.at[2], tok_r.at[t_y], pc.rel(dc=1))
    for g in gw:
        g.pass_on({}, ("y",))
    for g in gw:
        g.stage(1)
    norm_block(t_y)
    ga.stage(2)
    wait_tok(t_diag)
    norm_block(t_diag)
    h1_copy = pltpu.make_async_copy(h1t.at[: 4 * rows // 16], h1_out, loc.at[5])
    h1_copy.start()

    pack_rows(h1t, h1p, lens)
    seg = segment_matrix(hw)
    gq = own_heads(gains[4:5, :], pc.t, nt, hw)
    gk = own_heads(gains[5:6, :], pc.t, nt, hw)
    w_full = wa_all[...].reshape(width, 3 * hw)
    for i in range(3):
        wqkv[i] = w_full[:, i * hw : (i + 1) * hw]

    qt = LP // 4

    def project(j, carry):
        at = pl.ds(pl.multiple_of(j * qt, 16), qt)
        h = h1p[at, :]
        lane = iota((qt, 128), 1)
        kept = jnp.zeros((qt, 128), F32)
        for i, g in enumerate((gq, gk)):
            q = dot_nn(h, wqkv[i])
            qc = q - segment_mean(q, seg)
            inv = lax.rsqrt(segment_mean(qc * qc, seg) + EPS)
            qkv[at, i * 256 : i * 256 + hw] = (qc * inv * g).astype(BF)
            for k in range(hw // HD):
                kept = jnp.where(lane == 8 * (i + 1) + k, inv[:, k * HD : k * HD + 1], kept)
        lse[at, :] = kept
        qkv[at, 512 : 512 + hw] = dot_nn(h, wqkv[2]).astype(BF)
        return carry

    lax.fori_loop(0, 4, project, 0)
    qkv[:, 512 + hw :] = jnp.ones((LP, 256 - hw), BF)
    head, tail = MARGIN // 16, (MARGIN + LP) // 16
    op[:head] = jnp.zeros((head, 16, hw), BF)
    op[tail:] = jnp.zeros((op.shape[0] - tail, 16, hw), BF)

    for g in gw:
        g.stage(2)

    def attend(at, keys, h, limit):
        nrow = at.size
        q = jnp.where(head_mask(nrow, hw, h), qkv[at, :hw], jnp.zeros((), BF))
        s = dot_nt(q, qkv[keys, 256 : 256 + hw])
        p = jnp.exp2(s * EXP_SCALE)
        if limit is not None:
            p = jnp.where(iota(p.shape, 1) < limit, p, 0.0)
        oa = dot_nn(p.astype(BF), qkv[keys, 512:768])
        total = oa[:, hw : hw + 1]
        o = oa[:, :hw] * (1.0 / total)
        l2 = jnp.log2(total)
        lane = iota((nrow, 128), 1)
        if h == 0:
            of[at, :] = o
        else:
            of[at, :] = jnp.where(head_mask(nrow, hw, h), o, of[at, :])
        lse[at, :] = jnp.where(lane == h, l2, lse[at, :])

    nh = hw // HD
    for h in range(nh):
        def big(j, carry, h=h):
            attend(pl.ds(pl.multiple_of(j * 512, 512), 512), pl.ds(0, BIG), h, None)
            return carry

        lax.fori_loop(0, BIG // 512, big, 0)

        for k in range(3):
            at = pl.ds(BASES[1 + k], SMALL)
            attend(at, at, h, slots_of(lens)[1 + k][1])
        if h == 0:
            for g in gw:
                g.stage(3)

    ob[...] = of[...].astype(BF)
    op[head:tail] = ob[...].reshape(LP // 16, 16, hw)

    def unpack(i, carry):
        out = unpack_tile(op, i * 128, lens)
        osend[i // 4, pl.ds(pl.multiple_of(lax.rem(i, 4) * 128, 128), 128), :] = out.astype(BF)
        return carry

    lax.fori_loop(0, 16, unpack, 0)
    peers = [pc.rel(dy=1), pc.rel(dy=1, dc=1), pc.rel(dc=1)]
    for i, dev in enumerate(peers):
        cps.start(osend.at[dev[1]], o_own.at[pc.t], o_s.at[i], o_r.at[pc.t], dev)
    cp = pltpu.make_async_copy(osend.at[pc.t], o_own.at[pc.t], loc.at[0])
    cp.start()
    cp.wait()
    h1_copy.wait()
    go.last()
    for dev in peers:
        wait_recv(o_own.at[dev[1]], o_s.at[0], o_r.at[dev[1]], dev)

    def wait_prm_sent(r, carry):
        p = lax.rem(pc.me + r, n)
        pltpu.make_async_remote_copy(
            src_ref=prm, dst_ref=prm_all.at[pc.me], send_sem=prm_s.at[r], recv_sem=prm_r.at[pc.me],
            device_id=(p // nt, lax.rem(p, nt)), device_id_type=MESH,
        ).wait_send()
        return carry

    lax.fori_loop(1, n, wait_prm_sent, 0)
    cps.finish()


def call_ka(nf, nt, lens, tok, wa, wo, wu, wd, prm):
    nz = nf // 2
    rows, width = tok.shape
    r = wa.shape[0]
    hw = wa.shape[1] // 3
    cu, cd = wu.shape[1], wd.shape[1]
    orders = (("z", "x", "y"), ("z", "y", "x"), ("z", "x", "y"))
    S = jax.ShapeDtypeStruct
    V = pltpu.VMEM
    vm = pl.BlockSpec(memory_space=pltpu.VMEM)
    hb = pl.BlockSpec(memory_space=pl.ANY)
    outs = [
        (S((LP, 768), BF), vm), (S((LP, 128), F32), vm), (S((LP, hw), BF), vm), (S((3, width, hw), BF), vm),
        (S((8, width), F32), vm), (S((nt, rows, hw), BF), vm),
        (S((nt * rows // 16, 16, width), BF), hb),
        (S((nt, nf, r, hw), BF), hb), (S((2, nf, r, cu), BF), hb), (S((2, nf, r, cd), BF), hb),
    ]
    dma = pltpu.SemaphoreType.DMA
    scratch = [
        V((nt, rows, width), BF), V(((nt * rows + 192) // 16, 16, width), BF), V((LP, width), BF),
        V((nf, r, 3 * hw), BF), V((nf * nt, 8, 128), F32),
        V((LP, hw), F32), V(((MARGIN + LP + 160) // 16, 16, hw), BF), V((nt, rows, hw), BF),
        dma((nf * nt,)), dma((nf * nt,)), dma((3,)), dma((nt,)),
        dma((sends_of(nz, ("z", "x"), "row"),)), dma((nf,)),
        dma((sends_of(nz, orders[0], "full"),)), dma((nt, nf)),
        dma((sends_of(nz, orders[1], "half"),)), dma((2, nf)),
        dma((sends_of(nz, orders[2], "half"),)), dma((2, nf)),
        dma((3,)), dma((nt,)), dma((8,)),
    ]
    return pl.pallas_call(
        functools.partial(ka_kernel, nf, nt, orders),
        out_shape=[o[0] for o in outs],
        in_specs=[pl.BlockSpec(memory_space=pltpu.SMEM), vm, vm, hb, hb, hb, vm],
        out_specs=[o[1] for o in outs],
        scratch_shapes=scratch,
        compiler_params=pltpu.CompilerParams(
            collective_id=0, has_side_effects=True, vmem_limit_bytes=56 << 20
        ),
    )(lens, tok, wa, wo, wu, wd, prm)


class Scatter:
    def __init__(self, pc, copies, block, ra, rb, rz, send, recv, order, core=None):
        self.pc, self.copies, self.block = pc, copies, block
        self.ra, self.rb, self.rz = ra, rb, rz
        self.send, self.recv, self.order, self.core = send, recv, order, core
        self.count = 0
        self.waits = []
        self.steps = self.run()

    def next(self):
        next(self.steps, None)

    def put(self, src, dst, step):
        k = self.count
        self.copies.start(src, dst, self.send.at[k], self.recv.at[k], self.pc.rel(**step))
        self.waits.append((dst, k, self.pc.rel(**step)))
        self.count += 1

    def arrive(self):
        for dst, k, dev in self.waits:
            wait_recv(dst, self.send.at[k], self.recv.at[k], dev)
        self.waits = []

    def add(self, dst, src):
        dst[...] = (dst[...].astype(F32) + src[...].astype(F32)).astype(BF)

    def over(self, count, pair):
        def body(i, carry):
            dst, src = pair(i)
            self.add(dst, src)
            return carry

        lax.fori_loop(0, count, body, 0)

    def run(self):
        pc, nz, nf = self.pc, self.pc.nz, self.pc.nf
        if self.core is not None:
            part, rc = self.core
            for y in range(2):
                self.put(part.at[y * 2 + 1 - pc.c], rc.at[y], dict(dc=1))
            yield
            self.arrive()
            self.over(
                2 * nf,
                lambda i: (part.at[(i // nf) * 2 + pc.c, lax.rem(i, nf)], rc.at[i // nf, lax.rem(i, nf)]),
            )
        if self.order == ("y", "x"):
            for z in range(nz):
                for x in range(2):
                    self.put(self.block(1 - pc.y, z, x), self.ra.at[z * 2 + x], dict(dy=1))
            yield
            self.arrive()
            self.over(2 * nz, lambda i: (self.block(pc.y, i // 2, lax.rem(i, 2)), self.ra.at[i]))
            for z in range(nz):
                self.put(self.block(pc.y, z, 1 - pc.x), self.rb.at[z], dict(dx=1))
        elif self.order == ("x", "y"):
            for z in range(nz):
                for y in range(2):
                    self.put(self.block(y, z, 1 - pc.x), self.ra.at[z * 2 + y], dict(dx=1))
            yield
            self.arrive()
            self.over(2 * nz, lambda i: (self.block(lax.rem(i, 2), i // 2, pc.x), self.ra.at[i]))
            for z in range(nz):
                self.put(self.block(1 - pc.y, z, pc.x), self.rb.at[z], dict(dy=1))
        else:
            for z in range(nz):
                self.put(self.block(pc.y, z, 1 - pc.x), self.rb.at[z], dict(dx=1))
        yield
        self.arrive()
        self.over(nz, lambda z: (self.block(pc.y, z, pc.x), self.rb.at[z]))
        for dz in range(1, nz):
            z = lax.rem(pc.z + dz, nz)
            self.put(self.block(pc.y, z, pc.x), self.rz.at[dz], dict(dz=dz))
        yield

    def finish(self, out):
        self.arrive()
        pc = self.pc
        total = self.block(pc.y, pc.z, pc.x)[...].astype(F32)
        for dz in range(1, pc.nz):
            total = total + self.rz[dz].astype(F32)
        out[...] = total


def erf_parts(u):
    half = 0.5 * (1.0 + lax.erf(u * ROOT_HALF))
    return u * half, half + u * jnp.exp2(u * u * (-0.5 * 1.4426950408889634)) * DENSITY


def kc_kernel(
    nf, nt,
    lens, tok, cot, o_own, wo, wqkv, gains, lse, ob, qkv, h1, wu, wd,
    out_ref, dx_out, gq_out, gwo_out, gwu_out, gwd_out, small_out,
    sm, g1b, g2b, wb, inv2, h2a, dya, fs, hs, hr, dz, dos,
    dot_all, dop, delta, dhr, dhy, gq_own, gq_b, gq_z, sm_t, sm_f, sm_sum,
    o_part, o_rc, o_ra, o_rb, o_rz, u_own, u_ra, u_rb, u_rz, d_own, d_ra, d_rb, d_rz,
    h2_s, h2_r, dy_s, dy_r, f_s, f_r, hh_s, hh_r,
    do_s, do_r, o_s, o_r, u_s, u_r, d_s, d_r, dh_s, dh_r, gq_s, gq_r, st_s, st_r, sf_s, sf_r, loc,
):
    pc = Place(nf, nt)
    cps = Copies()
    rows, width = tok.shape
    hw = ob.shape[1]
    nh = hw // HD
    groups = rows // 16
    r = width // nf
    c_me, c_other = pc.c, 1 - pc.c
    core = pc.rel(dc=1)

    local = []
    for y in range(2):
        local.append((wu.at[y], wb.at[pl.ds(y * width, width)]))
        local.append((wd.at[y], wb.at[pl.ds((2 + y) * width, width)]))
    weights = []
    for i, (src, dst) in enumerate(local):
        cp = pltpu.make_async_copy(src, dst, loc.at[i])
        cp.start()
        weights.append(cp)
    cot_copy = pltpu.make_async_copy(cot, dya.at[pc.c], loc.at[7])
    cot_copy.start()
    barrier_all(pc)

    def slot_valid(t, first, count):
        row = iota((count, 1), 0) + (t * rows + first)
        total = lens[0, 0] + lens[0, 1] + lens[0, 2] + lens[0, 3]
        return jnp.where(row < total, 1.0, 0.0)

    half = rows // 2

    def own_dy(j, carry):
        at = pl.ds(pl.multiple_of(j * half, half), half)
        v = slot_valid(pc.t, j * half, half)
        dya[c_me, at, :] = (dya[c_me, at, :].astype(F32) * v).astype(BF)
        return carry

    cot_copy.wait()
    lax.fori_loop(0, 2, own_dy, 0)
    cps.start(dya.at[c_me], dya.at[c_me], dy_s.at[0], dy_r.at[0], core)
    gain, shift = gains[2:3, :], gains[3:4, :]
    none = jnp.zeros((1, width), F32)

    def colsum(x):
        return jnp.sum(x, axis=0, keepdims=True)

    def attn_out(j, carry):
        at = pl.ds(pl.multiple_of(j * half, half), half)
        v = slot_valid(pc.t, j * half, half)
        a = dot_nt(o_own[0, at, :], wo[0])
        for t in range(1, nt):
            a += dot_nt(o_own[t, at, :], wo[t])
        a = a * v
        x = tok[at, :].astype(F32)
        m = x + a
        h, n, inv = layer_norm_rows(m, gain, shift)
        sm[pl.ds(pl.multiple_of(j * half, half), half), :] = m
        sm[pl.ds(pl.multiple_of(rows + j * half, half), half), :] = n
        inv2[at, :] = jnp.broadcast_to(inv, (half, 128))
        h2a[c_me, at, :] = h.astype(BF)
        pltpu.make_async_remote_copy(
            src_ref=h2a.at[c_me, at], dst_ref=h2a.at[c_me, at], send_sem=h2_s.at[j], recv_sem=h2_r.at[j],
            device_id=core, device_id_type=MESH,
        ).start()
        return (carry[0] + colsum(x * x * v), carry[1] + colsum(a * a), carry[2] + colsum(m * m * v))

    sum_x, sum_a, sum_m = lax.fori_loop(0, 2, attn_out, (none, none, none))
    for cp in weights:
        cp.wait()

    def h2_copy(j, slot):
        at = pl.ds(pl.multiple_of(j * half, half), half)
        return pltpu.make_async_remote_copy(
            src_ref=h2a.at[slot, at], dst_ref=h2a.at[slot, at], send_sem=h2_s.at[j], recv_sem=h2_r.at[j],
            device_id=core, device_id_type=MESH,
        )

    def back_copy(j, src, dst, send, recv):
        at = pl.ds(pl.multiple_of(j * half, half), half)
        return pltpu.make_async_remote_copy(
            src_ref=src.at[at], dst_ref=dst.at[at], send_sem=send.at[j], recv_sem=recv.at[j],
            device_id=core, device_id_type=MESH,
        )

    def feed(i, carry):
        far = i // 2
        j = lax.rem(i, 2)
        slot = c_me + far * (1 - 2 * c_me)
        at = pl.ds(pl.multiple_of(j * half, half), half)

        @pl.when(far == 1)
        def _():
            h2_copy(j, c_other).wait_recv()

        @pl.when(i == 2)
        def _():
            wait_recv(dya.at[c_other], dy_s.at[0], dy_r.at[0], core)

        h = h2a[slot, at, :]
        g = dya[slot, at, :]
        f, dh = None, None
        for y in range(2):
            up = wb[y * width : (y + 1) * width, :]
            down = wb[(2 + y) * width : (3 + y) * width, :]
            act, slope = erf_parts(dot_nn(h, up))
            act = act.astype(BF)
            g1b[pl.ds(pl.multiple_of((y * 2 + slot) * rows + j * half, half), half), :] = act
            fy = dot_nt(act, down)
            du = (dot_nn(g, down) * slope).astype(BF)
            g2b[pl.ds((y * 2 + slot) * groups + j * (half // 16), half // 16)] = du.reshape(half // 16, 16, width)
            dy = dot_nt(du, up)
            f = fy if f is None else f + fy
            dh = dy if dh is None else dh + dy

        @pl.when(far == 0)
        def _():
            sm[pl.ds(pl.multiple_of(2 * rows + j * half, half), half), :] = f
            sm[pl.ds(pl.multiple_of(3 * rows + j * half, half), half), :] = dh

        @pl.when(far == 1)
        def _():
            fs[at, :] = f.astype(BF)
            hs[at, :] = dh.astype(BF)
            back_copy(j, hs, hr, hh_s, hh_r).start()
            back_copy(j, fs, fr_in, f_s, f_r).start()

        return carry

    fr_in = hr.at[pl.ds(rows, rows)]
    lax.fori_loop(0, 4, feed, 0)

    def rows_of(ref, y):
        return ref[pl.ds(y * 2 * rows, 2 * rows), :]

    dyall = dya[...].reshape(2 * rows, width)
    part_w = width // 2
    nblk = nf // 2

    def weight_grad(left, get_right, own):
        for q in range(2):
            lq = left[:, q * part_w : (q + 1) * part_w]

            def body(y, carry, lq=lq, q=q):
                g = dot_tn(lq, get_right(y)).astype(BF)
                own[y, q * nblk : (q + 1) * nblk] = g.reshape(nblk, r, width)
                return carry

            lax.fori_loop(0, 2, body, 0)

    weight_grad(dyall, lambda y: g1b[pl.ds(pl.multiple_of(y * 2 * rows, rows), 2 * rows), :], d_own)
    sc_d = Scatter(
        pc, cps, lambda y, z, x: d_own.at[y, z * 2 + x], d_ra, d_rb, d_rz, d_s, d_r, ("y", "x")
    )
    sc_d.next()
    qkv_copy = pltpu.make_async_copy(qkv, g1b, loc.at[4])
    qkv_copy.start()

    def ln_back(j, carry):
        at = pl.ds(pl.multiple_of(j * half, half), half)
        back_copy(j, hs, hr, hh_s, hh_r).wait_recv()
        back_copy(j, fs, fr_in, f_s, f_r).wait_recv()
        v = slot_valid(pc.t, j * half, half)
        e = sm[pl.ds(pl.multiple_of(3 * rows + j * half, half), half), :] + hr[at, :].astype(F32)
        f = sm[pl.ds(pl.multiple_of(2 * rows + j * half, half), half), :]
        f = (f + hr[pl.ds(pl.multiple_of(rows + j * half, half), half), :].astype(F32)) * v
        m = sm[pl.ds(pl.multiple_of(j * half, half), half), :]
        n = sm[pl.ds(pl.multiple_of(rows + j * half, half), half), :]
        out_ref[at, :] = (m + f).astype(BF)
        c = e * gain
        dm = dya[c_me, at, :].astype(F32) + inv2[at, 0:1] * (
            c - jnp.mean(c, axis=-1, keepdims=True) - n * jnp.mean(c * n, axis=-1, keepdims=True)
        )
        dx_out[at, :] = dm
        z = (dm * v).astype(BF)
        dz[at, :] = z
        for t in range(nt):
            d = dot_nn(z, wo[t]).astype(BF)
            dos[t, pl.ds(j * (half // 16), half // 16)] = d.reshape(half // 16, 16, hw)
        return (carry[0] + colsum(e * n), carry[1] + colsum(e), carry[2] + colsum(f * f))

    sum_g2, sum_b2, sum_f = lax.fori_loop(0, 2, ln_back, (none, none, none))
    peers = [pc.rel(dy=1), pc.rel(dy=1, dc=1), core]
    own_groups = pl.ds(pc.t * groups, groups)
    for i, dev in enumerate(peers):
        cps.start(dos.at[dev[1]], dot_all.at[own_groups], do_s.at[i], do_r.at[pc.t], dev)
    cp = pltpu.make_async_copy(dos.at[pc.t], dot_all.at[own_groups], loc.at[6])
    cp.start()
    h1_copy = pltpu.make_async_copy(h1, wb.at[pl.ds(0, nt * rows)], loc.at[5])
    h1_copy.start()

    hall = h2a[...].reshape(2 * rows, width)
    weight_grad(
        hall,
        lambda y: g2b[pl.ds(y * 2 * groups, 2 * groups)].reshape(2 * rows, width),
        u_own,
    )
    sc_u = Scatter(
        pc, cps, lambda y, z, x: u_own.at[y, z * 2 + x], u_ra, u_rb, u_rz, u_s, u_r, ("x", "y")
    )
    sc_u.next()
    for t in range(nt):
        o_part[t] = dot_tn(dz[...], o_own[t]).astype(BF).reshape(nf, r, hw)
    sc_o = Scatter(
        pc, cps, lambda y, z, x: o_part.at[y * 2 + pc.c, z * 2 + x], o_ra, o_rb, o_rz, o_s, o_r,
        ("y", "x"), (o_part, o_rc),
    )
    sc_o.next()

    small_out[...] = jnp.zeros(small_out.shape, F32)
    tail = 4 * groups
    dot_all[tail:] = jnp.zeros((dot_all.shape[0] - tail, 16, hw), BF)
    sm[...] = jnp.zeros(sm.shape, F32)
    head, mid = MARGIN // 16, (MARGIN + LP) // 16
    g2b[:head] = jnp.zeros((head, 16, width), BF)
    g2b[mid:] = jnp.zeros((g2b.shape[0] - mid, 16, width), BF)
    cp.wait()
    for dev in peers:
        wait_recv(dot_all.at[pl.ds(dev[1] * groups, groups)], do_s.at[0], do_r.at[dev[1]], dev)
    pack_rows(dot_all, dop, lens, True)

    dlt = LP // 4

    def deltas(j, carry):
        at = pl.ds(pl.multiple_of(j * dlt, 16), dlt)
        prod = dop[at, :].astype(F32) * ob[at, :].astype(F32)
        lane = iota((dlt, 128), 1)
        out = jnp.zeros((dlt, 128), F32)
        for h in range(nh):
            part_h = jnp.where(head_mask(dlt, hw, h), prod, 0.0)
            out = jnp.where(lane == h, jnp.sum(part_h, axis=-1, keepdims=True), out)
        delta[at, :] = out
        return carry

    lax.fori_loop(0, 4, deltas, 0)
    qkv_copy.wait()

    def back(at, keys, h, limit):
        nrow, nkey = at.size, keys.size
        zero = jnp.zeros((), BF)
        hm = head_mask(nrow, hw, h)
        q = jnp.where(hm, g1b[at, :hw], zero)
        s = dot_nt(q, g1b[keys, 256 : 256 + hw])
        p = jnp.exp2(s * EXP_SCALE - lse[at, h : h + 1])
        if limit is not None:
            p = jnp.where(iota(p.shape, 1) < limit, p, 0.0)
        g = jnp.where(hm, dop[at, :], zero)
        dp = dot_nt(g, g1b[keys, 512 : 512 + hw])
        ds = (p * (dp - delta[at, h : h + 1])).astype(BF)
        sm[keys, 512 : 512 + hw] += dot_tn(p.astype(BF), g)
        sm[keys, 256 : 256 + hw] += dot_tn(ds, q)
        km = jnp.where(head_mask(nkey, hw, h), g1b[keys, 256 : 256 + hw], zero)
        sm[at, :hw] += dot_nn(ds, km)

    for h in range(nh):
        def big(j, carry, h=h):
            back(pl.ds(pl.multiple_of(j * 256, 256), 256), pl.ds(0, BIG), h, None)
            return carry

        lax.fori_loop(0, BIG // 256, big, 0)
        for k in range(3):
            at = pl.ds(BASES[1 + k], SMALL)
            back(at, at, h, slots_of(lens)[1 + k][1])
        if h == 0:
            sc_o.next()
            sc_d.next()
        elif h == 1:
            sc_u.next()
            sc_o.next()
        else:
            sc_d.next()

    seg = segment_matrix(hw)
    gq = own_heads(gains[4:5, :], pc.t, nt, hw)
    gk = own_heads(gains[5:6, :], pc.t, nt, hw)

    def norms(j, carry):
        at = pl.ds(pl.multiple_of(j * dlt, 16), dlt)
        kept = lse[at, :]
        sums, outs = [], []
        for i, g in enumerate((gq, gk)):
            inv = jnp.broadcast_to(kept[:, 8 * (i + 1) : 8 * (i + 1) + 1], (dlt, hw))
            for k in range(1, nh):
                inv = jnp.where(head_mask(dlt, hw, k), kept[:, 8 * (i + 1) + k : 8 * (i + 1) + k + 1], inv)
            n = g1b[at, i * 256 : i * 256 + hw].astype(F32) / g
            e = sm[at, i * 256 : i * 256 + hw] * 0.125
            c = e * g
            d = inv * (c - segment_mean(c, seg) - n * segment_mean(c * n, seg))
            outs.append(d.astype(BF))
            sums.append(colsum(e * n))
        outs.append(sm[at, 512 : 512 + hw].astype(BF))
        for i, d in enumerate(outs):
            g2b[pl.ds(head + j * (dlt // 16), dlt // 16), :, i * 256 : i * 256 + hw] = d.reshape(dlt // 16, 16, hw)
        return (carry[0] + sums[0], carry[1] + sums[1])

    nones = jnp.zeros((1, hw), F32)
    sum_q, sum_k = lax.fori_loop(0, 4, norms, (nones, nones))

    def unpack(i, carry):
        out = unpack_tile(g2b, i * 128, lens)
        g1b[pl.ds(pl.multiple_of(i * 128, 128), 128), :] = out.astype(BF)
        return carry

    lax.fori_loop(0, 16, unpack, 0)
    h1_copy.wait()

    def project(t, sums):
        def body(j, carry):
            at = pl.ds(pl.multiple_of(t * rows + j * half, half), half)
            total = dot_nt(g1b[at, :hw], wqkv[0])
            total += dot_nt(g1b[at, 256 : 256 + hw], wqkv[1])
            total += dot_nt(g1b[at, 512 : 512 + hw], wqkv[2])
            low = total.astype(BF)
            g2b[pl.ds(t * groups + j * (half // 16), half // 16)] = low.reshape(half // 16, 16, width)
            return (carry[0] + colsum(total * wb[at, :].astype(F32)), carry[1] + colsum(total))

        return lax.fori_loop(0, 2, body, sums)

    def add_groups(t, src):
        def body(j, carry):
            at = pl.ds(t * groups + j * 4, 4)
            g2b[at] = (g2b[at].astype(F32) + src[pl.ds(j * 4, 4)].astype(F32)).astype(BF)
            return carry

        lax.fori_loop(0, groups // 4, body, 0)

    def block_of(t):
        return g2b.at[pl.ds(t * groups, groups)]

    t_fo, t_ff = (1 - pc.y) * 2 + c_other, (1 - pc.y) * 2 + c_me
    t_no = pc.y * 2 + c_other
    sums = project(t_fo, (none, none))
    cps.start(block_of(t_fo), dhr.at[0], dh_s.at[0], dh_r.at[0], core)
    sums = project(t_ff, sums)
    wait_recv(dhr.at[0], dh_s.at[0], dh_r.at[0], core)
    add_groups(t_ff, dhr.at[0])
    cps.start(block_of(t_ff), dhy, dh_s.at[2], dh_r.at[2], pc.rel(dy=1))
    sums = project(t_no, sums)
    cps.start(block_of(t_no), dhr.at[1], dh_s.at[1], dh_r.at[1], core)
    sum_h, sum_d = project(pc.t, sums)

    gain_one, shift_one = gains[0:1, :], gains[1:2, :]
    small_out[4:5, :hw] = sum_q
    small_out[5:6, :hw] = sum_k
    placed = pltpu.roll(small_out[...], pc.t * hw, 1)
    small_out[...] = placed
    small_out[0:1, :] = (sum_h - shift_one * sum_d) / gain_one
    small_out[1:2, :] = sum_d
    small_out[2:3, :] = sum_g2
    small_out[3:4, :] = sum_b2
    lane = iota((1, width), 1)
    stat = jnp.zeros((1, width), F32)
    counted = jnp.sum(slot_valid(pc.t, 0, rows))
    for i, v in enumerate((sum_x, sum_a, sum_m, sum_f)):
        stat = jnp.where(lane == i, jnp.sum(v), stat)
    small_out[6:7, :] = jnp.where(lane == 4, counted, stat)
    sm_sum[...] = small_out[...]
    for i, dev in enumerate(peers):
        cps.start(sm_sum, sm_t.at[pc.t], st_s.at[i], st_r.at[pc.t], dev)

    for q in range(2):
        hq = wb[: nt * rows, q * part_w : (q + 1) * part_w]
        g = dot_tn(hq, g1b[: nt * rows, :]).astype(BF)
        gq_own[q * nblk : (q + 1) * nblk] = g.reshape(nblk, r, width)
    sc_q = Scatter(
        pc, cps, lambda y, z, x: gq_own.at[z * 2 + x], None, gq_b, gq_z, gq_s, gq_r, ("x",)
    )
    sc_q.next()
    sc_u.next()
    sc_o.next()

    total = small_out[...]
    for dev in peers:
        wait_recv(sm_t.at[dev[1]], st_s.at[0], st_r.at[dev[1]], dev)
        total = total + sm_t[dev[1]]
    sm_f[0] = total
    far = [(lax.rem(pc.f + i, nf), pc.t) for i in range(1, nf)]
    for i, dev in enumerate(far):
        cps.start(sm_f.at[0], sm_f.at[1 + i], sf_s.at[i], sf_r.at[i], dev)
    sc_q.next()

    wait_recv(dhr.at[1], dh_s.at[1], dh_r.at[1], core)
    add_groups(pc.t, dhr.at[1])
    wait_recv(dhy, dh_s.at[2], dh_r.at[2], pc.rel(dy=1))

    def last(j, carry):
        at = pl.ds(pl.multiple_of(j * 128, 128), 128)
        near = g2b[pl.ds(pc.t * groups + j * 8, 8)].astype(F32)
        e = (near + dhy[pl.ds(j * 8, 8)].astype(F32)).reshape(128, width)
        x = tok[at, :].astype(F32)
        _, n, inv = layer_norm_rows(x, gain_one, 0.0)
        c = e * gain_one
        grad = inv * (
            c - jnp.mean(c, axis=-1, keepdims=True) - n * jnp.mean(c * n, axis=-1, keepdims=True)
        )
        dx_out[at, :] = dx_out[at, :] + grad
        return carry

    lax.fori_loop(0, rows // 128, last, 0)
    for i, dev in enumerate(far):
        wait_recv(sm_f.at[1 + i], sf_s.at[i], sf_r.at[i], dev)
        total = total + sm_f[1 + i]
    small_out[...] = total
    sc_q.finish(gq_out)
    sc_d.finish(gwd_out)
    sc_u.finish(gwu_out)
    sc_o.finish(gwo_out)

    def sent(j, carry):
        h2_copy(j, c_me).wait_send()
        back_copy(j, hs, hr, hh_s, hh_r).wait_send()
        back_copy(j, fs, fr_in, f_s, f_r).wait_send()
        return carry

    lax.fori_loop(0, 2, sent, 0)
    cps.finish()


def call_kc(nf, nt, lens, tok, cot, o_own, wo, wqkv, gains, lse, ob, qkv, h1, wu, wd):
    nz = nf // 2
    rows, width = tok.shape
    hw = ob.shape[1]
    r = width // nf
    S = jax.ShapeDtypeStruct
    V = pltpu.VMEM
    vm = pl.BlockSpec(memory_space=pltpu.VMEM)
    hb = pl.BlockSpec(memory_space=pl.ANY)
    dma = pltpu.SemaphoreType.DMA
    g3 = (MARGIN + LP + 160) // 16
    outs = [
        S((rows, width), BF), S((rows, width), F32), S((r, width), F32), S((r, hw), F32),
        S((r, width), F32), S((r, width), F32), S((8, width), F32),
    ]
    scratch = [
        V((LP, width), F32), V((LP, width), BF), V((g3, 16, width), BF), V((4 * width, width), BF),
        V((rows, 128), F32), V((2, rows, width), BF), V((2, rows, width), BF),
        V((rows, width), BF), V((rows, width), BF), V((2 * rows, width), BF),
        V((rows, width), BF), V((nt, rows // 16, 16, hw), BF),
        V(((nt * rows + 192) // 16, 16, hw), BF), V((LP, hw), BF), V((LP, 128), F32),
        V((2, rows // 16, 16, width), BF), V((rows // 16, 16, width), BF),
        V((nf, r, width), BF), V((nz, r, width), BF), V((nz, r, width), BF),
        V((nt, 8, width), F32), V((nf, 8, width), F32), V((8, width), F32),
        V((nt, nf, r, hw), BF), V((2, nf, r, hw), BF), V((nf, r, hw), BF), V((nz, r, hw), BF), V((nz, r, hw), BF),
    ]
    for _ in range(2):
        scratch += [V((2, nf, r, width), BF), V((nf, r, width), BF), V((nz, r, width), BF), V((nz, r, width), BF)]
    ns = 2 + 2 * nz + nz + nz
    scratch += [
        dma((2,)), dma((2,)), dma((1,)), dma((1,)), dma((2,)), dma((2,)), dma((2,)), dma((2,)),
        dma((3,)), dma((nt,)), dma((ns,)), dma((ns,)), dma((ns,)), dma((ns,)), dma((ns,)), dma((ns,)),
        dma((3,)), dma((3,)), dma((2 * nz,)), dma((2 * nz,)), dma((3,)), dma((nt,)), dma((nf,)), dma((nf,)), dma((8,)),
    ]
    return pl.pallas_call(
        functools.partial(kc_kernel, nf, nt),
        out_shape=outs,
        in_specs=[pl.BlockSpec(memory_space=pltpu.SMEM), vm, hb] + [vm] * 6 + [hb] * 4,
        out_specs=[vm] * 7,
        scratch_shapes=scratch,
        compiler_params=pltpu.CompilerParams(
            collective_id=1, has_side_effects=True, vmem_limit_bytes=64 << 20
        ),
    )(lens, tok, cot, o_own, wo, wqkv, gains, lse, ob, qkv, h1, wu, wd)


def local_fused(nf, nt, args):
    (tokens, lengths, pictures, w_query, w_key, w_value, w_out, w_up, w_down) = args[:9]
    smalls, cotangent = args[9:15], args[15]
    rows, width = tokens.shape[1:]
    hw = w_query.shape[1]
    per = smalls[0].shape[0]
    place = lax.axis_index("fsdp") * nt + lax.axis_index("tp")
    prm = jnp.zeros((8, 128), jnp.float32).at[:6, :per].set(jnp.stack(smalls))
    attn = jnp.concatenate([w_query, w_key, w_value], axis=1)
    qkv, lse, ob, wqkv, gains, o_own, h1, wo, wu, wd = call_ka(
        nf, nt, lengths, tokens[0], attn, w_out.T, w_up, w_down.T, prm
    )
    result, grad_in, gqkv, gwo, gwu, gwd, small = call_kc(
        nf, nt, lengths, tokens[0], cotangent[0], o_own, wo.reshape(nt, width, hw), wqkv, gains, lse, ob,
        qkv, h1.reshape(nt * rows, width),
        wu.reshape(2, width, wu.shape[3]), wd.reshape(2, width, wd.shape[3]),
    )
    own = lax.dynamic_slice_in_dim(small, place * per, per, 1)
    statistics = jnp.sqrt(small[6, :4] / (small[6, 4] * width))
    return (
        result[None], grad_in[None],
        gqkv[:, :hw], gqkv[:, 256 : 256 + hw], gqkv[:, 512 : 512 + hw], gwo.T, gwu, gwd.T,
        own[0], own[1], own[2], own[3], own[4], own[5], statistics,
    )


def solution(mesh):
    nf, nt = mesh.shape["fsdp"], mesh.shape["tp"]

    def local(*args):
        tokens, w_query = args[0], args[3]
        if nt == 4 and tokens.shape[0] == 1 and tokens.shape[1] == 512 and w_query.shape[0] % 32 == 0:
            return local_fused(nf, nt, args)
        return local_plain(*args)

    in_specs = (
        P("fsdp", "tp", None),
        P("fsdp", None),
        P("fsdp", None),
        P("fsdp", "tp"),
        P("fsdp", "tp"),
        P("fsdp", "tp"),
        P("tp", "fsdp"),
        P("fsdp", "tp"),
        P("tp", "fsdp"),
        P(("fsdp", "tp")),
        P(("fsdp", "tp")),
        P(("fsdp", "tp")),
        P(("fsdp", "tp")),
        P(("fsdp", "tp")),
        P(("fsdp", "tp")),
        P("fsdp", "tp", None),
    )
    out_specs = (
        P("fsdp", "tp", None),
        P("fsdp", "tp", None),
        P("fsdp", "tp"),
        P("fsdp", "tp"),
        P("fsdp", "tp"),
        P("tp", "fsdp"),
        P("fsdp", "tp"),
        P("tp", "fsdp"),
        P(("fsdp", "tp")),
        P(("fsdp", "tp")),
        P(("fsdp", "tp")),
        P(("fsdp", "tp")),
        P(("fsdp", "tp")),
        P(("fsdp", "tp")),
        P(),
    )
    return jax.shard_map(local, mesh=mesh, in_specs=in_specs, out_specs=out_specs, check_vma=False)
```

```python
import functools

import jax
import jax.numpy as jnp
from jax import lax
from jax.experimental import pallas as pl
from jax.experimental.pallas import tpu as pltpu
from jax.sharding import PartitionSpec as P

HD = 64


EPS = 1e-06
ROOT_HALF = 0.7071067811865476
DENSITY = 0.3989422804014327


def normalise(values, scaling, offset):
    centre = jnp.mean(values, axis=-1, keepdims=True)
    centred = values - centre
    spread = jnp.mean(centred * centred, axis=-1, keepdims=True)
    inverse = lax.rsqrt(spread + EPS)
    normed = centred * inverse
    return (normed * scaling + offset, normed, inverse)


def normalise_back(grad_out, normed, inverse, scaling):
    grad_unit = grad_out * scaling
    grad_values = inverse * (
        grad_unit
        - jnp.mean(grad_unit, axis=-1, keepdims=True)
        - normed * jnp.mean(grad_unit * normed, axis=-1, keepdims=True)
    )
    return (grad_values, jnp.sum(grad_out * normed, axis=(0, 1)), jnp.sum(grad_out, axis=(0, 1)))


def gelu_slope(values):
    return (
        0.5 * (1.0 + jax.scipy.special.erf(values * ROOT_HALF))
        + values * jnp.exp(-0.5 * values * values) * DENSITY
    )


def gather_tokens(values):
    return lax.all_gather(values, "tp", axis=1, tiled=True)


def gather_grads(values):
    return lax.all_gather(values, "tp", axis=1, tiled=True)


def reduce_tokens(values):
    return lax.psum_scatter(
        values.astype(jnp.bfloat16), "tp", scatter_dimension=1, tiled=True
    ).astype(jnp.float32)


def reduce_grads(values):
    return lax.psum_scatter(
        values.astype(jnp.bfloat16), "tp", scatter_dimension=1, tiled=True
    ).astype(jnp.float32)


def block_scores(query, keyed, picture_query, picture_key, key_mask):
    raw_scores = jnp.einsum("qhd,khd->hqk", query, keyed, preferred_element_type=jnp.float32)
    allowed = (picture_query[:, None] == picture_key[None, :]) & (key_mask[None, :] > 0)
    return jnp.where(allowed[None], raw_scores * query.shape[-1] ** (-0.5), -1e30)


def forward_row(packed):
    query_row, key_row, value_row, picture_row, mask_row = packed
    full_len = query_row.shape[0]
    block_len = min(512, full_len)
    block_count = full_len // block_len

    def forward_one_block(packed_block):
        query_block, picture_block = packed_block
        scores = block_scores(query_block, key_row, picture_block, picture_row, mask_row)
        highest = jnp.max(scores, axis=-1, keepdims=True)
        logsum = highest + jnp.log(jnp.sum(jnp.exp(scores - highest), axis=-1, keepdims=True))
        probability = jnp.exp(scores - logsum).astype(jnp.bfloat16)
        mixture = jnp.einsum(
            "hqk,khd->qhd", probability, value_row, preferred_element_type=jnp.float32
        )
        return (mixture, logsum)

    query_blocks = query_row.reshape((block_count, block_len) + query_row.shape[1:])
    return lax.map(forward_one_block, (query_blocks, picture_row.reshape(block_count, block_len)))


def backward_row(packed):
    query_row, key_row, value_row, picture_row, mask_row, grad_row, logsum_row = packed
    full_len = query_row.shape[0]
    block_len = min(512, full_len)
    block_count = full_len // block_len
    factor = query_row.shape[-1] ** (-0.5)

    def backward_one_block(running, packed_block):
        grad_key, grad_value = running
        query_block, picture_block, grad_block, logsum_block = packed_block
        scores = block_scores(query_block, key_row, picture_block, picture_row, mask_row)
        probability = jnp.exp(scores - logsum_block)
        prob_low = probability.astype(jnp.bfloat16)
        grad_prob = jnp.einsum(
            "qhd,khd->hqk", grad_block, value_row, preferred_element_type=jnp.float32
        )
        grad_value = grad_value + jnp.einsum(
            "hqk,qhd->khd", prob_low, grad_block, preferred_element_type=jnp.float32
        )
        centre = jnp.sum(probability * grad_prob, axis=-1, keepdims=True)
        grad_scores = (probability * (grad_prob - centre)).astype(jnp.bfloat16)
        grad_query = factor * jnp.einsum(
            "hqk,khd->qhd", grad_scores, key_row, preferred_element_type=jnp.float32
        )
        grad_key = grad_key + factor * jnp.einsum(
            "hqk,qhd->khd", grad_scores, query_block, preferred_element_type=jnp.float32
        )
        return ((grad_key, grad_value), grad_query)

    zero_state = jnp.zeros(key_row.shape, jnp.float32)
    block_shape = (block_count, block_len) + query_row.shape[1:]
    (grad_key, grad_value), grad_query = lax.scan(
        backward_one_block,
        (zero_state, zero_state),
        (
            query_row.reshape(block_shape),
            picture_row.reshape(block_count, block_len),
            grad_row.reshape(block_shape),
            logsum_row,
        ),
    )
    return (grad_query.reshape(key_row.shape), grad_key, grad_value)


def local_plain(
    tokens,
    lengths,
    pictures,
    w_query,
    w_key,
    w_value,
    w_out,
    w_up,
    w_down,
    norm1_gain,
    norm1_shift,
    norm2_gain,
    norm2_shift,
    query_gain,
    key_gain,
    cotangent,
):
    tp_place = lax.axis_index("tp")
    local_len = tokens.shape[1]
    model_width = tokens.shape[2]
    full_len = pictures.shape[1]
    local_width = w_query.shape[1]
    heads_local = local_width // HD
    gain_one, shift_one, gain_two, shift_two, gain_query, gain_key = (
        lax.all_gather(norm1_gain, ("fsdp", "tp"), axis=0, tiled=True),
        lax.all_gather(norm1_shift, ("fsdp", "tp"), axis=0, tiled=True),
        lax.all_gather(norm2_gain, ("fsdp", "tp"), axis=0, tiled=True),
        lax.all_gather(norm2_shift, ("fsdp", "tp"), axis=0, tiled=True),
        lax.all_gather(query_gain, ("fsdp", "tp"), axis=0, tiled=True),
        lax.all_gather(key_gain, ("fsdp", "tp"), axis=0, tiled=True),
    )
    positions = jnp.arange(full_len, dtype=jnp.int32)
    valid_full = (positions[None, :] < jnp.sum(lengths, axis=1)[:, None]).astype(jnp.float32)
    valid_here = lax.dynamic_slice_in_dim(valid_full, tp_place * local_len, local_len, 1)[
        :, :, None
    ]
    qgain_here = lax.dynamic_slice_in_dim(
        gain_query, tp_place * local_width, local_width, 0
    ).reshape(heads_local, HD)
    kgain_here = lax.dynamic_slice_in_dim(gain_key, tp_place * local_width, local_width, 0).reshape(
        heads_local, HD
    )
    front_query, front_key, front_value, front_out = (
        lax.all_gather(w_query, "fsdp", axis=0, tiled=True),
        lax.all_gather(w_key, "fsdp", axis=0, tiled=True),
        lax.all_gather(w_value, "fsdp", axis=0, tiled=True),
        lax.all_gather(w_out, "fsdp", axis=1, tiled=True),
    )
    inputs = tokens.astype(jnp.float32)
    hidden, normed_one, inverse_one = normalise(inputs, gain_one, shift_one)
    hidden_full = gather_tokens(hidden.astype(jnp.bfloat16))
    row_shape = hidden_full.shape[:2] + (heads_local, HD)
    query = jnp.dot(hidden_full, front_query, preferred_element_type=jnp.float32).reshape(row_shape)
    keyed = jnp.dot(hidden_full, front_key, preferred_element_type=jnp.float32).reshape(row_shape)
    value_low = (
        jnp.dot(hidden_full, front_value, preferred_element_type=jnp.float32)
        .astype(jnp.bfloat16)
        .reshape(row_shape)
    )
    query_norm, query_unit, query_inverse = normalise(query, qgain_here, 0.0)
    key_norm, key_unit, key_inverse = normalise(keyed, kgain_here, 0.0)
    query_low = query_norm.astype(jnp.bfloat16)
    key_low = key_norm.astype(jnp.bfloat16)
    mixture, logsum = lax.map(forward_row, (query_low, key_low, value_low, pictures, valid_full))
    mixture_low = mixture.reshape(hidden_full.shape[:2] + (local_width,)).astype(jnp.bfloat16)
    attn_branch = valid_here * reduce_tokens(
        jnp.dot(mixture_low, front_out, preferred_element_type=jnp.float32)
    )
    middle = inputs + attn_branch
    hidden_two, normed_two, inverse_two = normalise(middle, gain_two, shift_two)
    hidden_two_full = gather_tokens(hidden_two.astype(jnp.bfloat16))
    front_up, front_down = (
        lax.all_gather(w_up, "fsdp", axis=0, tiled=True),
        lax.all_gather(w_down, "fsdp", axis=1, tiled=True),
    )
    up_value = jnp.dot(hidden_two_full, front_up, preferred_element_type=jnp.float32)
    activated = jax.nn.gelu(up_value, approximate=False).astype(jnp.bfloat16)
    mlp_branch = valid_here * reduce_tokens(
        jnp.dot(activated, front_down, preferred_element_type=jnp.float32)
    )
    result = (middle + mlp_branch).astype(jnp.bfloat16)
    square_sums = jnp.stack(
        [
            jnp.sum(valid_here * inputs * inputs),
            jnp.sum(attn_branch * attn_branch),
            jnp.sum(valid_here * middle * middle),
            jnp.sum(mlp_branch * mlp_branch),
        ]
    )
    valid_count = jnp.sum(valid_here)
    back_up, back_down = (
        lax.all_gather(w_up, "fsdp", axis=0, tiled=True),
        lax.all_gather(w_down, "fsdp", axis=1, tiled=True),
    )
    back_query, back_key, back_value, back_out = (
        lax.all_gather(w_query, "fsdp", axis=0, tiled=True),
        lax.all_gather(w_key, "fsdp", axis=0, tiled=True),
        lax.all_gather(w_value, "fsdp", axis=0, tiled=True),
        lax.all_gather(w_out, "fsdp", axis=1, tiled=True),
    )
    grad_y = cotangent.astype(jnp.float32) * valid_here
    grad_y_full = gather_grads(grad_y.astype(jnp.bfloat16))
    grad_down = jnp.einsum(
        "rlf,rld->fd", activated, grad_y_full, preferred_element_type=jnp.float32
    )
    grad_act = jnp.dot(grad_y_full, back_down.T, preferred_element_type=jnp.float32)
    grad_pre = (grad_act * gelu_slope(up_value)).astype(jnp.bfloat16)
    grad_up = jnp.einsum(
        "rld,rlf->df", hidden_two_full, grad_pre, preferred_element_type=jnp.float32
    )
    grad_hidden_two = reduce_grads(jnp.dot(grad_pre, back_up.T, preferred_element_type=jnp.float32))
    mlp_grads = (
        lax.psum_scatter(grad_up, "fsdp", scatter_dimension=0, tiled=True),
        lax.psum_scatter(grad_down, "fsdp", scatter_dimension=1, tiled=True),
    )
    grad_mid_norm, grad_gain_two, grad_shift_two = normalise_back(
        grad_hidden_two, normed_two, inverse_two, gain_two
    )
    grad_middle = grad_y + grad_mid_norm
    grad_branch_here = (valid_here * grad_middle).astype(jnp.bfloat16)
    grad_branch_full = gather_grads(grad_branch_here)
    grad_out_proj = jnp.einsum(
        "rlh,rld->hd", mixture_low, grad_branch_full, preferred_element_type=jnp.float32
    )
    grad_mixture = jnp.dot(grad_branch_full, back_out.T, preferred_element_type=jnp.float32).astype(
        jnp.bfloat16
    )
    grad_qnorm, grad_knorm, grad_value_full = lax.map(
        backward_row,
        (
            query_low,
            key_low,
            value_low,
            pictures,
            valid_full,
            grad_mixture.reshape(row_shape),
            logsum,
        ),
    )
    grad_query_pre, grad_qgain, unused_one = normalise_back(
        grad_qnorm, query_unit, query_inverse, qgain_here
    )
    grad_key_pre, grad_kgain, unused_two = normalise_back(
        grad_knorm, key_unit, key_inverse, kgain_here
    )
    flat_shape = hidden_full.shape[:2] + (local_width,)
    grad_query_low = grad_query_pre.reshape(flat_shape).astype(jnp.bfloat16)
    grad_key_low = grad_key_pre.reshape(flat_shape).astype(jnp.bfloat16)
    grad_value_low = grad_value_full.reshape(flat_shape).astype(jnp.bfloat16)
    grad_wquery = jnp.einsum(
        "rld,rlh->dh", hidden_full, grad_query_low, preferred_element_type=jnp.float32
    )
    grad_wkey = jnp.einsum(
        "rld,rlh->dh", hidden_full, grad_key_low, preferred_element_type=jnp.float32
    )
    grad_wvalue = jnp.einsum(
        "rld,rlh->dh", hidden_full, grad_value_low, preferred_element_type=jnp.float32
    )
    grad_hidden_part = (
        jnp.dot(grad_query_low, back_query.T, preferred_element_type=jnp.float32)
        + jnp.dot(grad_key_low, back_key.T, preferred_element_type=jnp.float32)
        + jnp.dot(grad_value_low, back_value.T, preferred_element_type=jnp.float32)
    )
    grad_hidden = reduce_grads(grad_hidden_part)
    attn_grads = (
        lax.psum_scatter(grad_wquery, "fsdp", scatter_dimension=0, tiled=True),
        lax.psum_scatter(grad_wkey, "fsdp", scatter_dimension=0, tiled=True),
        lax.psum_scatter(grad_wvalue, "fsdp", scatter_dimension=0, tiled=True),
        lax.psum_scatter(grad_out_proj, "fsdp", scatter_dimension=1, tiled=True),
    )
    grad_in_norm, grad_gain_one, grad_shift_one = normalise_back(
        grad_hidden, normed_one, inverse_one, gain_one
    )
    grad_inputs = grad_middle + grad_in_norm
    zero_width = jnp.zeros((model_width,), jnp.float32)
    grad_qgain_full = lax.dynamic_update_slice_in_dim(
        zero_width, grad_qgain.reshape(local_width), tp_place * local_width, 0
    )
    grad_kgain_full = lax.dynamic_update_slice_in_dim(
        zero_width, grad_kgain.reshape(local_width), tp_place * local_width, 0
    )
    small_shards = (
        lax.psum_scatter(grad_gain_one, ("fsdp", "tp"), scatter_dimension=0, tiled=True),
        lax.psum_scatter(grad_shift_one, ("fsdp", "tp"), scatter_dimension=0, tiled=True),
        lax.psum_scatter(grad_gain_two, ("fsdp", "tp"), scatter_dimension=0, tiled=True),
        lax.psum_scatter(grad_shift_two, ("fsdp", "tp"), scatter_dimension=0, tiled=True),
        lax.psum_scatter(grad_qgain_full, ("fsdp", "tp"), scatter_dimension=0, tiled=True),
        lax.psum_scatter(grad_kgain_full, ("fsdp", "tp"), scatter_dimension=0, tiled=True),
    )
    totals, counted = lax.psum((square_sums, valid_count), ("fsdp", "tp"))
    statistics = jnp.sqrt(totals / (counted * model_width))
    return (
        result,
        grad_inputs,
        attn_grads[0],
        attn_grads[1],
        attn_grads[2],
        attn_grads[3],
        mlp_grads[0],
        mlp_grads[1],
        small_shards[0],
        small_shards[1],
        small_shards[2],
        small_shards[3],
        small_shards[4],
        small_shards[5],
        statistics,
    )


BIG = 1024
SMALL = 448
LP = BIG + 3 * SMALL
MARGIN = 128
EXP_SCALE = 0.125 * 1.4426950408889634
MESH = pl.DeviceIdType.MESH
BF = jnp.bfloat16
F32 = jnp.float32


def dot_nn(a, b):
    return lax.dot_general(a, b, (((1,), (0,)), ((), ())), preferred_element_type=F32)


def dot_nt(a, b):
    return lax.dot_general(a, b, (((1,), (1,)), ((), ())), preferred_element_type=F32)


def dot_tn(a, b):
    return lax.dot_general(a, b, (((0,), (0,)), ((), ())), preferred_element_type=F32)


def iota(shape, dim):
    return lax.broadcasted_iota(jnp.int32, shape, dim)


def head_mask(rows, width, h):
    lane = iota((rows, width), 1)
    return (lane >= h * HD) & (lane < (h + 1) * HD)


def segment_matrix(width):
    r = iota((width, width), 0) // HD
    c = iota((width, width), 1) // HD
    return jnp.where(r == c, 1.0 / HD, 0.0).astype(BF)


def segment_mean(x, seg):
    return dot_nn(x.astype(BF), seg)


class Place:
    def __init__(self, nf, nt):
        self.nf, self.nt = nf, nt
        self.nx = 2
        self.nz = nf // 2
        f = lax.axis_index("fsdp")
        t = lax.axis_index("tp")
        self.f, self.t = f, t
        self.z, self.x = f // 2, lax.rem(f, 2)
        self.y, self.c = t // 2, lax.rem(t, 2)
        self.me = f * nt + t

    def rel(self, dz=0, dx=0, dy=0, dc=0):
        z = lax.rem(self.z + dz, self.nz) if dz else self.z
        x = 1 - self.x if dx else self.x
        y = 1 - self.y if dy else self.y
        c = 1 - self.c if dc else self.c
        return (z * 2 + x, y * 2 + c)


class Copies:
    def __init__(self):
        self.sent = []

    def start(self, src, dst, send_sem, recv_sem, dev):
        cp = pltpu.make_async_remote_copy(
            src_ref=src,
            dst_ref=dst,
            send_sem=send_sem,
            recv_sem=recv_sem,
            device_id=dev,
            device_id_type=MESH,
        )
        cp.start()
        self.sent.append(cp)

    def finish(self):
        for cp in self.sent:
            cp.wait_send()
        self.sent = []


def wait_recv(dst, send_sem, recv_sem, dev):
    pltpu.make_async_remote_copy(
        src_ref=dst,
        dst_ref=dst,
        send_sem=send_sem,
        recv_sem=recv_sem,
        device_id=dev,
        device_id_type=MESH,
    ).wait_recv()


def barrier_peers(pc):
    steps = [dict(dz=i) for i in range(1, pc.nz)]
    steps += [dict(dx=1), dict(dy=1), dict(dc=1), dict(dy=1, dc=1)]
    bar = pltpu.get_barrier_semaphore()
    for step in steps:
        pl.semaphore_signal(bar, inc=1, device_id=pc.rel(**step), device_id_type=MESH)
    pl.semaphore_wait(bar, len(steps))


def axis_steps(pc, axis):
    if axis == "z":
        return [dict(dz=i) for i in range(1, pc.nz)]
    return [{"d" + axis: 1}]


def sends_of(nz, order):
    return sum(nz - 1 if axis == "z" else 1 for axis in order)


class Gather:
    def __init__(self, pc, copies, src, dst, send, recv, dims, order):
        self.pc, self.copies = pc, copies
        self.src, self.dst, self.send_sem, self.recv_sem = src, dst, send, recv
        self.dims, self.order = dims, order
        self.stages = []
        count = 0
        for axis in order:
            steps = axis_steps(pc, axis)
            self.stages.append([(count + i, step) for i, step in enumerate(steps)])
            count += len(steps)

    def index(self, stage, at=None):
        place = at or dict(z=self.pc.z, x=self.pc.x, y=self.pc.y, c=self.pc.c)
        done = self.order[:stage]
        return tuple(slice(None) if d in done else place[d] for d in self.dims)

    def keep(self, sem):
        self.local = pltpu.make_async_copy(self.src, self.dst.at[self.index(0)], sem)
        self.local.start()

    def send(self, k):
        if k == 1:
            self.local.wait()
        idx = self.index(k)
        src = self.src if k == 0 else self.dst.at[idx]
        for n, step in self.stages[k]:
            self.copies.start(
                src, self.dst.at[idx], self.send_sem.at[n], self.recv_sem.at[n], self.pc.rel(**step)
            )

    def wait(self, k):
        pc = self.pc
        for n, step in self.stages[k]:
            at = dict(z=pc.z, x=pc.x, y=pc.y, c=pc.c)
            if "dz" in step:
                at["z"] = lax.rem(pc.z + pc.nz - step["dz"], pc.nz)
            else:
                axis = self.order[k]
                at[axis] = 1 - at[axis]
            dst = self.dst.at[self.index(k, at)]
            wait_recv(dst, self.send_sem.at[n], self.recv_sem.at[n], pc.rel(**step))


def slots_of(lens_ref):
    lens = [lens_ref[0, p] for p in range(4)]
    starts = [0]
    for p in range(3):
        starts.append(starts[-1] + lens[p])
    big = 0
    for p in range(1, 4):
        big = jnp.where(lens[p] == BIG, p, big)
    sb = 0
    for p in range(1, 4):
        sb = jnp.where(big == p, starts[p], sb)
    out = [(sb, BIG)]
    for k in range(3):
        s = jnp.where(big <= k, starts[k + 1], starts[k])
        n = jnp.where(big <= k, lens[k + 1], lens[k])
        out.append((s, n))
    return out


BASES = (0, BIG, BIG + SMALL, BIG + 2 * SMALL)


def shift_matrix(rows, cols, r):
    return jnp.where(iota((rows, cols), 1) == iota((rows, cols), 0) + r, 1.0, 0.0).astype(BF)


def load_rows(src, first, count):
    return jnp.concatenate([src[first + m] for m in range(count)], axis=0)


def pack_rows(src, dst, lens, masked=False):
    def big(j, carry):
        s = slots_of(lens)[0][0]
        r = lax.rem(s, 16)
        d = shift_matrix(128, 144, r)
        out = dot_nn(d, load_rows(src, s // 16 + j * 8, 9)).astype(BF)
        dst[pl.ds(pl.multiple_of(j * 128, 128), 128), :] = out
        return carry

    lax.fori_loop(0, BIG // 128, big, 0)

    for k in range(3):

        def small(j, carry, k=k):
            s, n = slots_of(lens)[1 + k]
            r = lax.rem(s, 16)
            d = shift_matrix(112, 128, r)
            out = dot_nn(d, load_rows(src, s // 16 + j * 7, 8))
            if masked:
                out = jnp.where(iota(out.shape, 0) + j * 112 < n, out, 0.0)
            out = out.astype(BF)
            dst[pl.ds(pl.multiple_of(BASES[1 + k] + j * 112, 16), 112), :] = out
            return carry

        lax.fori_loop(0, 4, small, 0)


def unpack_tile(src, i0, lens):
    wa, ea, wb, sb = 0, 0, 0, 4096
    for (s, n), base in zip(slots_of(lens), BASES):
        inside = (s <= i0) & (i0 < s + n)
        begins = (s > i0) & (s <= i0 + 127)
        w = base + i0 - s + MARGIN
        wa = jnp.where(inside, w, wa)
        ea = jnp.where(inside, s + n - i0, ea)
        wb = jnp.where(begins, w, wb)
        sb = jnp.where(begins, s - i0, sb)
    out = None
    row = iota((128, 144), 0)
    col = iota((128, 144), 1)
    for w, ok in ((wa, lambda: row < ea), (wb, lambda: row >= sb)):
        r = lax.rem(w, 16)
        d = jnp.where((col == row + r) & ok(), 1.0, 0.0).astype(BF)
        part = dot_nn(d, load_rows(src, w // 16, 9))
        out = part if out is None else out + part
    return out


def layer_norm_rows(x, g, b):
    mean = jnp.mean(x, axis=-1, keepdims=True)
    xc = x - mean
    var = jnp.mean(xc * xc, axis=-1, keepdims=True)
    inv = lax.rsqrt(var + EPS)
    n = xc * inv
    return n * g + b, n, inv


def own_heads(row, t, nt, width):
    out = row[:, :width]
    for k in range(1, nt):
        out = jnp.where(t == k, row[:, k * width : (k + 1) * width], out)
    return out


def build_gains(tiles, gains, per):
    chunks = len(tiles) * per // 128
    lane = iota((8, 128), 1)
    acc = [jnp.zeros((8, 128), F32) for _ in range(chunks)]
    for d, tile in enumerate(tiles):
        j, a = divmod(d * per, 128)
        if a:
            tile = pltpu.roll(tile, a, 1)
        acc[j] = jnp.where((lane >= a) & (lane < a + per), tile, acc[j])
        if a + per > 128:
            acc[j + 1] = jnp.where(lane < a + per - 128, tile, acc[j + 1])
    for j in range(chunks):
        gains[:, j * 128 : (j + 1) * 128] = acc[j]


def ka_kernel(
    nf, nt, orders,
    lens, tok, wa, wo, wu, wd, prm,
    qkv_out, lse_out, ob_out, wqkv, gains, o_own, h1_out, wo_all, wu0_all, wu1_all, wd0_all, wd1_all,
    qkv, lse, ob, tok_all, h1t, h1p, wa_all, prm_all, of, op, osend,
    prm_s, prm_r, tok_s, tok_r, wa_s, wa_r, wo_s, wo_r,
    u0_s, u0_r, u1_s, u1_r, d0_s, d0_r, d1_s, d1_r, o_s, o_r, loc,
):
    pc = Place(nf, nt)
    cps = Copies()
    rows, width = tok.shape
    hw = ob.shape[1]
    cut = width // 2
    gp = Gather(pc, cps, prm, prm_all, prm_s, prm_r, "zxyc", orders["prm"])
    ga = Gather(pc, cps, wa, wa_all, wa_s, wa_r, "zx", orders["wa"])
    go = Gather(pc, cps, wo, wo_all, wo_s, wo_r, "yczx", orders["wo"])
    gu0 = Gather(pc, cps, wu.at[:, :cut], wu0_all, u0_s, u0_r, "yzx", orders["u0"])
    gu1 = Gather(pc, cps, wu.at[:, cut:], wu1_all, u1_s, u1_r, "yzx", orders["u1"])
    gd0 = Gather(pc, cps, wd.at[:, :cut], wd0_all, d0_s, d0_r, "yzx", orders["d0"])
    gd1 = Gather(pc, cps, wd.at[:, cut:], wd1_all, d1_s, d1_r, "yzx", orders["d1"])
    for i, g in enumerate((gp, ga, go, gd1, gu0, gd0, gu1)):
        g.keep(loc.at[i])
    barrier_peers(pc)

    cps.start(tok, tok_all.at[pc.t], tok_s.at[1], tok_r.at[pc.t], pc.rel(dc=1))
    gp.send(0)
    ga.send(0)
    gd1.send(0)
    cps.start(tok, tok_all.at[pc.t], tok_s.at[0], tok_r.at[pc.t], pc.rel(dy=1))
    h1t[4 * rows // 16 :] = jnp.zeros((h1t.shape[0] - 4 * rows // 16, 16, width), BF)
    for k in range(4):
        gp.wait(k)
        if k < 3:
            gp.send(k + 1)
    gd1.wait(0)
    gd1.send(1)
    go.send(0)
    tiles = []
    for d in range(nf * nt):
        f, t = divmod(d, nt)
        tiles.append(prm_all[f // 2, f % 2, t // 2, t % 2])
    build_gains(tiles, gains, width // (nf * nt))
    gain_one, shift_one = gains[0:1, :], gains[1:2, :]

    def norm_block(t, block):
        def body(j, carry):
            at = pl.ds(pl.multiple_of(j * 128, 128), 128)
            out, _, _ = layer_norm_rows(block[at, :].astype(F32), gain_one, shift_one)
            h1t[pl.ds(t * (rows // 16) + j * 8, 8)] = out.astype(BF).reshape(8, 16, width)
            return carry

        lax.fori_loop(0, rows // 128, body, 0)

    def wait_tok(t):
        wait_recv(tok_all.at[t], tok_s.at[0], tok_r.at[t], pc.rel(dc=1))

    norm_block(pc.t, tok)
    t_core, t_y, t_diag = pc.rel(dc=1)[1], pc.rel(dy=1)[1], pc.rel(dy=1, dc=1)[1]
    wait_tok(t_core)
    norm_block(t_core, tok_all.at[t_core])
    ga.wait(0)
    ga.send(1)
    gu0.send(0)
    gd0.send(0)
    wait_tok(t_y)
    cps.start(tok_all.at[t_y], tok_all.at[t_y], tok_s.at[2], tok_r.at[t_y], pc.rel(dc=1))
    norm_block(t_y, tok_all.at[t_y])
    wait_tok(t_diag)
    norm_block(t_diag, tok_all.at[t_diag])
    h1_copy = pltpu.make_async_copy(h1t.at[: 4 * rows // 16], h1_out, loc.at[0])
    h1_copy.start()

    pack_rows(h1t, h1p, lens)
    go.wait(0)
    go.send(1)
    gu0.wait(0)
    gu0.send(1)
    gd0.wait(0)
    gd0.send(1)
    gu1.send(0)
    gd1.wait(1)
    ga.wait(1)
    seg = segment_matrix(hw)
    gq = own_heads(gains[4:5, :], pc.t, nt, hw)
    gk = own_heads(gains[5:6, :], pc.t, nt, hw)
    w_full = wa_all[...].reshape(width, 3 * hw)
    for i in range(3):
        wqkv[i] = w_full[:, i * hw : (i + 1) * hw]

    qt = LP // 4

    def project(j, carry):
        at = pl.ds(pl.multiple_of(j * qt, 16), qt)
        h = h1p[at, :]
        lane = iota((qt, 128), 1)
        kept = jnp.zeros((qt, 128), F32)
        for i, g in enumerate((gq, gk)):
            q = dot_nn(h, wqkv[i])
            qc = q - segment_mean(q, seg)
            inv = lax.rsqrt(segment_mean(qc * qc, seg) + EPS)
            qkv[at, i * 256 : i * 256 + hw] = (qc * inv * g).astype(BF)
            for k in range(hw // HD):
                kept = jnp.where(lane == 8 * (i + 1) + k, inv[:, k * HD : k * HD + 1], kept)
        lse[at, :] = kept
        qkv[at, 512 : 512 + hw] = dot_nn(h, wqkv[2]).astype(BF)
        return carry

    lax.fori_loop(0, 4, project, 0)
    qkv[:, 512 + hw :] = jnp.ones((LP, 256 - hw), BF)
    saves = [h1_copy, pltpu.make_async_copy(qkv, qkv_out, loc.at[2])]
    saves[-1].start()
    head, tail = MARGIN // 16, (MARGIN + LP) // 16
    op[:head] = jnp.zeros((head, 16, hw), BF)
    op[tail:] = jnp.zeros((op.shape[0] - tail, 16, hw), BF)

    gu0.wait(1)
    gu0.send(2)
    gd0.wait(1)
    gd0.send(2)
    go.wait(1)
    go.send(2)
    gd1.send(2)

    def attend(at, keys, h, limit):
        nrow = at.size
        q = jnp.where(head_mask(nrow, hw, h), qkv[at, :hw], jnp.zeros((), BF))
        s = dot_nt(q, qkv[keys, 256 : 256 + hw])
        p = jnp.exp2(s * EXP_SCALE)
        if limit is not None:
            p = jnp.where(iota(p.shape, 1) < limit, p, 0.0)
        oa = dot_nn(p.astype(BF), qkv[keys, 512:768])
        total = oa[:, hw : hw + 1]
        o = oa[:, :hw] * (1.0 / total)
        l2 = jnp.log2(total)
        lane = iota((nrow, 128), 1)
        if h == 0:
            of[at, :] = o
        else:
            of[at, :] = jnp.where(head_mask(nrow, hw, h), o, of[at, :])
        lse[at, :] = jnp.where(lane == h, l2, lse[at, :])

    nh = hw // HD
    for h in range(nh):
        def big(j, carry, h=h):
            attend(pl.ds(pl.multiple_of(j * 512, 512), 512), pl.ds(0, BIG), h, None)
            return carry

        lax.fori_loop(0, BIG // 512, big, 0)

        for k in range(3):
            at = pl.ds(BASES[1 + k], SMALL)
            attend(at, at, h, slots_of(lens)[1 + k][1])
        if h == 0:
            gu1.wait(0)
            gu1.send(1)
        elif h == 2:
            go.wait(2)
            go.send(3)
            gu1.wait(1)
            gu1.send(2)

    ob[...] = of[...].astype(BF)
    for i, (src, dst) in enumerate(((lse, lse_out), (ob, ob_out))):
        saves.append(pltpu.make_async_copy(src, dst, loc.at[3 + i]))
        saves[-1].start()
    op[head:tail] = ob[...].reshape(LP // 16, 16, hw)

    def unpack_block(t):
        def unpack(i, carry):
            out = unpack_tile(op, t * rows + i * 128, lens)
            osend[t, pl.ds(pl.multiple_of(i * 128, 128), 128), :] = out.astype(BF)
            return carry

        lax.fori_loop(0, rows // 128, unpack, 0)

    peers = [pc.rel(dy=1, dc=1), pc.rel(dy=1), pc.rel(dc=1)]
    for i, dev in enumerate(peers):
        unpack_block(dev[1])
        cps.start(osend.at[dev[1]], o_own.at[pc.t], o_s.at[i], o_r.at[pc.t], dev)
    unpack_block(pc.t)
    cp = pltpu.make_async_copy(osend.at[pc.t], o_own.at[pc.t], loc.at[1])
    cp.start()
    cp.wait()
    for cp in saves:
        cp.wait()
    go.wait(3)
    for g in (gu0, gd0, gu1, gd1):
        g.wait(2)
    for dev in peers:
        wait_recv(o_own.at[dev[1]], o_s.at[0], o_r.at[dev[1]], dev)
    cps.finish()


def call_ka(nf, nt, lens, tok, wa, wo, wu, wd, prm):
    nz = nf // 2
    rows, width = tok.shape
    r = wa.shape[0]
    hw = wa.shape[1] // 3
    cut = width // 2
    orders = dict(
        prm=("z", "x", "y", "c"), wa=("z", "x"), wo=("z", "y", "x", "c"),
        u0=("z", "y", "x"), d0=("z", "x", "y"), u1=("z", "y", "x"), d1=("y", "x", "z"),
    )
    S = jax.ShapeDtypeStruct
    V = pltpu.VMEM
    vm = pl.BlockSpec(memory_space=pltpu.VMEM)
    hb = pl.BlockSpec(memory_space=pl.ANY)
    half = (S((2, nz, 2, r, cut), BF), hb)
    outs = [
        (S((LP, 768), BF), hb), (S((LP, 128), F32), hb), (S((LP, hw), BF), hb), (S((3, width, hw), BF), vm),
        (S((8, width), F32), vm), (S((nt, rows, hw), BF), vm),
        (S((nt * rows // 16, 16, width), BF), hb), (S((2, 2, nz, 2, r, hw), BF), hb), half, half, half, half,
    ]
    dma = pltpu.SemaphoreType.DMA
    scratch = [
        V((LP, 768), BF), V((LP, 128), F32), V((LP, hw), BF),
        V((nt, rows, width), BF), V(((nt * rows + 192) // 16, 16, width), BF), V((LP, width), BF),
        V((nz, 2, r, 3 * hw), BF), V((nz, 2, 2, 2, 8, 128), F32),
        V((LP, hw), F32), V(((MARGIN + LP + 160) // 16, 16, hw), BF), V((nt, rows, hw), BF),
    ]
    p = sends_of(nz, orders["prm"])
    scratch += [dma((p,)), dma((p,)), dma((3,)), dma((nt,))]
    for name in ("wa", "wo", "u0", "u1", "d0", "d1"):
        p = sends_of(nz, orders[name])
        scratch += [dma((p,)), dma((p,))]
    scratch += [dma((3,)), dma((nt,)), dma((8,))]
    return pl.pallas_call(
        functools.partial(ka_kernel, nf, nt, orders),
        out_shape=[o[0] for o in outs],
        in_specs=[pl.BlockSpec(memory_space=pltpu.SMEM), vm, vm, hb, hb, hb, vm],
        out_specs=[o[1] for o in outs],
        scratch_shapes=scratch,
        compiler_params=pltpu.CompilerParams(
            collective_id=0, has_side_effects=True, vmem_limit_bytes=56 << 20
        ),
    )(lens, tok, wa, wo, wu, wd, prm)


class Scatter:
    def __init__(self, pc, copies, own, land, send, recv, dims, order):
        self.pc, self.copies, self.own, self.land = pc, copies, own, land
        self.send_sem, self.recv_sem, self.dims, self.order = send, recv, dims, order
        self.place = dict(z=pc.z, x=pc.x, y=pc.y, c=pc.c)
        self.stage = 0
        self.count = 0
        self.waits = []

    def index(self, done, at):
        return tuple(at[d] if d in done else slice(None) for d in self.dims)

    def start(self):
        pc, axis = self.pc, self.order[self.stage]
        done = self.order[: self.stage + 1]
        self.waits = []
        for i, step in enumerate(axis_steps(pc, axis)):
            at = dict(self.place)
            at[axis] = lax.rem(pc.z + step["dz"], pc.nz) if axis == "z" else 1 - at[axis]
            dst = self.land[self.stage].at[i]
            n, dev = self.count, pc.rel(**step)
            self.copies.start(self.own.at[self.index(done, at)], dst, self.send_sem.at[n], self.recv_sem.at[n], dev)
            self.waits.append((dst, n, dev))
            self.count += 1

    def arrive(self):
        for dst, n, dev in self.waits:
            wait_recv(dst, self.send_sem.at[n], self.recv_sem.at[n], dev)
        land = self.land[self.stage]
        done = self.order[: self.stage + 1]
        rest = [d for d in self.dims if d not in done]
        sizes = [self.pc.nz if d == "z" else 2 for d in rest]
        count = 1
        for n in sizes:
            count *= n

        def body(i, carry):
            at, k = dict(self.place), i
            for d, n in reversed(list(zip(rest, sizes))):
                at[d] = lax.rem(k, n)
                k = k // n
            dst = self.own.at[tuple(at[d] for d in self.dims)]
            total = dst[...].astype(F32)
            for n in range(len(self.waits)):
                total = total + land[(n,) + tuple(at[d] for d in rest)].astype(F32)
            dst[...] = total.astype(BF)
            return carry

        lax.fori_loop(0, count, body, 0)
        self.stage += 1

    def next(self):
        self.arrive()
        self.start()

    def finish(self, out):
        for dst, n, dev in self.waits:
            wait_recv(dst, self.send_sem.at[n], self.recv_sem.at[n], dev)
        total = self.own[tuple(self.place[d] for d in self.dims)].astype(F32)
        for n in range(len(self.waits)):
            total = total + self.land[self.stage][n].astype(F32)
        out(total)


def landing(nz, dims, order, block):
    out = []
    for k, axis in enumerate(order):
        rest = [d for d in dims if d not in order[: k + 1]]
        n = nz - 1 if axis == "z" else 1
        out.append((n,) + tuple(nz if d == "z" else 2 for d in rest) + block)
    return out


def erf_parts(u):
    half = 0.5 * (1.0 + lax.erf(u * ROOT_HALF))
    return u * half, half + u * jnp.exp2(u * u * (-0.5 * 1.4426950408889634)) * DENSITY


def kc_kernel(
    nf, nt, orders,
    lens, tok, cot, o_own, wo, wqkv, gains, lse, ob, qkv, h1, wu0, wu1, wd0, wd1,
    out_ref, dx_out, gqk_out, gv_out, gwo_out, gwu_out, gwd_out, small_out,
    *rest,
):
    (sm, g1b, g2b, wb, inv2, h2a, dya, fs, hs, hr, dz, dos, dot_all, dop, delta, dhr, dhy, gq0_own, gq1_own, sm_src, sm_dst,
     o_part, u0_own, u1_own, d0_own, d1_own, h2_s, h2_r, dy_s, dy_r, f_s, f_r, hh_s, hh_r, do_s, do_r, dh_s, dh_r,
     st_s, st_r, loc) = rest[:41]
    rest = list(rest[41:])
    lands = {}
    for name in ("o", "u0", "u1", "d0", "d1", "q0", "q1"):
        k = len(orders[name])
        lands[name] = (rest[:k], rest[k], rest[k + 1])
        rest = rest[k + 2 :]
    pc = Place(nf, nt)
    cps = Copies()
    rows, width = tok.shape
    hw = ob.shape[1]
    nh = hw // HD
    groups = rows // 16
    r = width // nf
    c_me, c_other = pc.c, 1 - pc.c
    core = pc.rel(dc=1)

    local = []
    cut = width // 2
    for y in range(2):
        for base, lo, hi in ((y, wu0, wu1), (2 + y, wd0, wd1)):
            local.append((lo.at[y], wb.at[pl.ds(base * width, width), pl.ds(0, cut)]))
            local.append((hi.at[y], wb.at[pl.ds(base * width, width), pl.ds(cut, cut)]))
    weights = []
    for i, (src, dst) in enumerate(local):
        cp = pltpu.make_async_copy(src, dst, loc.at[i])
        cp.start()
        weights.append(cp)
    cot_copy = pltpu.make_async_copy(cot, dya.at[pc.c], loc.at[8])
    cot_copy.start()
    barrier_peers(pc)

    def slot_valid(t, first, count):
        row = iota((count, 1), 0) + (t * rows + first)
        total = lens[0, 0] + lens[0, 1] + lens[0, 2] + lens[0, 3]
        return jnp.where(row < total, 1.0, 0.0)

    half = rows // 2

    def own_dy(j, carry):
        at = pl.ds(pl.multiple_of(j * half, half), half)
        v = slot_valid(pc.t, j * half, half)
        dya[c_me, at, :] = (dya[c_me, at, :].astype(F32) * v).astype(BF)
        return carry

    cot_copy.wait()
    lax.fori_loop(0, 2, own_dy, 0)
    cps.start(dya.at[c_me], dya.at[c_me], dy_s.at[0], dy_r.at[0], core)
    gain, shift = gains[2:3, :], gains[3:4, :]
    none = jnp.zeros((1, width), F32)

    def colsum(x):
        return jnp.sum(x, axis=0, keepdims=True)

    def attn_out(j, carry):
        at = pl.ds(pl.multiple_of(j * half, half), half)
        v = slot_valid(pc.t, j * half, half)
        a = dot_nt(o_own[0, at, :], wo[0])
        for t in range(1, nt):
            a += dot_nt(o_own[t, at, :], wo[t])
        a = a * v
        x = tok[at, :].astype(F32)
        m = x + a
        h, n, inv = layer_norm_rows(m, gain, shift)
        sm[pl.ds(pl.multiple_of(j * half, half), half), :] = m
        sm[pl.ds(pl.multiple_of(rows + j * half, half), half), :] = n
        inv2[at, :] = jnp.broadcast_to(inv, (half, 128))
        h2a[c_me, at, :] = h.astype(BF)
        pltpu.make_async_remote_copy(
            src_ref=h2a.at[c_me, at], dst_ref=h2a.at[c_me, at], send_sem=h2_s.at[j], recv_sem=h2_r.at[j],
            device_id=core, device_id_type=MESH,
        ).start()
        return (carry[0] + colsum(x * x * v), carry[1] + colsum(a * a), carry[2] + colsum(m * m * v))

    sum_x, sum_a, sum_m = lax.fori_loop(0, 2, attn_out, (none, none, none))
    for cp in weights:
        cp.wait()

    def h2_copy(j, slot):
        at = pl.ds(pl.multiple_of(j * half, half), half)
        return pltpu.make_async_remote_copy(
            src_ref=h2a.at[slot, at], dst_ref=h2a.at[slot, at], send_sem=h2_s.at[j], recv_sem=h2_r.at[j],
            device_id=core, device_id_type=MESH,
        )

    def back_copy(j, src, dst, send, recv):
        at = pl.ds(pl.multiple_of(j * half, half), half)
        return pltpu.make_async_remote_copy(
            src_ref=src.at[at], dst_ref=dst.at[at], send_sem=send.at[j], recv_sem=recv.at[j],
            device_id=core, device_id_type=MESH,
        )

    def feed(i, carry):
        far = i // 2
        j = lax.rem(i, 2)
        slot = c_me + far * (1 - 2 * c_me)
        at = pl.ds(pl.multiple_of(j * half, half), half)

        @pl.when(far == 1)
        def _():
            h2_copy(j, c_other).wait_recv()

        @pl.when(i == 2)
        def _():
            wait_recv(dya.at[c_other], dy_s.at[0], dy_r.at[0], core)

        h = h2a[slot, at, :]
        g = dya[slot, at, :]
        f, dh = None, None
        for y in range(2):
            up = wb[y * width : (y + 1) * width, :]
            down = wb[(2 + y) * width : (3 + y) * width, :]
            act, slope = erf_parts(dot_nn(h, up))
            act = act.astype(BF)
            g1b[pl.ds(pl.multiple_of((y * 2 + slot) * rows + j * half, half), half), :] = act
            fy = dot_nt(act, down)
            du = (dot_nn(g, down) * slope).astype(BF)
            g2b[pl.ds((y * 2 + slot) * groups + j * (half // 16), half // 16)] = du.reshape(half // 16, 16, width)
            dy = dot_nt(du, up)
            f = fy if f is None else f + fy
            dh = dy if dh is None else dh + dy

        @pl.when(far == 0)
        def _():
            sm[pl.ds(pl.multiple_of(2 * rows + j * half, half), half), :] = f
            sm[pl.ds(pl.multiple_of(3 * rows + j * half, half), half), :] = dh

        @pl.when(far == 1)
        def _():
            fs[at, :] = f.astype(BF)
            hs[at, :] = dh.astype(BF)
            back_copy(j, hs, hr, hh_s, hh_r).start()
            back_copy(j, fs, fr_in, f_s, f_r).start()

        return carry

    fr_in = hr.at[pl.ds(rows, rows)]
    lax.fori_loop(0, 4, feed, 0)

    def rows_of(ref, y):
        return ref[pl.ds(y * 2 * rows, 2 * rows), :]

    dyall = dya[...].reshape(2 * rows, width)
    part_w = width // 2
    zblk = pc.nz // 2

    def weight_grad(left, get_right, lo, hi):
        for q in range(2):
            lq = left[:, q * part_w : (q + 1) * part_w]

            def body(y, carry, lq=lq, q=q):
                g = dot_tn(lq, get_right(y)).astype(BF)
                lo[y, q * zblk : (q + 1) * zblk] = g[:, :cut].reshape(zblk, 2, r, cut)
                hi[y, q * zblk : (q + 1) * zblk] = g[:, cut:].reshape(zblk, 2, r, cut)
                return carry

            lax.fori_loop(0, 2, body, 0)

    def scatter(name, own, dims):
        land, send, recv = lands[name]
        return Scatter(pc, cps, own, land, send, recv, dims, orders[name])

    weight_grad(dyall, lambda y: g1b[pl.ds(pl.multiple_of(y * 2 * rows, rows), 2 * rows), :], d0_own, d1_own)
    sc_d0 = scatter("d0", d0_own, "yzx")
    sc_d1 = scatter("d1", d1_own, "yzx")
    sc_d0.start()
    sc_d1.start()
    qkv_copy = pltpu.make_async_copy(qkv, g1b, loc.at[0])
    qkv_copy.start()

    def ln_back(j, carry):
        at = pl.ds(pl.multiple_of(j * half, half), half)
        back_copy(j, hs, hr, hh_s, hh_r).wait_recv()
        back_copy(j, fs, fr_in, f_s, f_r).wait_recv()
        v = slot_valid(pc.t, j * half, half)
        e = sm[pl.ds(pl.multiple_of(3 * rows + j * half, half), half), :] + hr[at, :].astype(F32)
        f = sm[pl.ds(pl.multiple_of(2 * rows + j * half, half), half), :]
        f = (f + hr[pl.ds(pl.multiple_of(rows + j * half, half), half), :].astype(F32)) * v
        m = sm[pl.ds(pl.multiple_of(j * half, half), half), :]
        n = sm[pl.ds(pl.multiple_of(rows + j * half, half), half), :]
        out_ref[at, :] = (m + f).astype(BF)
        c = e * gain
        dm = dya[c_me, at, :].astype(F32) + inv2[at, 0:1] * (
            c - jnp.mean(c, axis=-1, keepdims=True) - n * jnp.mean(c * n, axis=-1, keepdims=True)
        )
        dx_out[at, :] = dm
        z = (dm * v).astype(BF)
        dz[at, :] = z
        for t in range(nt):
            d = dot_nn(z, wo[t]).astype(BF)
            dos[t, pl.ds(j * (half // 16), half // 16)] = d.reshape(half // 16, 16, hw)
        return (carry[0] + colsum(e * n), carry[1] + colsum(e), carry[2] + colsum(f * f))

    sum_g2, sum_b2, sum_f = lax.fori_loop(0, 2, ln_back, (none, none, none))
    peers = [pc.rel(dy=1), pc.rel(dy=1, dc=1), core]
    own_groups = pl.ds(pc.t * groups, groups)
    for i, dev in enumerate(peers):
        cps.start(dos.at[dev[1]], dot_all.at[own_groups], do_s.at[i], do_r.at[pc.t], dev)
    cp = pltpu.make_async_copy(dos.at[pc.t], dot_all.at[own_groups], loc.at[2])
    cp.start()
    h1_copy = pltpu.make_async_copy(h1, wb.at[pl.ds(0, nt * rows)], loc.at[1])
    h1_copy.start()

    hall = h2a[...].reshape(2 * rows, width)
    weight_grad(
        hall,
        lambda y: g2b[pl.ds(y * 2 * groups, 2 * groups)].reshape(2 * rows, width),
        u0_own, u1_own,
    )
    sc_u0 = scatter("u0", u0_own, "yzx")
    sc_u1 = scatter("u1", u1_own, "yzx")
    sc_u0.start()
    for t in range(nt):
        o_part[t // 2, t % 2] = dot_tn(dz[...], o_own[t]).astype(BF).reshape(pc.nz, 2, r, hw)
    sc_o = scatter("o", o_part, "yczx")
    sc_o.start()

    small_out[...] = jnp.zeros(small_out.shape, F32)
    tail = 4 * groups
    dot_all[tail:] = jnp.zeros((dot_all.shape[0] - tail, 16, hw), BF)
    sm[...] = jnp.zeros(sm.shape, F32)
    head, mid = MARGIN // 16, (MARGIN + LP) // 16
    g2b[:head] = jnp.zeros((head, 16, width), BF)
    g2b[mid:] = jnp.zeros((g2b.shape[0] - mid, 16, width), BF)
    cp.wait()
    for dev in peers:
        wait_recv(dot_all.at[pl.ds(dev[1] * groups, groups)], do_s.at[0], do_r.at[dev[1]], dev)
    sc_u1.start()
    pack_rows(dot_all, dop, lens, True)

    dlt = LP // 4

    def deltas(j, carry):
        at = pl.ds(pl.multiple_of(j * dlt, 16), dlt)
        prod = dop[at, :].astype(F32) * ob[at, :].astype(F32)
        lane = iota((dlt, 128), 1)
        out = jnp.zeros((dlt, 128), F32)
        for h in range(nh):
            part_h = jnp.where(head_mask(dlt, hw, h), prod, 0.0)
            out = jnp.where(lane == h, jnp.sum(part_h, axis=-1, keepdims=True), out)
        delta[at, :] = out
        return carry

    lax.fori_loop(0, 4, deltas, 0)
    qkv_copy.wait()

    def back(at, keys, h, limit):
        nrow, nkey = at.size, keys.size
        zero = jnp.zeros((), BF)
        hm = head_mask(nrow, hw, h)
        q = jnp.where(hm, g1b[at, :hw], zero)
        s = dot_nt(q, g1b[keys, 256 : 256 + hw])
        p = jnp.exp2(s * EXP_SCALE - lse[at, h : h + 1])
        if limit is not None:
            p = jnp.where(iota(p.shape, 1) < limit, p, 0.0)
        g = jnp.where(hm, dop[at, :], zero)
        dp = dot_nt(g, g1b[keys, 512 : 512 + hw])
        ds = (p * (dp - delta[at, h : h + 1])).astype(BF)
        sm[keys, 512 : 512 + hw] += dot_tn(p.astype(BF), g)
        sm[keys, 256 : 256 + hw] += dot_tn(ds, q)
        km = jnp.where(head_mask(nkey, hw, h), g1b[keys, 256 : 256 + hw], zero)
        sm[at, :hw] += dot_nn(ds, km)

    for h in range(nh):
        def big(j, carry, h=h):
            back(pl.ds(pl.multiple_of(j * 256, 256), 256), pl.ds(0, BIG), h, None)
            return carry

        lax.fori_loop(0, BIG // 256, big, 0)
        for k in range(3):
            at = pl.ds(BASES[1 + k], SMALL)
            back(at, at, h, slots_of(lens)[1 + k][1])
        if h == 0:
            sc_d0.next()
            sc_o.next()
        elif h == 1:
            sc_u0.next()
            sc_d1.next()
            sc_o.next()
        else:
            sc_u1.next()
            sc_d0.next()
            sc_o.next()

    seg = segment_matrix(hw)
    gq = own_heads(gains[4:5, :], pc.t, nt, hw)
    gk = own_heads(gains[5:6, :], pc.t, nt, hw)

    def norms(j, carry):
        at = pl.ds(pl.multiple_of(j * dlt, 16), dlt)
        kept = lse[at, :]
        sums, outs = [], []
        for i, g in enumerate((gq, gk)):
            inv = jnp.broadcast_to(kept[:, 8 * (i + 1) : 8 * (i + 1) + 1], (dlt, hw))
            for k in range(1, nh):
                inv = jnp.where(head_mask(dlt, hw, k), kept[:, 8 * (i + 1) + k : 8 * (i + 1) + k + 1], inv)
            n = g1b[at, i * 256 : i * 256 + hw].astype(F32) / g
            e = sm[at, i * 256 : i * 256 + hw] * 0.125
            c = e * g
            d = inv * (c - segment_mean(c, seg) - n * segment_mean(c * n, seg))
            outs.append(d.astype(BF))
            sums.append(colsum(e * n))
        outs.append(sm[at, 512 : 512 + hw].astype(BF))
        for i, d in enumerate(outs):
            g2b[pl.ds(head + j * (dlt // 16), dlt // 16), :, i * 256 : i * 256 + hw] = d.reshape(dlt // 16, 16, hw)
        return (carry[0] + sums[0], carry[1] + sums[1])

    nones = jnp.zeros((1, hw), F32)
    sum_q, sum_k = lax.fori_loop(0, 4, norms, (nones, nones))
    sc_u0.next()
    sc_d1.next()

    def unpack(i, carry):
        out = unpack_tile(g2b, i * 128, lens)
        g1b[pl.ds(pl.multiple_of(i * 128, 128), 128), :] = out.astype(BF)
        return carry

    lax.fori_loop(0, 16, unpack, 0)
    h1_copy.wait()
    sc_u1.next()

    def project(t, sums):
        def body(j, carry):
            at = pl.ds(pl.multiple_of(t * rows + j * half, half), half)
            total = dot_nt(g1b[at, :hw], wqkv[0])
            total += dot_nt(g1b[at, 256 : 256 + hw], wqkv[1])
            total += dot_nt(g1b[at, 512 : 512 + hw], wqkv[2])
            low = total.astype(BF)
            g2b[pl.ds(t * groups + j * (half // 16), half // 16)] = low.reshape(half // 16, 16, width)
            return (carry[0] + colsum(total * wb[at, :].astype(F32)), carry[1] + colsum(total))

        return lax.fori_loop(0, 2, body, sums)

    def add_groups(t, src):
        def body(j, carry):
            at = pl.ds(t * groups + j * 4, 4)
            g2b[at] = (g2b[at].astype(F32) + src[pl.ds(j * 4, 4)].astype(F32)).astype(BF)
            return carry

        lax.fori_loop(0, groups // 4, body, 0)

    def block_of(t):
        return g2b.at[pl.ds(t * groups, groups)]

    t_fo, t_ff = (1 - pc.y) * 2 + c_other, (1 - pc.y) * 2 + c_me
    t_no = pc.y * 2 + c_other
    sc_q = [scatter("q0", gq0_own, "zx"), scatter("q1", gq1_own, "zx")]

    def attn_grad(piece):
        for q in range(2):
            hq = wb[: nt * rows, q * part_w : (q + 1) * part_w]
            if piece == 0:
                g = dot_tn(hq, g1b[: nt * rows, :512])
                g = jnp.concatenate([g[:, :hw], g[:, 256 : 256 + hw]], axis=1)
            else:
                g = dot_tn(hq, g1b[: nt * rows, 512 : 512 + hw])
            own = (gq0_own, gq1_own)[piece]
            own[q * zblk : (q + 1) * zblk] = g.astype(BF).reshape(zblk, 2, r, g.shape[1])
        sc_q[piece].start()

    sums = project(t_fo, (none, none))
    cps.start(block_of(t_fo), dhr.at[0], dh_s.at[0], dh_r.at[0], core)
    sums = project(t_ff, sums)
    wait_recv(dhr.at[0], dh_s.at[0], dh_r.at[0], core)
    add_groups(t_ff, dhr.at[0])
    cps.start(block_of(t_ff), dhy, dh_s.at[2], dh_r.at[2], pc.rel(dy=1))
    attn_grad(0)
    sums = project(t_no, sums)
    cps.start(block_of(t_no), dhr.at[1], dh_s.at[1], dh_r.at[1], core)
    sum_h, sum_d = project(pc.t, sums)
    attn_grad(1)

    gain_one, shift_one = gains[0:1, :], gains[1:2, :]
    small_out[4:5, :hw] = sum_q
    small_out[5:6, :hw] = sum_k
    placed = pltpu.roll(small_out[...], pc.t * hw, 1)
    small_out[...] = placed
    small_out[0:1, :] = (sum_h - shift_one * sum_d) / gain_one
    small_out[1:2, :] = sum_d
    small_out[2:3, :] = sum_g2
    small_out[3:4, :] = sum_b2
    lane = iota((1, width), 1)
    stat = jnp.zeros((1, width), F32)
    counted = jnp.sum(slot_valid(pc.t, 0, rows))
    for i, v in enumerate((sum_x, sum_a, sum_m, sum_f)):
        stat = jnp.where(lane == i, jnp.sum(v), stat)
    small_out[6:7, :] = jnp.where(lane == 4, counted, stat)
    small_stages = [[dict(dc=1)], [dict(dy=1)], [dict(dx=1)], axis_steps(pc, "z")]
    total = small_out[...]

    def small_send(k, total):
        sm_src[k] = total
        for i, step in enumerate(small_stages[k]):
            cps.start(sm_src.at[k], sm_dst.at[k + i], st_s.at[k + i], st_r.at[k + i], pc.rel(**step))

    def small_add(k, total):
        for i, step in enumerate(small_stages[k]):
            wait_recv(sm_dst.at[k + i], st_s.at[k + i], st_r.at[k + i], pc.rel(**step))
            total = total + sm_dst[k + i]
        return total

    small_send(0, total)
    total = small_add(0, total)
    small_send(1, total)
    for s in sc_q:
        s.next()
    total = small_add(1, total)
    small_send(2, total)
    total = small_add(2, total)
    small_send(3, total)

    wait_recv(dhr.at[1], dh_s.at[1], dh_r.at[1], core)
    add_groups(pc.t, dhr.at[1])
    wait_recv(dhy, dh_s.at[2], dh_r.at[2], pc.rel(dy=1))

    def last(j, carry):
        at = pl.ds(pl.multiple_of(j * 128, 128), 128)
        near = g2b[pl.ds(pc.t * groups + j * 8, 8)].astype(F32)
        e = (near + dhy[pl.ds(j * 8, 8)].astype(F32)).reshape(128, width)
        x = tok[at, :].astype(F32)
        _, n, inv = layer_norm_rows(x, gain_one, 0.0)
        c = e * gain_one
        grad = inv * (
            c - jnp.mean(c, axis=-1, keepdims=True) - n * jnp.mean(c * n, axis=-1, keepdims=True)
        )
        dx_out[at, :] = dx_out[at, :] + grad
        return carry

    lax.fori_loop(0, rows // 128, last, 0)
    small_out[...] = small_add(3, total)

    def store(ref, at=None):
        def put(total):
            if at is None:
                ref[...] = total
            else:
                ref[:, at : at + cut] = total

        return put

    sc_q[0].finish(store(gqk_out))
    sc_q[1].finish(store(gv_out))
    sc_o.finish(store(gwo_out))
    sc_d0.finish(store(gwd_out, 0))
    sc_d1.finish(store(gwd_out, cut))
    sc_u0.finish(store(gwu_out, 0))
    sc_u1.finish(store(gwu_out, cut))

    def sent(j, carry):
        h2_copy(j, c_me).wait_send()
        back_copy(j, hs, hr, hh_s, hh_r).wait_send()
        back_copy(j, fs, fr_in, f_s, f_r).wait_send()
        return carry

    lax.fori_loop(0, 2, sent, 0)
    cps.finish()


def call_kc(nf, nt, lens, tok, cot, o_own, wo, wqkv, gains, lse, ob, qkv, h1, wu0, wu1, wd0, wd1):
    nz = nf // 2
    rows, width = tok.shape
    hw = ob.shape[1]
    r = width // nf
    cut = width // 2
    orders = dict(
        o=("c", "x", "y", "z"), u0=("x", "y", "z"), u1=("y", "x", "z"),
        d0=("x", "y", "z"), d1=("z", "x", "y"), q0=("x", "z"), q1=("x", "z"),
    )
    S = jax.ShapeDtypeStruct
    V = pltpu.VMEM
    vm = pl.BlockSpec(memory_space=pltpu.VMEM)
    hb = pl.BlockSpec(memory_space=pl.ANY)
    dma = pltpu.SemaphoreType.DMA
    g3 = (MARGIN + LP + 160) // 16
    outs = [
        S((rows, width), BF), S((rows, width), F32), S((r, 2 * hw), F32), S((r, hw), F32), S((r, hw), F32),
        S((r, width), F32), S((r, width), F32), S((8, width), F32),
    ]
    own = (2, nz, 2, r, cut)
    scratch = [
        V((LP, width), F32), V((LP, width), BF), V((g3, 16, width), BF), V((4 * width, width), BF),
        V((rows, 128), F32), V((2, rows, width), BF), V((2, rows, width), BF),
        V((rows, width), BF), V((rows, width), BF), V((2 * rows, width), BF),
        V((rows, width), BF), V((nt, rows // 16, 16, hw), BF),
        V(((nt * rows + 192) // 16, 16, hw), BF), V((LP, hw), BF), V((LP, 128), F32),
        V((2, rows // 16, 16, width), BF), V((rows // 16, 16, width), BF),
        V((nz, 2, r, 2 * hw), BF), V((nz, 2, r, hw), BF), V((4, 8, width), F32), V((2 + nz, 8, width), F32),
        V((2, 2, nz, 2, r, hw), BF), V(own, BF), V(own, BF), V(own, BF), V(own, BF),
        dma((2,)), dma((2,)), dma((1,)), dma((1,)), dma((2,)), dma((2,)), dma((2,)), dma((2,)),
        dma((3,)), dma((nt,)), dma((3,)), dma((3,)), dma((2 + nz,)), dma((2 + nz,)), dma((9,)),
    ]
    for name in ("o", "u0", "u1", "d0", "d1", "q0", "q1"):
        dims = {"o": "yczx", "q0": "zx", "q1": "zx"}.get(name, "yzx")
        block = (r, {"o": hw, "q0": 2 * hw, "q1": hw}.get(name, cut))
        scratch += [V(shape, BF) for shape in landing(nz, dims, orders[name], block)]
        n = sends_of(nz, orders[name])
        scratch += [dma((n,)), dma((n,))]
    return pl.pallas_call(
        functools.partial(kc_kernel, nf, nt, orders),
        out_shape=outs,
        in_specs=[pl.BlockSpec(memory_space=pltpu.SMEM), vm, hb] + [vm] * 6 + [hb] * 6,
        out_specs=[vm] * 8,
        scratch_shapes=scratch,
        compiler_params=pltpu.CompilerParams(
            collective_id=1, has_side_effects=True, vmem_limit_bytes=64 << 20
        ),
    )(lens, tok, cot, o_own, wo, wqkv, gains, lse, ob, qkv, h1, wu0, wu1, wd0, wd1)


def local_fused(nf, nt, args):
    (tokens, lengths, pictures, w_query, w_key, w_value, w_out, w_up, w_down) = args[:9]
    smalls, cotangent = args[9:15], args[15]
    rows, width = tokens.shape[1:]
    hw = w_query.shape[1]
    per = smalls[0].shape[0]
    place = lax.axis_index("fsdp") * nt + lax.axis_index("tp")
    prm = jnp.zeros((8, 128), jnp.float32).at[:6, :per].set(jnp.stack(smalls))
    attn = jnp.concatenate([w_query, w_key, w_value], axis=1)
    qkv, lse, ob, wqkv, gains, o_own, h1, wo, *halves = call_ka(
        nf, nt, lengths, tokens[0], attn, w_out.T, w_up, w_down.T, prm
    )
    result, grad_in, gqk, gv, gwo, gwu, gwd, small = call_kc(
        nf, nt, lengths, tokens[0], cotangent[0], o_own, wo.reshape(nt, width, hw), wqkv, gains, lse, ob,
        qkv, h1.reshape(nt * rows, width),
        *[w.reshape(2, width, width // 2) for w in halves],
    )
    own = lax.dynamic_slice_in_dim(small, place * per, per, 1)
    statistics = jnp.sqrt(small[6, :4] / (small[6, 4] * width))
    return (
        result[None], grad_in[None],
        gqk[:, :hw], gqk[:, hw:], gv, gwo.T, gwu, gwd.T,
        own[0], own[1], own[2], own[3], own[4], own[5], statistics,
    )


def solution(mesh):
    nf, nt = mesh.shape["fsdp"], mesh.shape["tp"]

    def local(*args):
        tokens, w_query = args[0], args[3]
        if nt == 4 and tokens.shape[0] == 1 and tokens.shape[1] == 512 and w_query.shape[0] % 32 == 0:
            return local_fused(nf, nt, args)
        return local_plain(*args)

    in_specs = (
        P("fsdp", "tp", None),
        P("fsdp", None),
        P("fsdp", None),
        P("fsdp", "tp"),
        P("fsdp", "tp"),
        P("fsdp", "tp"),
        P("tp", "fsdp"),
        P("fsdp", "tp"),
        P("tp", "fsdp"),
        P(("fsdp", "tp")),
        P(("fsdp", "tp")),
        P(("fsdp", "tp")),
        P(("fsdp", "tp")),
        P(("fsdp", "tp")),
        P(("fsdp", "tp")),
        P("fsdp", "tp", None),
    )
    out_specs = (
        P("fsdp", "tp", None),
        P("fsdp", "tp", None),
        P("fsdp", "tp"),
        P("fsdp", "tp"),
        P("fsdp", "tp"),
        P("tp", "fsdp"),
        P("fsdp", "tp"),
        P("tp", "fsdp"),
        P(("fsdp", "tp")),
        P(("fsdp", "tp")),
        P(("fsdp", "tp")),
        P(("fsdp", "tp")),
        P(("fsdp", "tp")),
        P(("fsdp", "tp")),
        P(),
    )
    return jax.shard_map(local, mesh=mesh, in_specs=in_specs, out_specs=out_specs, check_vma=False)
```

```python
import functools

import jax
import jax.numpy as jnp
from jax import lax
from jax.experimental import pallas as pl
from jax.experimental.pallas import tpu as pltpu
from jax.sharding import PartitionSpec as P

HD = 64


EPS = 1e-06
ROOT_HALF = 0.7071067811865476
DENSITY = 0.3989422804014327


def normalise(values, scaling, offset):
    centre = jnp.mean(values, axis=-1, keepdims=True)
    centred = values - centre
    spread = jnp.mean(centred * centred, axis=-1, keepdims=True)
    inverse = lax.rsqrt(spread + EPS)
    normed = centred * inverse
    return (normed * scaling + offset, normed, inverse)


def normalise_back(grad_out, normed, inverse, scaling):
    grad_unit = grad_out * scaling
    grad_values = inverse * (
        grad_unit
        - jnp.mean(grad_unit, axis=-1, keepdims=True)
        - normed * jnp.mean(grad_unit * normed, axis=-1, keepdims=True)
    )
    return (grad_values, jnp.sum(grad_out * normed, axis=(0, 1)), jnp.sum(grad_out, axis=(0, 1)))


def gelu_slope(values):
    return (
        0.5 * (1.0 + jax.scipy.special.erf(values * ROOT_HALF))
        + values * jnp.exp(-0.5 * values * values) * DENSITY
    )


def gather_tokens(values):
    return lax.all_gather(values, "tp", axis=1, tiled=True)


def gather_grads(values):
    return lax.all_gather(values, "tp", axis=1, tiled=True)


def reduce_tokens(values):
    return lax.psum_scatter(
        values.astype(jnp.bfloat16), "tp", scatter_dimension=1, tiled=True
    ).astype(jnp.float32)


def reduce_grads(values):
    return lax.psum_scatter(
        values.astype(jnp.bfloat16), "tp", scatter_dimension=1, tiled=True
    ).astype(jnp.float32)


def block_scores(query, keyed, picture_query, picture_key, key_mask):
    raw_scores = jnp.einsum("qhd,khd->hqk", query, keyed, preferred_element_type=jnp.float32)
    allowed = (picture_query[:, None] == picture_key[None, :]) & (key_mask[None, :] > 0)
    return jnp.where(allowed[None], raw_scores * query.shape[-1] ** (-0.5), -1e30)


def forward_row(packed):
    query_row, key_row, value_row, picture_row, mask_row = packed
    full_len = query_row.shape[0]
    block_len = min(512, full_len)
    block_count = full_len // block_len

    def forward_one_block(packed_block):
        query_block, picture_block = packed_block
        scores = block_scores(query_block, key_row, picture_block, picture_row, mask_row)
        highest = jnp.max(scores, axis=-1, keepdims=True)
        logsum = highest + jnp.log(jnp.sum(jnp.exp(scores - highest), axis=-1, keepdims=True))
        probability = jnp.exp(scores - logsum).astype(jnp.bfloat16)
        mixture = jnp.einsum(
            "hqk,khd->qhd", probability, value_row, preferred_element_type=jnp.float32
        )
        return (mixture, logsum)

    query_blocks = query_row.reshape((block_count, block_len) + query_row.shape[1:])
    return lax.map(forward_one_block, (query_blocks, picture_row.reshape(block_count, block_len)))


def backward_row(packed):
    query_row, key_row, value_row, picture_row, mask_row, grad_row, logsum_row = packed
    full_len = query_row.shape[0]
    block_len = min(512, full_len)
    block_count = full_len // block_len
    factor = query_row.shape[-1] ** (-0.5)

    def backward_one_block(running, packed_block):
        grad_key, grad_value = running
        query_block, picture_block, grad_block, logsum_block = packed_block
        scores = block_scores(query_block, key_row, picture_block, picture_row, mask_row)
        probability = jnp.exp(scores - logsum_block)
        prob_low = probability.astype(jnp.bfloat16)
        grad_prob = jnp.einsum(
            "qhd,khd->hqk", grad_block, value_row, preferred_element_type=jnp.float32
        )
        grad_value = grad_value + jnp.einsum(
            "hqk,qhd->khd", prob_low, grad_block, preferred_element_type=jnp.float32
        )
        centre = jnp.sum(probability * grad_prob, axis=-1, keepdims=True)
        grad_scores = (probability * (grad_prob - centre)).astype(jnp.bfloat16)
        grad_query = factor * jnp.einsum(
            "hqk,khd->qhd", grad_scores, key_row, preferred_element_type=jnp.float32
        )
        grad_key = grad_key + factor * jnp.einsum(
            "hqk,qhd->khd", grad_scores, query_block, preferred_element_type=jnp.float32
        )
        return ((grad_key, grad_value), grad_query)

    zero_state = jnp.zeros(key_row.shape, jnp.float32)
    block_shape = (block_count, block_len) + query_row.shape[1:]
    (grad_key, grad_value), grad_query = lax.scan(
        backward_one_block,
        (zero_state, zero_state),
        (
            query_row.reshape(block_shape),
            picture_row.reshape(block_count, block_len),
            grad_row.reshape(block_shape),
            logsum_row,
        ),
    )
    return (grad_query.reshape(key_row.shape), grad_key, grad_value)


def local_plain(
    tokens,
    lengths,
    pictures,
    w_query,
    w_key,
    w_value,
    w_out,
    w_up,
    w_down,
    norm1_gain,
    norm1_shift,
    norm2_gain,
    norm2_shift,
    query_gain,
    key_gain,
    cotangent,
):
    tp_place = lax.axis_index("tp")
    local_len = tokens.shape[1]
    model_width = tokens.shape[2]
    full_len = pictures.shape[1]
    local_width = w_query.shape[1]
    heads_local = local_width // HD
    gain_one, shift_one, gain_two, shift_two, gain_query, gain_key = (
        lax.all_gather(norm1_gain, ("fsdp", "tp"), axis=0, tiled=True),
        lax.all_gather(norm1_shift, ("fsdp", "tp"), axis=0, tiled=True),
        lax.all_gather(norm2_gain, ("fsdp", "tp"), axis=0, tiled=True),
        lax.all_gather(norm2_shift, ("fsdp", "tp"), axis=0, tiled=True),
        lax.all_gather(query_gain, ("fsdp", "tp"), axis=0, tiled=True),
        lax.all_gather(key_gain, ("fsdp", "tp"), axis=0, tiled=True),
    )
    positions = jnp.arange(full_len, dtype=jnp.int32)
    valid_full = (positions[None, :] < jnp.sum(lengths, axis=1)[:, None]).astype(jnp.float32)
    valid_here = lax.dynamic_slice_in_dim(valid_full, tp_place * local_len, local_len, 1)[
        :, :, None
    ]
    qgain_here = lax.dynamic_slice_in_dim(
        gain_query, tp_place * local_width, local_width, 0
    ).reshape(heads_local, HD)
    kgain_here = lax.dynamic_slice_in_dim(gain_key, tp_place * local_width, local_width, 0).reshape(
        heads_local, HD
    )
    front_query, front_key, front_value, front_out = (
        lax.all_gather(w_query, "fsdp", axis=0, tiled=True),
        lax.all_gather(w_key, "fsdp", axis=0, tiled=True),
        lax.all_gather(w_value, "fsdp", axis=0, tiled=True),
        lax.all_gather(w_out, "fsdp", axis=1, tiled=True),
    )
    inputs = tokens.astype(jnp.float32)
    hidden, normed_one, inverse_one = normalise(inputs, gain_one, shift_one)
    hidden_full = gather_tokens(hidden.astype(jnp.bfloat16))
    row_shape = hidden_full.shape[:2] + (heads_local, HD)
    query = jnp.dot(hidden_full, front_query, preferred_element_type=jnp.float32).reshape(row_shape)
    keyed = jnp.dot(hidden_full, front_key, preferred_element_type=jnp.float32).reshape(row_shape)
    value_low = (
        jnp.dot(hidden_full, front_value, preferred_element_type=jnp.float32)
        .astype(jnp.bfloat16)
        .reshape(row_shape)
    )
    query_norm, query_unit, query_inverse = normalise(query, qgain_here, 0.0)
    key_norm, key_unit, key_inverse = normalise(keyed, kgain_here, 0.0)
    query_low = query_norm.astype(jnp.bfloat16)
    key_low = key_norm.astype(jnp.bfloat16)
    mixture, logsum = lax.map(forward_row, (query_low, key_low, value_low, pictures, valid_full))
    mixture_low = mixture.reshape(hidden_full.shape[:2] + (local_width,)).astype(jnp.bfloat16)
    attn_branch = valid_here * reduce_tokens(
        jnp.dot(mixture_low, front_out, preferred_element_type=jnp.float32)
    )
    middle = inputs + attn_branch
    hidden_two, normed_two, inverse_two = normalise(middle, gain_two, shift_two)
    hidden_two_full = gather_tokens(hidden_two.astype(jnp.bfloat16))
    front_up, front_down = (
        lax.all_gather(w_up, "fsdp", axis=0, tiled=True),
        lax.all_gather(w_down, "fsdp", axis=1, tiled=True),
    )
    up_value = jnp.dot(hidden_two_full, front_up, preferred_element_type=jnp.float32)
    activated = jax.nn.gelu(up_value, approximate=False).astype(jnp.bfloat16)
    mlp_branch = valid_here * reduce_tokens(
        jnp.dot(activated, front_down, preferred_element_type=jnp.float32)
    )
    result = (middle + mlp_branch).astype(jnp.bfloat16)
    square_sums = jnp.stack(
        [
            jnp.sum(valid_here * inputs * inputs),
            jnp.sum(attn_branch * attn_branch),
            jnp.sum(valid_here * middle * middle),
            jnp.sum(mlp_branch * mlp_branch),
        ]
    )
    valid_count = jnp.sum(valid_here)
    back_up, back_down = (
        lax.all_gather(w_up, "fsdp", axis=0, tiled=True),
        lax.all_gather(w_down, "fsdp", axis=1, tiled=True),
    )
    back_query, back_key, back_value, back_out = (
        lax.all_gather(w_query, "fsdp", axis=0, tiled=True),
        lax.all_gather(w_key, "fsdp", axis=0, tiled=True),
        lax.all_gather(w_value, "fsdp", axis=0, tiled=True),
        lax.all_gather(w_out, "fsdp", axis=1, tiled=True),
    )
    grad_y = cotangent.astype(jnp.float32) * valid_here
    grad_y_full = gather_grads(grad_y.astype(jnp.bfloat16))
    grad_down = jnp.einsum(
        "rlf,rld->fd", activated, grad_y_full, preferred_element_type=jnp.float32
    )
    grad_act = jnp.dot(grad_y_full, back_down.T, preferred_element_type=jnp.float32)
    grad_pre = (grad_act * gelu_slope(up_value)).astype(jnp.bfloat16)
    grad_up = jnp.einsum(
        "rld,rlf->df", hidden_two_full, grad_pre, preferred_element_type=jnp.float32
    )
    grad_hidden_two = reduce_grads(jnp.dot(grad_pre, back_up.T, preferred_element_type=jnp.float32))
    mlp_grads = (
        lax.psum_scatter(grad_up, "fsdp", scatter_dimension=0, tiled=True),
        lax.psum_scatter(grad_down, "fsdp", scatter_dimension=1, tiled=True),
    )
    grad_mid_norm, grad_gain_two, grad_shift_two = normalise_back(
        grad_hidden_two, normed_two, inverse_two, gain_two
    )
    grad_middle = grad_y + grad_mid_norm
    grad_branch_here = (valid_here * grad_middle).astype(jnp.bfloat16)
    grad_branch_full = gather_grads(grad_branch_here)
    grad_out_proj = jnp.einsum(
        "rlh,rld->hd", mixture_low, grad_branch_full, preferred_element_type=jnp.float32
    )
    grad_mixture = jnp.dot(grad_branch_full, back_out.T, preferred_element_type=jnp.float32).astype(
        jnp.bfloat16
    )
    grad_qnorm, grad_knorm, grad_value_full = lax.map(
        backward_row,
        (
            query_low,
            key_low,
            value_low,
            pictures,
            valid_full,
            grad_mixture.reshape(row_shape),
            logsum,
        ),
    )
    grad_query_pre, grad_qgain, unused_one = normalise_back(
        grad_qnorm, query_unit, query_inverse, qgain_here
    )
    grad_key_pre, grad_kgain, unused_two = normalise_back(
        grad_knorm, key_unit, key_inverse, kgain_here
    )
    flat_shape = hidden_full.shape[:2] + (local_width,)
    grad_query_low = grad_query_pre.reshape(flat_shape).astype(jnp.bfloat16)
    grad_key_low = grad_key_pre.reshape(flat_shape).astype(jnp.bfloat16)
    grad_value_low = grad_value_full.reshape(flat_shape).astype(jnp.bfloat16)
    grad_wquery = jnp.einsum(
        "rld,rlh->dh", hidden_full, grad_query_low, preferred_element_type=jnp.float32
    )
    grad_wkey = jnp.einsum(
        "rld,rlh->dh", hidden_full, grad_key_low, preferred_element_type=jnp.float32
    )
    grad_wvalue = jnp.einsum(
        "rld,rlh->dh", hidden_full, grad_value_low, preferred_element_type=jnp.float32
    )
    grad_hidden_part = (
        jnp.dot(grad_query_low, back_query.T, preferred_element_type=jnp.float32)
        + jnp.dot(grad_key_low, back_key.T, preferred_element_type=jnp.float32)
        + jnp.dot(grad_value_low, back_value.T, preferred_element_type=jnp.float32)
    )
    grad_hidden = reduce_grads(grad_hidden_part)
    attn_grads = (
        lax.psum_scatter(grad_wquery, "fsdp", scatter_dimension=0, tiled=True),
        lax.psum_scatter(grad_wkey, "fsdp", scatter_dimension=0, tiled=True),
        lax.psum_scatter(grad_wvalue, "fsdp", scatter_dimension=0, tiled=True),
        lax.psum_scatter(grad_out_proj, "fsdp", scatter_dimension=1, tiled=True),
    )
    grad_in_norm, grad_gain_one, grad_shift_one = normalise_back(
        grad_hidden, normed_one, inverse_one, gain_one
    )
    grad_inputs = grad_middle + grad_in_norm
    zero_width = jnp.zeros((model_width,), jnp.float32)
    grad_qgain_full = lax.dynamic_update_slice_in_dim(
        zero_width, grad_qgain.reshape(local_width), tp_place * local_width, 0
    )
    grad_kgain_full = lax.dynamic_update_slice_in_dim(
        zero_width, grad_kgain.reshape(local_width), tp_place * local_width, 0
    )
    small_shards = (
        lax.psum_scatter(grad_gain_one, ("fsdp", "tp"), scatter_dimension=0, tiled=True),
        lax.psum_scatter(grad_shift_one, ("fsdp", "tp"), scatter_dimension=0, tiled=True),
        lax.psum_scatter(grad_gain_two, ("fsdp", "tp"), scatter_dimension=0, tiled=True),
        lax.psum_scatter(grad_shift_two, ("fsdp", "tp"), scatter_dimension=0, tiled=True),
        lax.psum_scatter(grad_qgain_full, ("fsdp", "tp"), scatter_dimension=0, tiled=True),
        lax.psum_scatter(grad_kgain_full, ("fsdp", "tp"), scatter_dimension=0, tiled=True),
    )
    totals, counted = lax.psum((square_sums, valid_count), ("fsdp", "tp"))
    statistics = jnp.sqrt(totals / (counted * model_width))
    return (
        result,
        grad_inputs,
        attn_grads[0],
        attn_grads[1],
        attn_grads[2],
        attn_grads[3],
        mlp_grads[0],
        mlp_grads[1],
        small_shards[0],
        small_shards[1],
        small_shards[2],
        small_shards[3],
        small_shards[4],
        small_shards[5],
        statistics,
    )


BIG = 1024
SMALL = 448
LP = BIG + 3 * SMALL
MARGIN = 128
EXP_SCALE = 0.125 * 1.4426950408889634
MESH = pl.DeviceIdType.MESH
BF = jnp.bfloat16
F32 = jnp.float32


def dot_nn(a, b):
    return lax.dot_general(a, b, (((1,), (0,)), ((), ())), preferred_element_type=F32)


def dot_nt(a, b):
    return lax.dot_general(a, b, (((1,), (1,)), ((), ())), preferred_element_type=F32)


def dot_tn(a, b):
    return lax.dot_general(a, b, (((0,), (0,)), ((), ())), preferred_element_type=F32)


def iota(shape, dim):
    return lax.broadcasted_iota(jnp.int32, shape, dim)


def head_mask(rows, width, h):
    lane = iota((rows, width), 1)
    return (lane >= h * HD) & (lane < (h + 1) * HD)


def segment_matrix(width):
    r = iota((width, width), 0) // HD
    c = iota((width, width), 1) // HD
    return jnp.where(r == c, 1.0 / HD, 0.0).astype(BF)


def segment_mean(x, seg):
    return dot_nn(x.astype(BF), seg)


class Place:
    def __init__(self, nf, nt):
        self.nf, self.nt = nf, nt
        self.nx = 2
        self.nz = nf // 2
        f = lax.axis_index("fsdp")
        t = lax.axis_index("tp")
        self.f, self.t = f, t
        self.z, self.x = f // 2, lax.rem(f, 2)
        self.y, self.c = t // 2, lax.rem(t, 2)
        self.me = f * nt + t

    def rel(self, dz=0, dx=0, dy=0, dc=0):
        z = lax.rem(self.z + dz, self.nz) if dz else self.z
        x = 1 - self.x if dx else self.x
        y = 1 - self.y if dy else self.y
        c = 1 - self.c if dc else self.c
        return (z * 2 + x, y * 2 + c)


class Copies:
    def __init__(self):
        self.sent = []

    def start(self, src, dst, send_sem, recv_sem, dev):
        cp = pltpu.make_async_remote_copy(
            src_ref=src,
            dst_ref=dst,
            send_sem=send_sem,
            recv_sem=recv_sem,
            device_id=dev,
            device_id_type=MESH,
        )
        cp.start()
        self.sent.append(cp)

    def finish(self):
        for cp in self.sent:
            cp.wait_send()
        self.sent = []


def wait_recv(dst, send_sem, recv_sem, dev):
    pltpu.make_async_remote_copy(
        src_ref=dst,
        dst_ref=dst,
        send_sem=send_sem,
        recv_sem=recv_sem,
        device_id=dev,
        device_id_type=MESH,
    ).wait_recv()


def barrier_peers(pc):
    steps = [dict(dz=i) for i in range(1, pc.nz)]
    steps += [dict(dx=1), dict(dy=1), dict(dc=1), dict(dy=1, dc=1)]
    bar = pltpu.get_barrier_semaphore()
    for step in steps:
        pl.semaphore_signal(bar, inc=1, device_id=pc.rel(**step), device_id_type=MESH)
    pl.semaphore_wait(bar, len(steps))


def axis_steps(pc, axis):
    if axis == "z":
        return [dict(dz=i) for i in range(1, pc.nz)]
    return [{"d" + axis: 1}]


def sends_of(nz, order):
    return sum(nz - 1 if axis == "z" else 1 for axis in order)


class Gather:
    def __init__(self, pc, copies, src, dst, send, recv, dims, order):
        self.pc, self.copies = pc, copies
        self.src, self.dst, self.send_sem, self.recv_sem = src, dst, send, recv
        self.dims, self.order = dims, order
        self.stages = []
        count = 0
        for axis in order:
            steps = axis_steps(pc, axis)
            self.stages.append([(count + i, step) for i, step in enumerate(steps)])
            count += len(steps)

    def index(self, stage, at=None):
        place = at or dict(z=self.pc.z, x=self.pc.x, y=self.pc.y, c=self.pc.c)
        done = self.order[:stage]
        return tuple(slice(None) if d in done else place[d] for d in self.dims)

    def keep(self, sem):
        self.local = pltpu.make_async_copy(self.src, self.dst.at[self.index(0)], sem)
        self.local.start()

    def send(self, k):
        if k == 1:
            self.local.wait()
        idx = self.index(k)
        src = self.src if k == 0 else self.dst.at[idx]
        for n, step in self.stages[k]:
            self.copies.start(
                src, self.dst.at[idx], self.send_sem.at[n], self.recv_sem.at[n], self.pc.rel(**step)
            )

    def wait(self, k):
        pc = self.pc
        for n, step in self.stages[k]:
            at = dict(z=pc.z, x=pc.x, y=pc.y, c=pc.c)
            if "dz" in step:
                at["z"] = lax.rem(pc.z + pc.nz - step["dz"], pc.nz)
            else:
                axis = self.order[k]
                at[axis] = 1 - at[axis]
            dst = self.dst.at[self.index(k, at)]
            wait_recv(dst, self.send_sem.at[n], self.recv_sem.at[n], pc.rel(**step))


def slots_of(lens_ref):
    lens = [lens_ref[0, p] for p in range(4)]
    starts = [0]
    for p in range(3):
        starts.append(starts[-1] + lens[p])
    big = 0
    for p in range(1, 4):
        big = jnp.where(lens[p] == BIG, p, big)
    sb = 0
    for p in range(1, 4):
        sb = jnp.where(big == p, starts[p], sb)
    out = [(sb, BIG)]
    for k in range(3):
        s = jnp.where(big <= k, starts[k + 1], starts[k])
        n = jnp.where(big <= k, lens[k + 1], lens[k])
        out.append((s, n))
    return out


def small_length(lens, k):
    slots = slots_of(lens)
    return jnp.where(k == 0, slots[1][1], jnp.where(k == 1, slots[2][1], slots[3][1]))


BASES = (0, BIG, BIG + SMALL, BIG + 2 * SMALL)


def shift_matrix(rows, cols, r):
    return jnp.where(iota((rows, cols), 1) == iota((rows, cols), 0) + r, 1.0, 0.0).astype(BF)


def load_rows(src, first, count):
    return jnp.concatenate([src[first + m] for m in range(count)], axis=0)


def pack_rows(src, dst, lens, masked=False):
    def big(j, carry):
        s = slots_of(lens)[0][0]
        r = lax.rem(s, 16)
        d = shift_matrix(128, 144, r)
        out = dot_nn(d, load_rows(src, s // 16 + j * 8, 9)).astype(BF)
        dst[pl.ds(pl.multiple_of(j * 128, 128), 128), :] = out
        return carry

    lax.fori_loop(0, BIG // 128, big, 0)

    for k in range(3):

        def small(j, carry, k=k):
            s, n = slots_of(lens)[1 + k]
            r = lax.rem(s, 16)
            d = shift_matrix(112, 128, r)
            out = dot_nn(d, load_rows(src, s // 16 + j * 7, 8))
            if masked:
                out = jnp.where(iota(out.shape, 0) + j * 112 < n, out, 0.0)
            out = out.astype(BF)
            dst[pl.ds(pl.multiple_of(BASES[1 + k] + j * 112, 16), 112), :] = out
            return carry

        lax.fori_loop(0, 4, small, 0)


def unpack_tile(src, i0, lens):
    wa, ea, wb, sb = 0, 0, 0, 4096
    for (s, n), base in zip(slots_of(lens), BASES):
        inside = (s <= i0) & (i0 < s + n)
        begins = (s > i0) & (s <= i0 + 127)
        w = base + i0 - s + MARGIN
        wa = jnp.where(inside, w, wa)
        ea = jnp.where(inside, s + n - i0, ea)
        wb = jnp.where(begins, w, wb)
        sb = jnp.where(begins, s - i0, sb)
    out = None
    row = iota((128, 144), 0)
    col = iota((128, 144), 1)
    for w, ok in ((wa, lambda: row < ea), (wb, lambda: row >= sb)):
        r = lax.rem(w, 16)
        d = jnp.where((col == row + r) & ok(), 1.0, 0.0).astype(BF)
        part = dot_nn(d, load_rows(src, w // 16, 9))
        out = part if out is None else out + part
    return out


def layer_norm_rows(x, g, b):
    mean = jnp.mean(x, axis=-1, keepdims=True)
    xc = x - mean
    var = jnp.mean(xc * xc, axis=-1, keepdims=True)
    inv = lax.rsqrt(var + EPS)
    n = xc * inv
    return n * g + b, n, inv


def own_heads(row, t, nt, width):
    out = row[:, :width]
    for k in range(1, nt):
        out = jnp.where(t == k, row[:, k * width : (k + 1) * width], out)
    return out


def build_gains(tiles, gains, per):
    chunks = len(tiles) * per // 128
    lane = iota((8, 128), 1)
    acc = [jnp.zeros((8, 128), F32) for _ in range(chunks)]
    for d, tile in enumerate(tiles):
        j, a = divmod(d * per, 128)
        if a:
            tile = pltpu.roll(tile, a, 1)
        acc[j] = jnp.where((lane >= a) & (lane < a + per), tile, acc[j])
        if a + per > 128:
            acc[j + 1] = jnp.where(lane < a + per - 128, tile, acc[j + 1])
    for j in range(chunks):
        gains[:, j * 128 : (j + 1) * 128] = acc[j]


def ka_kernel(
    nf, nt, orders,
    lens, tok, wq, wk, wv, wo_in, wu, wd, s0, s1, s2, s3, s4, s5,
    qkv_out, lse_out, ob_out, wqkv, gains, o_own, h1_out, wo_all, wu0_all, wu1_all, wd0_all, wd1_all,
    wa, wo, prm, qkv, lse, ob, tok_all, h1t, h1p, wa_all, prm_all, of, op, osend,
    prm_s, prm_r, tok_s, tok_r, wa_s, wa_r, wo_s, wo_r,
    u0_s, u0_r, u1_s, u1_r, d0_s, d0_r, d1_s, d1_r, o_s, o_r, loc,
):
    pc = Place(nf, nt)
    cps = Copies()
    rows, width = tok.shape
    hw = ob.shape[1]
    cut = width // 2
    wa[...] = jnp.concatenate([wq[...], wk[...], wv[...]], axis=1)
    wo[...] = wo_in[...].T
    prm[...] = jnp.zeros(prm.shape, F32)
    for i, small in enumerate((s0, s1, s2, s3, s4, s5)):
        prm[i : i + 1, : small.shape[1]] = small[...]
    gp = Gather(pc, cps, prm, prm_all, prm_s, prm_r, "zxyc", orders["prm"])
    ga = Gather(pc, cps, wa, wa_all, wa_s, wa_r, "zx", orders["wa"])
    go = Gather(pc, cps, wo, wo_all, wo_s, wo_r, "yczx", orders["wo"])
    gu0 = Gather(pc, cps, wu.at[:, :cut], wu0_all, u0_s, u0_r, "yzx", orders["u0"])
    gu1 = Gather(pc, cps, wu.at[:, cut:], wu1_all, u1_s, u1_r, "yzx", orders["u1"])
    gd0 = Gather(pc, cps, wd.at[:, :cut], wd0_all, d0_s, d0_r, "yzx", orders["d0"])
    gd1 = Gather(pc, cps, wd.at[:, cut:], wd1_all, d1_s, d1_r, "yzx", orders["d1"])
    for i, g in enumerate((gp, ga, go, gd1, gu0, gd0, gu1)):
        g.keep(loc.at[i])
    barrier_peers(pc)

    cps.start(tok, tok_all.at[pc.t], tok_s.at[1], tok_r.at[pc.t], pc.rel(dc=1))
    gp.send(0)
    ga.send(0)
    gd1.send(0)
    cps.start(tok, tok_all.at[pc.t], tok_s.at[0], tok_r.at[pc.t], pc.rel(dy=1))
    h1t[4 * rows // 16 :] = jnp.zeros((h1t.shape[0] - 4 * rows // 16, 16, width), BF)
    for k in range(4):
        gp.wait(k)
        if k < 3:
            gp.send(k + 1)
    gd1.wait(0)
    gd1.send(1)
    go.send(0)
    tiles = []
    for d in range(nf * nt):
        f, t = divmod(d, nt)
        tiles.append(prm_all[f // 2, f % 2, t // 2, t % 2])
    build_gains(tiles, gains, width // (nf * nt))
    gain_one, shift_one = gains[0:1, :], gains[1:2, :]

    def norm_block(t, block):
        def body(j, carry):
            at = pl.ds(pl.multiple_of(j * 128, 128), 128)
            out, _, _ = layer_norm_rows(block[at, :].astype(F32), gain_one, shift_one)
            h1t[pl.ds(t * (rows // 16) + j * 8, 8)] = out.astype(BF).reshape(8, 16, width)
            return carry

        lax.fori_loop(0, rows // 128, body, 0)

    def wait_tok(t):
        wait_recv(tok_all.at[t], tok_s.at[0], tok_r.at[t], pc.rel(dc=1))

    norm_block(pc.t, tok)
    t_core, t_y, t_diag = pc.rel(dc=1)[1], pc.rel(dy=1)[1], pc.rel(dy=1, dc=1)[1]
    wait_tok(t_core)
    norm_block(t_core, tok_all.at[t_core])
    ga.wait(0)
    ga.send(1)
    gu0.send(0)
    gd0.send(0)
    wait_tok(t_y)
    cps.start(tok_all.at[t_y], tok_all.at[t_y], tok_s.at[2], tok_r.at[t_y], pc.rel(dc=1))
    norm_block(t_y, tok_all.at[t_y])
    wait_tok(t_diag)
    norm_block(t_diag, tok_all.at[t_diag])
    h1_copy = pltpu.make_async_copy(h1t.at[: 4 * rows // 16], h1_out, loc.at[0])
    h1_copy.start()

    pack_rows(h1t, h1p, lens)
    go.wait(0)
    go.send(1)
    gu0.wait(0)
    gu0.send(1)
    gd0.wait(0)
    gd0.send(1)
    gu1.send(0)
    gd1.wait(1)
    ga.wait(1)
    seg = segment_matrix(hw)
    gq = own_heads(gains[4:5, :], pc.t, nt, hw)
    gk = own_heads(gains[5:6, :], pc.t, nt, hw)
    w_full = wa_all[...].reshape(width, 3 * hw)
    for i in range(3):
        wqkv[i] = w_full[:, i * hw : (i + 1) * hw]

    qt = LP // 4

    def project(j, carry):
        at = pl.ds(pl.multiple_of(j * qt, 16), qt)
        h = h1p[at, :]
        lane = iota((qt, 128), 1)
        kept = jnp.zeros((qt, 128), F32)
        for i, g in enumerate((gq, gk)):
            q = dot_nn(h, wqkv[i])
            qc = q - segment_mean(q, seg)
            inv = lax.rsqrt(segment_mean(qc * qc, seg) + EPS)
            qkv[at, i * 256 : i * 256 + hw] = (qc * inv * g).astype(BF)
            for k in range(hw // HD):
                kept = jnp.where(lane == 8 * (i + 1) + k, inv[:, k * HD : k * HD + 1], kept)
        lse[at, :] = kept
        qkv[at, 512 : 512 + hw] = dot_nn(h, wqkv[2]).astype(BF)
        return carry

    lax.fori_loop(0, 4, project, 0)
    qkv[:, 512 + hw :] = jnp.ones((LP, 256 - hw), BF)
    saves = [h1_copy, pltpu.make_async_copy(qkv, qkv_out, loc.at[2])]
    saves[-1].start()
    head, tail = MARGIN // 16, (MARGIN + LP) // 16
    op[:head] = jnp.zeros((head, 16, hw), BF)
    op[tail:] = jnp.zeros((op.shape[0] - tail, 16, hw), BF)

    gu0.wait(1)
    gu0.send(2)
    gu1.wait(0)
    gu1.send(1)
    gd0.wait(1)
    gd0.send(2)
    go.wait(1)
    go.send(2)
    gd1.send(2)

    def attend(at, keys, h, limit):
        nrow = at.size
        q = jnp.where(head_mask(nrow, hw, h), qkv[at, :hw], jnp.zeros((), BF))
        s = dot_nt(q, qkv[keys, 256 : 256 + hw])
        p = jnp.exp2(s * EXP_SCALE)
        if limit is not None:
            p = jnp.where(iota(p.shape, 1) < limit, p, 0.0)
        oa = dot_nn(p.astype(BF), qkv[keys, 512:768])
        total = oa[:, hw : hw + 1]
        o = oa[:, :hw] * (1.0 / total)
        l2 = jnp.log2(total)
        lane = iota((nrow, 128), 1)
        if h == 0:
            of[at, :] = o
        else:
            of[at, :] = jnp.where(head_mask(nrow, hw, h), o, of[at, :])
        lse[at, :] = jnp.where(lane == h, l2, lse[at, :])

    nh = hw // HD
    for h in range(nh):
        def big(j, carry, h=h):
            attend(pl.ds(pl.multiple_of(j * 512, 512), 512), pl.ds(0, BIG), h, None)
            return carry

        lax.fori_loop(0, BIG // 512, big, 0)

        def small(k, carry, h=h):
            at = pl.ds(pl.multiple_of(BIG + k * SMALL, 16), SMALL)
            attend(at, at, h, small_length(lens, k))
            return carry

        lax.fori_loop(0, 3, small, 0)
        if h == 1:
            gu1.wait(1)
            gu1.send(2)
        elif h == 2:
            go.wait(2)
            go.send(3)

    ob[...] = of[...].astype(BF)
    for i, (src, dst) in enumerate(((lse, lse_out), (ob, ob_out))):
        saves.append(pltpu.make_async_copy(src, dst, loc.at[3 + i]))
        saves[-1].start()
    op[head:tail] = ob[...].reshape(LP // 16, 16, hw)

    def unpack_block(t):
        def unpack(i, carry):
            out = unpack_tile(op, t * rows + i * 128, lens)
            osend[t, pl.ds(pl.multiple_of(i * 128, 128), 128), :] = out.astype(BF)
            return carry

        lax.fori_loop(0, rows // 128, unpack, 0)

    peers = [pc.rel(dy=1, dc=1), pc.rel(dy=1), pc.rel(dc=1)]
    for i, dev in enumerate(peers):
        unpack_block(dev[1])
        cps.start(osend.at[dev[1]], o_own.at[pc.t], o_s.at[i], o_r.at[pc.t], dev)
    unpack_block(pc.t)
    cp = pltpu.make_async_copy(osend.at[pc.t], o_own.at[pc.t], loc.at[1])
    cp.start()
    cp.wait()
    for cp in saves:
        cp.wait()
    go.wait(3)
    for g in (gu0, gd0, gu1, gd1):
        g.wait(2)
    for dev in peers:
        wait_recv(o_own.at[dev[1]], o_s.at[0], o_r.at[dev[1]], dev)
    cps.finish()


def call_ka(nf, nt, lens, tok, wq, wk, wv, wo, wu, wd, smalls):
    nz = nf // 2
    rows, width = tok.shape
    r, hw = wq.shape
    cut = width // 2
    orders = dict(
        prm=("z", "x", "y", "c"), wa=("z", "x"), wo=("z", "y", "x", "c"),
        u0=("z", "y", "x"), d0=("z", "x", "y"), u1=("z", "y", "x"), d1=("y", "x", "z"),
    )
    S = jax.ShapeDtypeStruct
    V = pltpu.VMEM
    vm = pl.BlockSpec(memory_space=pltpu.VMEM)
    hb = pl.BlockSpec(memory_space=pl.ANY)
    half = (S((2, nz, 2, r, cut), BF), hb)
    outs = [
        (S((LP, 768), BF), hb), (S((LP, 128), F32), hb), (S((LP, hw), BF), hb), (S((3, width, hw), BF), vm),
        (S((8, width), F32), vm), (S((nt, rows, hw), BF), vm),
        (S((nt * rows // 16, 16, width), BF), hb), (S((2, 2, nz, 2, r, hw), BF), hb), half, half, half, half,
    ]
    dma = pltpu.SemaphoreType.DMA
    scratch = [
        V((r, 3 * hw), BF), V((r, hw), BF), V((8, 128), F32),
        V((LP, 768), BF), V((LP, 128), F32), V((LP, hw), BF),
        V((nt, rows, width), BF), V(((nt * rows + 192) // 16, 16, width), BF), V((LP, width), BF),
        V((nz, 2, r, 3 * hw), BF), V((nz, 2, 2, 2, 8, 128), F32),
        V((LP, hw), F32), V(((MARGIN + LP + 160) // 16, 16, hw), BF), V((nt, rows, hw), BF),
    ]
    p = sends_of(nz, orders["prm"])
    scratch += [dma((p,)), dma((p,)), dma((3,)), dma((nt,))]
    for name in ("wa", "wo", "u0", "u1", "d0", "d1"):
        p = sends_of(nz, orders[name])
        scratch += [dma((p,)), dma((p,))]
    scratch += [dma((3,)), dma((nt,)), dma((8,))]
    return pl.pallas_call(
        functools.partial(ka_kernel, nf, nt, orders),
        out_shape=[o[0] for o in outs],
        in_specs=[pl.BlockSpec(memory_space=pltpu.SMEM)] + [vm] * 5 + [hb] * 2 + [vm] * 6,
        out_specs=[o[1] for o in outs],
        scratch_shapes=scratch,
        compiler_params=pltpu.CompilerParams(
            collective_id=0, has_side_effects=True, vmem_limit_bytes=56 << 20
        ),
    )(lens, tok, wq, wk, wv, wo, wu, wd, *[v.reshape(1, -1) for v in smalls])


class Scatter:
    def __init__(self, pc, copies, own, land, send, recv, dims, order):
        self.pc, self.copies, self.own, self.land = pc, copies, own, land
        self.send_sem, self.recv_sem, self.dims, self.order = send, recv, dims, order
        self.place = dict(z=pc.z, x=pc.x, y=pc.y, c=pc.c)
        self.stage = 0
        self.count = 0
        self.waits = []

    def index(self, done, at):
        return tuple(at[d] if d in done else slice(None) for d in self.dims)

    def start(self):
        pc, axis = self.pc, self.order[self.stage]
        done = self.order[: self.stage + 1]
        self.waits = []
        for i, step in enumerate(axis_steps(pc, axis)):
            at = dict(self.place)
            at[axis] = lax.rem(pc.z + step["dz"], pc.nz) if axis == "z" else 1 - at[axis]
            dst = self.land[self.stage].at[i]
            n, dev = self.count, pc.rel(**step)
            self.copies.start(self.own.at[self.index(done, at)], dst, self.send_sem.at[n], self.recv_sem.at[n], dev)
            self.waits.append((dst, n, dev))
            self.count += 1

    def arrive(self):
        for dst, n, dev in self.waits:
            wait_recv(dst, self.send_sem.at[n], self.recv_sem.at[n], dev)
        land = self.land[self.stage]
        done = self.order[: self.stage + 1]
        rest = [d for d in self.dims if d not in done]
        sizes = [self.pc.nz if d == "z" else 2 for d in rest]
        count = 1
        for n in sizes:
            count *= n

        def body(i, carry):
            at, k = dict(self.place), i
            for d, n in reversed(list(zip(rest, sizes))):
                at[d] = lax.rem(k, n)
                k = k // n
            dst = self.own.at[tuple(at[d] for d in self.dims)]
            total = dst[...].astype(F32)
            for n in range(len(self.waits)):
                total = total + land[(n,) + tuple(at[d] for d in rest)].astype(F32)
            dst[...] = total.astype(BF)
            return carry

        lax.fori_loop(0, count, body, 0)
        self.stage += 1

    def next(self):
        self.arrive()
        self.start()

    def finish(self, out):
        for dst, n, dev in self.waits:
            wait_recv(dst, self.send_sem.at[n], self.recv_sem.at[n], dev)
        total = self.own[tuple(self.place[d] for d in self.dims)].astype(F32)
        for n in range(len(self.waits)):
            total = total + self.land[self.stage][n].astype(F32)
        out(total)


def landing(nz, dims, order, block):
    out = []
    for k, axis in enumerate(order):
        rest = [d for d in dims if d not in order[: k + 1]]
        n = nz - 1 if axis == "z" else 1
        out.append((n,) + tuple(nz if d == "z" else 2 for d in rest) + block)
    return out


def erf_parts(u):
    half = 0.5 * (1.0 + lax.erf(u * ROOT_HALF))
    return u * half, half + u * jnp.exp2(u * u * (-0.5 * 1.4426950408889634)) * DENSITY


def kc_kernel(
    nf, nt, orders,
    lens, tok, cot, o_own, wo, wqkv, gains, lse, ob, qkv, h1, wu0, wu1, wd0, wd1,
    out_ref, dx_out, gqk_out, gv_out, gwo_out, gwu_out, gwd_out, small_out,
    *rest,
):
    (sm, g1b, g2b, wb, inv2, h2a, dya, fs, hs, hr, dz, dos, dot_all, dop, delta, dhr, dhy, gq0_own, gq1_own, sm_src, sm_dst,
     o_part, u0_own, u1_own, d0_own, d1_own, h2_s, h2_r, dy_s, dy_r, f_s, f_r, hh_s, hh_r, do_s, do_r, dh_s, dh_r,
     st_s, st_r, loc) = rest[:41]
    rest = list(rest[41:])
    lands = {}
    for name in ("o", "u0", "u1", "d0", "d1", "q0", "q1"):
        k = len(orders[name])
        lands[name] = (rest[:k], rest[k], rest[k + 1])
        rest = rest[k + 2 :]
    pc = Place(nf, nt)
    cps = Copies()
    rows, width = tok.shape
    hw = ob.shape[1]
    nh = hw // HD
    groups = rows // 16
    r = width // nf
    c_me, c_other = pc.c, 1 - pc.c
    core = pc.rel(dc=1)

    local = []
    cut = width // 2
    for y in range(2):
        for base, lo, hi in ((y, wu0, wu1), (2 + y, wd0, wd1)):
            local.append((lo.at[y], wb.at[pl.ds(base * width, width), pl.ds(0, cut)]))
            local.append((hi.at[y], wb.at[pl.ds(base * width, width), pl.ds(cut, cut)]))
    weights = []
    for i, (src, dst) in enumerate(local):
        cp = pltpu.make_async_copy(src, dst, loc.at[i])
        cp.start()
        weights.append(cp)
    cot_copy = pltpu.make_async_copy(cot, dya.at[pc.c], loc.at[8])
    cot_copy.start()
    barrier_peers(pc)

    def slot_valid(t, first, count):
        row = iota((count, 1), 0) + (t * rows + first)
        total = lens[0, 0] + lens[0, 1] + lens[0, 2] + lens[0, 3]
        return jnp.where(row < total, 1.0, 0.0)

    half = rows // 2

    def own_dy(j, carry):
        at = pl.ds(pl.multiple_of(j * half, half), half)
        v = slot_valid(pc.t, j * half, half)
        dya[c_me, at, :] = (dya[c_me, at, :].astype(F32) * v).astype(BF)
        return carry

    cot_copy.wait()
    lax.fori_loop(0, 2, own_dy, 0)
    cps.start(dya.at[c_me], dya.at[c_me], dy_s.at[0], dy_r.at[0], core)
    gain, shift = gains[2:3, :], gains[3:4, :]
    none = jnp.zeros((1, width), F32)

    def colsum(x):
        return jnp.sum(x, axis=0, keepdims=True)

    def attn_out(j, carry):
        at = pl.ds(pl.multiple_of(j * half, half), half)
        v = slot_valid(pc.t, j * half, half)
        a = dot_nt(o_own[0, at, :], wo[0])
        for t in range(1, nt):
            a += dot_nt(o_own[t, at, :], wo[t])
        a = a * v
        x = tok[at, :].astype(F32)
        m = x + a
        h, n, inv = layer_norm_rows(m, gain, shift)
        sm[pl.ds(pl.multiple_of(j * half, half), half), :] = m
        sm[pl.ds(pl.multiple_of(rows + j * half, half), half), :] = n
        inv2[at, :] = jnp.broadcast_to(inv, (half, 128))
        h2a[c_me, at, :] = h.astype(BF)
        pltpu.make_async_remote_copy(
            src_ref=h2a.at[c_me, at], dst_ref=h2a.at[c_me, at], send_sem=h2_s.at[j], recv_sem=h2_r.at[j],
            device_id=core, device_id_type=MESH,
        ).start()
        return (carry[0] + colsum(x * x * v), carry[1] + colsum(a * a), carry[2] + colsum(m * m * v))

    sum_x, sum_a, sum_m = lax.fori_loop(0, 2, attn_out, (none, none, none))
    for cp in weights:
        cp.wait()

    def h2_copy(j, slot):
        at = pl.ds(pl.multiple_of(j * half, half), half)
        return pltpu.make_async_remote_copy(
            src_ref=h2a.at[slot, at], dst_ref=h2a.at[slot, at], send_sem=h2_s.at[j], recv_sem=h2_r.at[j],
            device_id=core, device_id_type=MESH,
        )

    def back_copy(j, src, dst, send, recv):
        at = pl.ds(pl.multiple_of(j * half, half), half)
        return pltpu.make_async_remote_copy(
            src_ref=src.at[at], dst_ref=dst.at[at], send_sem=send.at[j], recv_sem=recv.at[j],
            device_id=core, device_id_type=MESH,
        )

    def feed(i, carry):
        far = i // 2
        j = lax.rem(i, 2)
        slot = c_me + far * (1 - 2 * c_me)
        at = pl.ds(pl.multiple_of(j * half, half), half)

        @pl.when(far == 1)
        def _():
            h2_copy(j, c_other).wait_recv()

        @pl.when(i == 2)
        def _():
            wait_recv(dya.at[c_other], dy_s.at[0], dy_r.at[0], core)

        h = h2a[slot, at, :]
        g = dya[slot, at, :]
        f, dh = None, None
        for y in range(2):
            up = wb[y * width : (y + 1) * width, :]
            down = wb[(2 + y) * width : (3 + y) * width, :]
            act, slope = erf_parts(dot_nn(h, up))
            act = act.astype(BF)
            g1b[pl.ds(pl.multiple_of((y * 2 + slot) * rows + j * half, half), half), :] = act
            fy = dot_nt(act, down)
            du = (dot_nn(g, down) * slope).astype(BF)
            g2b[pl.ds((y * 2 + slot) * groups + j * (half // 16), half // 16)] = du.reshape(half // 16, 16, width)
            dy = dot_nt(du, up)
            f = fy if f is None else f + fy
            dh = dy if dh is None else dh + dy

        @pl.when(far == 0)
        def _():
            sm[pl.ds(pl.multiple_of(2 * rows + j * half, half), half), :] = f
            sm[pl.ds(pl.multiple_of(3 * rows + j * half, half), half), :] = dh

        @pl.when(far == 1)
        def _():
            fs[at, :] = f.astype(BF)
            hs[at, :] = dh.astype(BF)
            back_copy(j, hs, hr, hh_s, hh_r).start()
            back_copy(j, fs, fr_in, f_s, f_r).start()

        return carry

    fr_in = hr.at[pl.ds(rows, rows)]
    lax.fori_loop(0, 4, feed, 0)

    def rows_of(ref, y):
        return ref[pl.ds(y * 2 * rows, 2 * rows), :]

    dyall = dya[...].reshape(2 * rows, width)
    part_w = width // 2
    zblk = pc.nz // 2

    def weight_grad(left, get_right, lo, hi):
        for q in range(2):
            lq = left[:, q * part_w : (q + 1) * part_w]

            def body(y, carry, lq=lq, q=q):
                g = dot_tn(lq, get_right(y)).astype(BF)
                lo[y, q * zblk : (q + 1) * zblk] = g[:, :cut].reshape(zblk, 2, r, cut)
                hi[y, q * zblk : (q + 1) * zblk] = g[:, cut:].reshape(zblk, 2, r, cut)
                return carry

            lax.fori_loop(0, 2, body, 0)

    def scatter(name, own, dims):
        land, send, recv = lands[name]
        return Scatter(pc, cps, own, land, send, recv, dims, orders[name])

    weight_grad(dyall, lambda y: g1b[pl.ds(pl.multiple_of(y * 2 * rows, rows), 2 * rows), :], d0_own, d1_own)
    sc_d0 = scatter("d0", d0_own, "yzx")
    sc_d1 = scatter("d1", d1_own, "yzx")
    sc_d0.start()
    sc_d1.start()
    qkv_copy = pltpu.make_async_copy(qkv, g1b, loc.at[0])
    qkv_copy.start()

    def ln_back(j, carry):
        at = pl.ds(pl.multiple_of(j * half, half), half)
        back_copy(j, hs, hr, hh_s, hh_r).wait_recv()
        back_copy(j, fs, fr_in, f_s, f_r).wait_recv()
        v = slot_valid(pc.t, j * half, half)
        e = sm[pl.ds(pl.multiple_of(3 * rows + j * half, half), half), :] + hr[at, :].astype(F32)
        f = sm[pl.ds(pl.multiple_of(2 * rows + j * half, half), half), :]
        f = (f + hr[pl.ds(pl.multiple_of(rows + j * half, half), half), :].astype(F32)) * v
        m = sm[pl.ds(pl.multiple_of(j * half, half), half), :]
        n = sm[pl.ds(pl.multiple_of(rows + j * half, half), half), :]
        out_ref[at, :] = (m + f).astype(BF)
        c = e * gain
        dm = dya[c_me, at, :].astype(F32) + inv2[at, 0:1] * (
            c - jnp.mean(c, axis=-1, keepdims=True) - n * jnp.mean(c * n, axis=-1, keepdims=True)
        )
        dx_out[at, :] = dm
        z = (dm * v).astype(BF)
        dz[at, :] = z
        for t in range(nt):
            d = dot_nn(z, wo[t]).astype(BF)
            dos[t, pl.ds(j * (half // 16), half // 16)] = d.reshape(half // 16, 16, hw)
        return (carry[0] + colsum(e * n), carry[1] + colsum(e), carry[2] + colsum(f * f))

    sum_g2, sum_b2, sum_f = lax.fori_loop(0, 2, ln_back, (none, none, none))
    peers = [pc.rel(dy=1), pc.rel(dy=1, dc=1), core]
    own_groups = pl.ds(pc.t * groups, groups)
    for i, dev in enumerate(peers):
        cps.start(dos.at[dev[1]], dot_all.at[own_groups], do_s.at[i], do_r.at[pc.t], dev)
    cp = pltpu.make_async_copy(dos.at[pc.t], dot_all.at[own_groups], loc.at[2])
    cp.start()
    h1_copy = pltpu.make_async_copy(h1, wb.at[pl.ds(0, nt * rows)], loc.at[1])
    h1_copy.start()

    hall = h2a[...].reshape(2 * rows, width)
    weight_grad(
        hall,
        lambda y: g2b[pl.ds(y * 2 * groups, 2 * groups)].reshape(2 * rows, width),
        u0_own, u1_own,
    )
    sc_u0 = scatter("u0", u0_own, "yzx")
    sc_u1 = scatter("u1", u1_own, "yzx")
    sc_u0.start()
    for t in range(nt):
        o_part[t // 2, t % 2] = dot_tn(dz[...], o_own[t]).astype(BF).reshape(pc.nz, 2, r, hw)
    sc_o = scatter("o", o_part, "yczx")
    sc_o.start()

    small_out[...] = jnp.zeros(small_out.shape, F32)
    tail = 4 * groups
    dot_all[tail:] = jnp.zeros((dot_all.shape[0] - tail, 16, hw), BF)
    sm[...] = jnp.zeros(sm.shape, F32)
    head, mid = MARGIN // 16, (MARGIN + LP) // 16
    g2b[:head] = jnp.zeros((head, 16, width), BF)
    g2b[mid:] = jnp.zeros((g2b.shape[0] - mid, 16, width), BF)
    cp.wait()
    for dev in peers:
        wait_recv(dot_all.at[pl.ds(dev[1] * groups, groups)], do_s.at[0], do_r.at[dev[1]], dev)
    sc_u1.start()
    pack_rows(dot_all, dop, lens, True)

    dlt = LP // 4

    def deltas(j, carry):
        at = pl.ds(pl.multiple_of(j * dlt, 16), dlt)
        prod = dop[at, :].astype(F32) * ob[at, :].astype(F32)
        lane = iota((dlt, 128), 1)
        out = jnp.zeros((dlt, 128), F32)
        for h in range(nh):
            part_h = jnp.where(head_mask(dlt, hw, h), prod, 0.0)
            out = jnp.where(lane == h, jnp.sum(part_h, axis=-1, keepdims=True), out)
        delta[at, :] = out
        return carry

    lax.fori_loop(0, 4, deltas, 0)
    qkv_copy.wait()

    def back(at, keys, h, limit):
        nrow, nkey = at.size, keys.size
        zero = jnp.zeros((), BF)
        hm = head_mask(nrow, hw, h)
        q = jnp.where(hm, g1b[at, :hw], zero)
        s = dot_nt(q, g1b[keys, 256 : 256 + hw])
        p = jnp.exp2(s * EXP_SCALE - lse[at, h : h + 1])
        if limit is not None:
            p = jnp.where(iota(p.shape, 1) < limit, p, 0.0)
        g = jnp.where(hm, dop[at, :], zero)
        dp = dot_nt(g, g1b[keys, 512 : 512 + hw])
        ds = (p * (dp - delta[at, h : h + 1])).astype(BF)
        sm[keys, 512 : 512 + hw] += dot_tn(p.astype(BF), g)
        sm[keys, 256 : 256 + hw] += dot_tn(ds, q)
        km = jnp.where(head_mask(nkey, hw, h), g1b[keys, 256 : 256 + hw], zero)
        sm[at, :hw] += dot_nn(ds, km)

    for h in range(nh):
        def big(j, carry, h=h):
            back(pl.ds(pl.multiple_of(j * 256, 256), 256), pl.ds(0, BIG), h, None)
            return carry

        lax.fori_loop(0, BIG // 256, big, 0)
        def small(k, carry, h=h):
            at = pl.ds(pl.multiple_of(BIG + k * SMALL, 16), SMALL)
            back(at, at, h, small_length(lens, k))
            return carry

        lax.fori_loop(0, 3, small, 0)
        if h == 0:
            sc_d0.next()
            sc_o.next()
        elif h == 1:
            sc_u0.next()
            sc_d1.next()
            sc_o.next()
        else:
            sc_u1.next()
            sc_d0.next()
            sc_o.next()

    seg = segment_matrix(hw)
    gq = own_heads(gains[4:5, :], pc.t, nt, hw)
    gk = own_heads(gains[5:6, :], pc.t, nt, hw)

    def norms(j, carry):
        at = pl.ds(pl.multiple_of(j * dlt, 16), dlt)
        kept = lse[at, :]
        sums, outs = [], []
        for i, g in enumerate((gq, gk)):
            inv = jnp.broadcast_to(kept[:, 8 * (i + 1) : 8 * (i + 1) + 1], (dlt, hw))
            for k in range(1, nh):
                inv = jnp.where(head_mask(dlt, hw, k), kept[:, 8 * (i + 1) + k : 8 * (i + 1) + k + 1], inv)
            n = g1b[at, i * 256 : i * 256 + hw].astype(F32) / g
            e = sm[at, i * 256 : i * 256 + hw] * 0.125
            c = e * g
            d = inv * (c - segment_mean(c, seg) - n * segment_mean(c * n, seg))
            outs.append(d.astype(BF))
            sums.append(colsum(e * n))
        outs.append(sm[at, 512 : 512 + hw].astype(BF))
        for i, d in enumerate(outs):
            g2b[pl.ds(head + j * (dlt // 16), dlt // 16), :, i * 256 : i * 256 + hw] = d.reshape(dlt // 16, 16, hw)
        return (carry[0] + sums[0], carry[1] + sums[1])

    nones = jnp.zeros((1, hw), F32)
    sum_q, sum_k = lax.fori_loop(0, 4, norms, (nones, nones))
    sc_u0.next()
    sc_d1.next()

    def unpack(i, carry):
        out = unpack_tile(g2b, i * 128, lens)
        g1b[pl.ds(pl.multiple_of(i * 128, 128), 128), :] = out.astype(BF)
        return carry

    lax.fori_loop(0, 16, unpack, 0)
    h1_copy.wait()
    sc_u1.next()

    def project(t, sums):
        def body(j, carry):
            at = pl.ds(pl.multiple_of(t * rows + j * half, half), half)
            total = dot_nt(g1b[at, :hw], wqkv[0])
            total += dot_nt(g1b[at, 256 : 256 + hw], wqkv[1])
            total += dot_nt(g1b[at, 512 : 512 + hw], wqkv[2])
            low = total.astype(BF)
            g2b[pl.ds(t * groups + j * (half // 16), half // 16)] = low.reshape(half // 16, 16, width)
            return (carry[0] + colsum(total * wb[at, :].astype(F32)), carry[1] + colsum(total))

        return lax.fori_loop(0, 2, body, sums)

    def add_groups(t, src):
        def body(j, carry):
            at = pl.ds(t * groups + j * 4, 4)
            g2b[at] = (g2b[at].astype(F32) + src[pl.ds(j * 4, 4)].astype(F32)).astype(BF)
            return carry

        lax.fori_loop(0, groups // 4, body, 0)

    def block_of(t):
        return g2b.at[pl.ds(t * groups, groups)]

    t_fo, t_ff = (1 - pc.y) * 2 + c_other, (1 - pc.y) * 2 + c_me
    t_no = pc.y * 2 + c_other
    sc_q = [scatter("q0", gq0_own, "zx"), scatter("q1", gq1_own, "zx")]

    def attn_grad(piece):
        for q in range(2):
            hq = wb[: nt * rows, q * part_w : (q + 1) * part_w]
            if piece == 0:
                g = dot_tn(hq, g1b[: nt * rows, :512])
                g = jnp.concatenate([g[:, :hw], g[:, 256 : 256 + hw]], axis=1)
            else:
                g = dot_tn(hq, g1b[: nt * rows, 512 : 512 + hw])
            own = (gq0_own, gq1_own)[piece]
            own[q * zblk : (q + 1) * zblk] = g.astype(BF).reshape(zblk, 2, r, g.shape[1])
        sc_q[piece].start()

    sums = project(t_fo, (none, none))
    cps.start(block_of(t_fo), dhr.at[0], dh_s.at[0], dh_r.at[0], core)
    sums = project(t_ff, sums)
    wait_recv(dhr.at[0], dh_s.at[0], dh_r.at[0], core)
    add_groups(t_ff, dhr.at[0])
    cps.start(block_of(t_ff), dhy, dh_s.at[2], dh_r.at[2], pc.rel(dy=1))
    attn_grad(0)
    sums = project(t_no, sums)
    cps.start(block_of(t_no), dhr.at[1], dh_s.at[1], dh_r.at[1], core)
    sum_h, sum_d = project(pc.t, sums)
    attn_grad(1)

    gain_one, shift_one = gains[0:1, :], gains[1:2, :]
    small_out[4:5, :hw] = sum_q
    small_out[5:6, :hw] = sum_k
    placed = pltpu.roll(small_out[...], pc.t * hw, 1)
    small_out[...] = placed
    small_out[0:1, :] = (sum_h - shift_one * sum_d) / gain_one
    small_out[1:2, :] = sum_d
    small_out[2:3, :] = sum_g2
    small_out[3:4, :] = sum_b2
    lane = iota((1, width), 1)
    stat = jnp.zeros((1, width), F32)
    counted = jnp.sum(slot_valid(pc.t, 0, rows))
    for i, v in enumerate((sum_x, sum_a, sum_m, sum_f)):
        stat = jnp.where(lane == i, jnp.sum(v), stat)
    small_out[6:7, :] = jnp.where(lane == 4, counted, stat)
    small_stages = [[dict(dc=1)], [dict(dy=1)], [dict(dx=1)], axis_steps(pc, "z")]
    total = small_out[...]

    def small_send(k, total):
        sm_src[k] = total
        for i, step in enumerate(small_stages[k]):
            cps.start(sm_src.at[k], sm_dst.at[k + i], st_s.at[k + i], st_r.at[k + i], pc.rel(**step))

    def small_add(k, total):
        for i, step in enumerate(small_stages[k]):
            wait_recv(sm_dst.at[k + i], st_s.at[k + i], st_r.at[k + i], pc.rel(**step))
            total = total + sm_dst[k + i]
        return total

    small_send(0, total)
    total = small_add(0, total)
    small_send(1, total)
    for s in sc_q:
        s.next()
    total = small_add(1, total)
    small_send(2, total)
    total = small_add(2, total)
    small_send(3, total)

    wait_recv(dhr.at[1], dh_s.at[1], dh_r.at[1], core)
    add_groups(pc.t, dhr.at[1])
    wait_recv(dhy, dh_s.at[2], dh_r.at[2], pc.rel(dy=1))

    def last(j, carry):
        at = pl.ds(pl.multiple_of(j * 128, 128), 128)
        near = g2b[pl.ds(pc.t * groups + j * 8, 8)].astype(F32)
        e = (near + dhy[pl.ds(j * 8, 8)].astype(F32)).reshape(128, width)
        x = tok[at, :].astype(F32)
        _, n, inv = layer_norm_rows(x, gain_one, 0.0)
        c = e * gain_one
        grad = inv * (
            c - jnp.mean(c, axis=-1, keepdims=True) - n * jnp.mean(c * n, axis=-1, keepdims=True)
        )
        dx_out[at, :] = dx_out[at, :] + grad
        return carry

    lax.fori_loop(0, rows // 128, last, 0)
    small_out[...] = small_add(3, total)
    stat = small_out[6:7, :]
    counted = jnp.sum(jnp.where(lane == 4, stat, 0.0))
    small_out[7:8, :] = jnp.where(lane < 4, jnp.sqrt(stat / (counted * width)), 0.0)

    def store(ref, at=None):
        def put(total):
            if at is None:
                ref[...] = total
            else:
                ref[:, at : at + cut] = total

        return put

    sc_q[0].finish(store(gqk_out))
    sc_q[1].finish(store(gv_out))
    sc_o.finish(store(gwo_out))
    sc_d0.finish(store(gwd_out, 0))
    sc_d1.finish(store(gwd_out, cut))
    sc_u0.finish(store(gwu_out, 0))
    sc_u1.finish(store(gwu_out, cut))

    def sent(j, carry):
        h2_copy(j, c_me).wait_send()
        back_copy(j, hs, hr, hh_s, hh_r).wait_send()
        back_copy(j, fs, fr_in, f_s, f_r).wait_send()
        return carry

    lax.fori_loop(0, 2, sent, 0)
    cps.finish()


def call_kc(nf, nt, lens, tok, cot, o_own, wo, wqkv, gains, lse, ob, qkv, h1, wu0, wu1, wd0, wd1):
    nz = nf // 2
    rows, width = tok.shape
    hw = ob.shape[1]
    r = width // nf
    cut = width // 2
    orders = dict(
        o=("c", "x", "y", "z"), u0=("x", "y", "z"), u1=("y", "x", "z"),
        d0=("x", "y", "z"), d1=("z", "x", "y"), q0=("x", "z"), q1=("x", "z"),
    )
    S = jax.ShapeDtypeStruct
    V = pltpu.VMEM
    vm = pl.BlockSpec(memory_space=pltpu.VMEM)
    hb = pl.BlockSpec(memory_space=pl.ANY)
    dma = pltpu.SemaphoreType.DMA
    g3 = (MARGIN + LP + 160) // 16
    outs = [
        S((rows, width), BF), S((rows, width), F32), S((r, 2 * hw), F32), S((r, hw), F32), S((r, hw), F32),
        S((r, width), F32), S((r, width), F32), S((8, width), F32),
    ]
    own = (2, nz, 2, r, cut)
    scratch = [
        V((LP, width), F32), V((LP, width), BF), V((g3, 16, width), BF), V((4 * width, width), BF),
        V((rows, 128), F32), V((2, rows, width), BF), V((2, rows, width), BF),
        V((rows, width), BF), V((rows, width), BF), V((2 * rows, width), BF),
        V((rows, width), BF), V((nt, rows // 16, 16, hw), BF),
        V(((nt * rows + 192) // 16, 16, hw), BF), V((LP, hw), BF), V((LP, 128), F32),
        V((2, rows // 16, 16, width), BF), V((rows // 16, 16, width), BF),
        V((nz, 2, r, 2 * hw), BF), V((nz, 2, r, hw), BF), V((4, 8, width), F32), V((2 + nz, 8, width), F32),
        V((2, 2, nz, 2, r, hw), BF), V(own, BF), V(own, BF), V(own, BF), V(own, BF),
        dma((2,)), dma((2,)), dma((1,)), dma((1,)), dma((2,)), dma((2,)), dma((2,)), dma((2,)),
        dma((3,)), dma((nt,)), dma((3,)), dma((3,)), dma((2 + nz,)), dma((2 + nz,)), dma((9,)),
    ]
    for name in ("o", "u0", "u1", "d0", "d1", "q0", "q1"):
        dims = {"o": "yczx", "q0": "zx", "q1": "zx"}.get(name, "yzx")
        block = (r, {"o": hw, "q0": 2 * hw, "q1": hw}.get(name, cut))
        scratch += [V(shape, BF) for shape in landing(nz, dims, orders[name], block)]
        n = sends_of(nz, orders[name])
        scratch += [dma((n,)), dma((n,))]
    return pl.pallas_call(
        functools.partial(kc_kernel, nf, nt, orders),
        out_shape=outs,
        in_specs=[pl.BlockSpec(memory_space=pltpu.SMEM), vm, hb] + [vm] * 6 + [hb] * 6,
        out_specs=[vm] * 8,
        scratch_shapes=scratch,
        compiler_params=pltpu.CompilerParams(
            collective_id=1, has_side_effects=True, vmem_limit_bytes=64 << 20
        ),
    )(lens, tok, cot, o_own, wo, wqkv, gains, lse, ob, qkv, h1, wu0, wu1, wd0, wd1)


def local_fused(nf, nt, args):
    (tokens, lengths, pictures, w_query, w_key, w_value, w_out, w_up, w_down) = args[:9]
    smalls, cotangent = args[9:15], args[15]
    rows, width = tokens.shape[1:]
    hw = w_query.shape[1]
    per = smalls[0].shape[0]
    place = lax.axis_index("fsdp") * nt + lax.axis_index("tp")
    qkv, lse, ob, wqkv, gains, o_own, h1, wo, *halves = call_ka(
        nf, nt, lengths, tokens[0], w_query, w_key, w_value, w_out, w_up, w_down.T, smalls
    )
    result, grad_in, gqk, gv, gwo, gwu, gwd, small = call_kc(
        nf, nt, lengths, tokens[0], cotangent[0], o_own, wo.reshape(nt, width, hw), wqkv, gains, lse, ob,
        qkv, h1.reshape(nt * rows, width),
        *[w.reshape(2, width, width // 2) for w in halves],
    )
    own = lax.dynamic_slice_in_dim(small, place * per, per, 1)
    statistics = small[7, :4]
    return (
        result[None], grad_in[None],
        gqk[:, :hw], gqk[:, hw:], gv, gwo.T, gwu, gwd.T,
        own[0], own[1], own[2], own[3], own[4], own[5], statistics,
    )


def solution(mesh):
    nf, nt = mesh.shape["fsdp"], mesh.shape["tp"]

    def local(*args):
        tokens, w_query = args[0], args[3]
        if nt == 4 and tokens.shape[0] == 1 and tokens.shape[1] == 512 and w_query.shape[0] % 32 == 0:
            return local_fused(nf, nt, args)
        return local_plain(*args)

    in_specs = (
        P("fsdp", "tp", None),
        P("fsdp", None),
        P("fsdp", None),
        P("fsdp", "tp"),
        P("fsdp", "tp"),
        P("fsdp", "tp"),
        P("tp", "fsdp"),
        P("fsdp", "tp"),
        P("tp", "fsdp"),
        P(("fsdp", "tp")),
        P(("fsdp", "tp")),
        P(("fsdp", "tp")),
        P(("fsdp", "tp")),
        P(("fsdp", "tp")),
        P(("fsdp", "tp")),
        P("fsdp", "tp", None),
    )
    out_specs = (
        P("fsdp", "tp", None),
        P("fsdp", "tp", None),
        P("fsdp", "tp"),
        P("fsdp", "tp"),
        P("fsdp", "tp"),
        P("tp", "fsdp"),
        P("fsdp", "tp"),
        P("tp", "fsdp"),
        P(("fsdp", "tp")),
        P(("fsdp", "tp")),
        P(("fsdp", "tp")),
        P(("fsdp", "tp")),
        P(("fsdp", "tp")),
        P(("fsdp", "tp")),
        P(),
    )
    return jax.shard_map(local, mesh=mesh, in_specs=in_specs, out_specs=out_specs, check_vma=False)
```

```python
import functools

import jax
import jax.numpy as jnp
from jax import lax
from jax.experimental import pallas as pl
from jax.experimental.pallas import tpu as pltpu
from jax.sharding import PartitionSpec as P

HD = 64


EPS = 1e-06
ROOT_HALF = 0.7071067811865476
DENSITY = 0.3989422804014327


def normalise(values, scaling, offset):
    centre = jnp.mean(values, axis=-1, keepdims=True)
    centred = values - centre
    spread = jnp.mean(centred * centred, axis=-1, keepdims=True)
    inverse = lax.rsqrt(spread + EPS)
    normed = centred * inverse
    return (normed * scaling + offset, normed, inverse)


def normalise_back(grad_out, normed, inverse, scaling):
    grad_unit = grad_out * scaling
    grad_values = inverse * (
        grad_unit
        - jnp.mean(grad_unit, axis=-1, keepdims=True)
        - normed * jnp.mean(grad_unit * normed, axis=-1, keepdims=True)
    )
    return (grad_values, jnp.sum(grad_out * normed, axis=(0, 1)), jnp.sum(grad_out, axis=(0, 1)))


def gelu_slope(values):
    return (
        0.5 * (1.0 + jax.scipy.special.erf(values * ROOT_HALF))
        + values * jnp.exp(-0.5 * values * values) * DENSITY
    )


def gather_tokens(values):
    return lax.all_gather(values, "tp", axis=1, tiled=True)


def gather_grads(values):
    return lax.all_gather(values, "tp", axis=1, tiled=True)


def reduce_tokens(values):
    return lax.psum_scatter(
        values.astype(jnp.bfloat16), "tp", scatter_dimension=1, tiled=True
    ).astype(jnp.float32)


def reduce_grads(values):
    return lax.psum_scatter(
        values.astype(jnp.bfloat16), "tp", scatter_dimension=1, tiled=True
    ).astype(jnp.float32)


def block_scores(query, keyed, picture_query, picture_key, key_mask):
    raw_scores = jnp.einsum("qhd,khd->hqk", query, keyed, preferred_element_type=jnp.float32)
    allowed = (picture_query[:, None] == picture_key[None, :]) & (key_mask[None, :] > 0)
    return jnp.where(allowed[None], raw_scores * query.shape[-1] ** (-0.5), -1e30)


def forward_row(packed):
    query_row, key_row, value_row, picture_row, mask_row = packed
    full_len = query_row.shape[0]
    block_len = min(512, full_len)
    block_count = full_len // block_len

    def forward_one_block(packed_block):
        query_block, picture_block = packed_block
        scores = block_scores(query_block, key_row, picture_block, picture_row, mask_row)
        highest = jnp.max(scores, axis=-1, keepdims=True)
        logsum = highest + jnp.log(jnp.sum(jnp.exp(scores - highest), axis=-1, keepdims=True))
        probability = jnp.exp(scores - logsum).astype(jnp.bfloat16)
        mixture = jnp.einsum(
            "hqk,khd->qhd", probability, value_row, preferred_element_type=jnp.float32
        )
        return (mixture, logsum)

    query_blocks = query_row.reshape((block_count, block_len) + query_row.shape[1:])
    return lax.map(forward_one_block, (query_blocks, picture_row.reshape(block_count, block_len)))


def backward_row(packed):
    query_row, key_row, value_row, picture_row, mask_row, grad_row, logsum_row = packed
    full_len = query_row.shape[0]
    block_len = min(512, full_len)
    block_count = full_len // block_len
    factor = query_row.shape[-1] ** (-0.5)

    def backward_one_block(running, packed_block):
        grad_key, grad_value = running
        query_block, picture_block, grad_block, logsum_block = packed_block
        scores = block_scores(query_block, key_row, picture_block, picture_row, mask_row)
        probability = jnp.exp(scores - logsum_block)
        prob_low = probability.astype(jnp.bfloat16)
        grad_prob = jnp.einsum(
            "qhd,khd->hqk", grad_block, value_row, preferred_element_type=jnp.float32
        )
        grad_value = grad_value + jnp.einsum(
            "hqk,qhd->khd", prob_low, grad_block, preferred_element_type=jnp.float32
        )
        centre = jnp.sum(probability * grad_prob, axis=-1, keepdims=True)
        grad_scores = (probability * (grad_prob - centre)).astype(jnp.bfloat16)
        grad_query = factor * jnp.einsum(
            "hqk,khd->qhd", grad_scores, key_row, preferred_element_type=jnp.float32
        )
        grad_key = grad_key + factor * jnp.einsum(
            "hqk,qhd->khd", grad_scores, query_block, preferred_element_type=jnp.float32
        )
        return ((grad_key, grad_value), grad_query)

    zero_state = jnp.zeros(key_row.shape, jnp.float32)
    block_shape = (block_count, block_len) + query_row.shape[1:]
    (grad_key, grad_value), grad_query = lax.scan(
        backward_one_block,
        (zero_state, zero_state),
        (
            query_row.reshape(block_shape),
            picture_row.reshape(block_count, block_len),
            grad_row.reshape(block_shape),
            logsum_row,
        ),
    )
    return (grad_query.reshape(key_row.shape), grad_key, grad_value)


def local_plain(
    tokens,
    lengths,
    pictures,
    w_query,
    w_key,
    w_value,
    w_out,
    w_up,
    w_down,
    norm1_gain,
    norm1_shift,
    norm2_gain,
    norm2_shift,
    query_gain,
    key_gain,
    cotangent,
):
    tp_place = lax.axis_index("tp")
    local_len = tokens.shape[1]
    model_width = tokens.shape[2]
    full_len = pictures.shape[1]
    local_width = w_query.shape[1]
    heads_local = local_width // HD
    gain_one, shift_one, gain_two, shift_two, gain_query, gain_key = (
        lax.all_gather(norm1_gain, ("fsdp", "tp"), axis=0, tiled=True),
        lax.all_gather(norm1_shift, ("fsdp", "tp"), axis=0, tiled=True),
        lax.all_gather(norm2_gain, ("fsdp", "tp"), axis=0, tiled=True),
        lax.all_gather(norm2_shift, ("fsdp", "tp"), axis=0, tiled=True),
        lax.all_gather(query_gain, ("fsdp", "tp"), axis=0, tiled=True),
        lax.all_gather(key_gain, ("fsdp", "tp"), axis=0, tiled=True),
    )
    positions = jnp.arange(full_len, dtype=jnp.int32)
    valid_full = (positions[None, :] < jnp.sum(lengths, axis=1)[:, None]).astype(jnp.float32)
    valid_here = lax.dynamic_slice_in_dim(valid_full, tp_place * local_len, local_len, 1)[
        :, :, None
    ]
    qgain_here = lax.dynamic_slice_in_dim(
        gain_query, tp_place * local_width, local_width, 0
    ).reshape(heads_local, HD)
    kgain_here = lax.dynamic_slice_in_dim(gain_key, tp_place * local_width, local_width, 0).reshape(
        heads_local, HD
    )
    front_query, front_key, front_value, front_out = (
        lax.all_gather(w_query, "fsdp", axis=0, tiled=True),
        lax.all_gather(w_key, "fsdp", axis=0, tiled=True),
        lax.all_gather(w_value, "fsdp", axis=0, tiled=True),
        lax.all_gather(w_out, "fsdp", axis=1, tiled=True),
    )
    inputs = tokens.astype(jnp.float32)
    hidden, normed_one, inverse_one = normalise(inputs, gain_one, shift_one)
    hidden_full = gather_tokens(hidden.astype(jnp.bfloat16))
    row_shape = hidden_full.shape[:2] + (heads_local, HD)
    query = jnp.dot(hidden_full, front_query, preferred_element_type=jnp.float32).reshape(row_shape)
    keyed = jnp.dot(hidden_full, front_key, preferred_element_type=jnp.float32).reshape(row_shape)
    value_low = (
        jnp.dot(hidden_full, front_value, preferred_element_type=jnp.float32)
        .astype(jnp.bfloat16)
        .reshape(row_shape)
    )
    query_norm, query_unit, query_inverse = normalise(query, qgain_here, 0.0)
    key_norm, key_unit, key_inverse = normalise(keyed, kgain_here, 0.0)
    query_low = query_norm.astype(jnp.bfloat16)
    key_low = key_norm.astype(jnp.bfloat16)
    mixture, logsum = lax.map(forward_row, (query_low, key_low, value_low, pictures, valid_full))
    mixture_low = mixture.reshape(hidden_full.shape[:2] + (local_width,)).astype(jnp.bfloat16)
    attn_branch = valid_here * reduce_tokens(
        jnp.dot(mixture_low, front_out, preferred_element_type=jnp.float32)
    )
    middle = inputs + attn_branch
    hidden_two, normed_two, inverse_two = normalise(middle, gain_two, shift_two)
    hidden_two_full = gather_tokens(hidden_two.astype(jnp.bfloat16))
    front_up, front_down = (
        lax.all_gather(w_up, "fsdp", axis=0, tiled=True),
        lax.all_gather(w_down, "fsdp", axis=1, tiled=True),
    )
    up_value = jnp.dot(hidden_two_full, front_up, preferred_element_type=jnp.float32)
    activated = jax.nn.gelu(up_value, approximate=False).astype(jnp.bfloat16)
    mlp_branch = valid_here * reduce_tokens(
        jnp.dot(activated, front_down, preferred_element_type=jnp.float32)
    )
    result = (middle + mlp_branch).astype(jnp.bfloat16)
    square_sums = jnp.stack(
        [
            jnp.sum(valid_here * inputs * inputs),
            jnp.sum(attn_branch * attn_branch),
            jnp.sum(valid_here * middle * middle),
            jnp.sum(mlp_branch * mlp_branch),
        ]
    )
    valid_count = jnp.sum(valid_here)
    back_up, back_down = (
        lax.all_gather(w_up, "fsdp", axis=0, tiled=True),
        lax.all_gather(w_down, "fsdp", axis=1, tiled=True),
    )
    back_query, back_key, back_value, back_out = (
        lax.all_gather(w_query, "fsdp", axis=0, tiled=True),
        lax.all_gather(w_key, "fsdp", axis=0, tiled=True),
        lax.all_gather(w_value, "fsdp", axis=0, tiled=True),
        lax.all_gather(w_out, "fsdp", axis=1, tiled=True),
    )
    grad_y = cotangent.astype(jnp.float32) * valid_here
    grad_y_full = gather_grads(grad_y.astype(jnp.bfloat16))
    grad_down = jnp.einsum(
        "rlf,rld->fd", activated, grad_y_full, preferred_element_type=jnp.float32
    )
    grad_act = jnp.dot(grad_y_full, back_down.T, preferred_element_type=jnp.float32)
    grad_pre = (grad_act * gelu_slope(up_value)).astype(jnp.bfloat16)
    grad_up = jnp.einsum(
        "rld,rlf->df", hidden_two_full, grad_pre, preferred_element_type=jnp.float32
    )
    grad_hidden_two = reduce_grads(jnp.dot(grad_pre, back_up.T, preferred_element_type=jnp.float32))
    mlp_grads = (
        lax.psum_scatter(grad_up, "fsdp", scatter_dimension=0, tiled=True),
        lax.psum_scatter(grad_down, "fsdp", scatter_dimension=1, tiled=True),
    )
    grad_mid_norm, grad_gain_two, grad_shift_two = normalise_back(
        grad_hidden_two, normed_two, inverse_two, gain_two
    )
    grad_middle = grad_y + grad_mid_norm
    grad_branch_here = (valid_here * grad_middle).astype(jnp.bfloat16)
    grad_branch_full = gather_grads(grad_branch_here)
    grad_out_proj = jnp.einsum(
        "rlh,rld->hd", mixture_low, grad_branch_full, preferred_element_type=jnp.float32
    )
    grad_mixture = jnp.dot(grad_branch_full, back_out.T, preferred_element_type=jnp.float32).astype(
        jnp.bfloat16
    )
    grad_qnorm, grad_knorm, grad_value_full = lax.map(
        backward_row,
        (
            query_low,
            key_low,
            value_low,
            pictures,
            valid_full,
            grad_mixture.reshape(row_shape),
            logsum,
        ),
    )
    grad_query_pre, grad_qgain, unused_one = normalise_back(
        grad_qnorm, query_unit, query_inverse, qgain_here
    )
    grad_key_pre, grad_kgain, unused_two = normalise_back(
        grad_knorm, key_unit, key_inverse, kgain_here
    )
    flat_shape = hidden_full.shape[:2] + (local_width,)
    grad_query_low = grad_query_pre.reshape(flat_shape).astype(jnp.bfloat16)
    grad_key_low = grad_key_pre.reshape(flat_shape).astype(jnp.bfloat16)
    grad_value_low = grad_value_full.reshape(flat_shape).astype(jnp.bfloat16)
    grad_wquery = jnp.einsum(
        "rld,rlh->dh", hidden_full, grad_query_low, preferred_element_type=jnp.float32
    )
    grad_wkey = jnp.einsum(
        "rld,rlh->dh", hidden_full, grad_key_low, preferred_element_type=jnp.float32
    )
    grad_wvalue = jnp.einsum(
        "rld,rlh->dh", hidden_full, grad_value_low, preferred_element_type=jnp.float32
    )
    grad_hidden_part = (
        jnp.dot(grad_query_low, back_query.T, preferred_element_type=jnp.float32)
        + jnp.dot(grad_key_low, back_key.T, preferred_element_type=jnp.float32)
        + jnp.dot(grad_value_low, back_value.T, preferred_element_type=jnp.float32)
    )
    grad_hidden = reduce_grads(grad_hidden_part)
    attn_grads = (
        lax.psum_scatter(grad_wquery, "fsdp", scatter_dimension=0, tiled=True),
        lax.psum_scatter(grad_wkey, "fsdp", scatter_dimension=0, tiled=True),
        lax.psum_scatter(grad_wvalue, "fsdp", scatter_dimension=0, tiled=True),
        lax.psum_scatter(grad_out_proj, "fsdp", scatter_dimension=1, tiled=True),
    )
    grad_in_norm, grad_gain_one, grad_shift_one = normalise_back(
        grad_hidden, normed_one, inverse_one, gain_one
    )
    grad_inputs = grad_middle + grad_in_norm
    zero_width = jnp.zeros((model_width,), jnp.float32)
    grad_qgain_full = lax.dynamic_update_slice_in_dim(
        zero_width, grad_qgain.reshape(local_width), tp_place * local_width, 0
    )
    grad_kgain_full = lax.dynamic_update_slice_in_dim(
        zero_width, grad_kgain.reshape(local_width), tp_place * local_width, 0
    )
    small_shards = (
        lax.psum_scatter(grad_gain_one, ("fsdp", "tp"), scatter_dimension=0, tiled=True),
        lax.psum_scatter(grad_shift_one, ("fsdp", "tp"), scatter_dimension=0, tiled=True),
        lax.psum_scatter(grad_gain_two, ("fsdp", "tp"), scatter_dimension=0, tiled=True),
        lax.psum_scatter(grad_shift_two, ("fsdp", "tp"), scatter_dimension=0, tiled=True),
        lax.psum_scatter(grad_qgain_full, ("fsdp", "tp"), scatter_dimension=0, tiled=True),
        lax.psum_scatter(grad_kgain_full, ("fsdp", "tp"), scatter_dimension=0, tiled=True),
    )
    totals, counted = lax.psum((square_sums, valid_count), ("fsdp", "tp"))
    statistics = jnp.sqrt(totals / (counted * model_width))
    return (
        result,
        grad_inputs,
        attn_grads[0],
        attn_grads[1],
        attn_grads[2],
        attn_grads[3],
        mlp_grads[0],
        mlp_grads[1],
        small_shards[0],
        small_shards[1],
        small_shards[2],
        small_shards[3],
        small_shards[4],
        small_shards[5],
        statistics,
    )


BIG = 1024
SMALL = 448
LP = BIG + 3 * SMALL
MARGIN = 128
EXP_SCALE = 0.125 * 1.4426950408889634
MESH = pl.DeviceIdType.MESH
BF = jnp.bfloat16
F32 = jnp.float32


def dot_nn(a, b):
    return lax.dot_general(a, b, (((1,), (0,)), ((), ())), preferred_element_type=F32)


def dot_nt(a, b):
    return lax.dot_general(a, b, (((1,), (1,)), ((), ())), preferred_element_type=F32)


def dot_tn(a, b):
    return lax.dot_general(a, b, (((0,), (0,)), ((), ())), preferred_element_type=F32)


def iota(shape, dim):
    return lax.broadcasted_iota(jnp.int32, shape, dim)


def head_mask(rows, width, h):
    lane = iota((rows, width), 1)
    return (lane >= h * HD) & (lane < (h + 1) * HD)


def segment_matrix(width):
    r = iota((width, width), 0) // HD
    c = iota((width, width), 1) // HD
    return jnp.where(r == c, 1.0 / HD, 0.0).astype(BF)


def segment_mean(x, seg):
    return dot_nn(x.astype(BF), seg)


class Place:
    def __init__(self, nf, nt):
        self.nf, self.nt = nf, nt
        self.nx = 2
        self.nz = nf // 2
        f = lax.axis_index("fsdp")
        t = lax.axis_index("tp")
        self.f, self.t = f, t
        self.z, self.x = f // 2, lax.rem(f, 2)
        self.y, self.c = t // 2, lax.rem(t, 2)
        self.me = f * nt + t

    def rel(self, dz=0, dx=0, dy=0, dc=0):
        z = lax.rem(self.z + dz, self.nz) if dz else self.z
        x = 1 - self.x if dx else self.x
        y = 1 - self.y if dy else self.y
        c = 1 - self.c if dc else self.c
        return (z * 2 + x, y * 2 + c)


class Copies:
    def __init__(self):
        self.sent = []

    def start(self, src, dst, send_sem, recv_sem, dev):
        cp = pltpu.make_async_remote_copy(
            src_ref=src,
            dst_ref=dst,
            send_sem=send_sem,
            recv_sem=recv_sem,
            device_id=dev,
            device_id_type=MESH,
        )
        cp.start()
        self.sent.append(cp)

    def finish(self):
        for cp in self.sent:
            cp.wait_send()
        self.sent = []


def wait_recv(dst, send_sem, recv_sem, dev):
    pltpu.make_async_remote_copy(
        src_ref=dst,
        dst_ref=dst,
        send_sem=send_sem,
        recv_sem=recv_sem,
        device_id=dev,
        device_id_type=MESH,
    ).wait_recv()


def barrier_peers(pc):
    steps = [dict(dz=i) for i in range(1, pc.nz)]
    steps += [dict(dx=1), dict(dy=1), dict(dc=1), dict(dy=1, dc=1)]
    bar = pltpu.get_barrier_semaphore()
    for step in steps:
        pl.semaphore_signal(bar, inc=1, device_id=pc.rel(**step), device_id_type=MESH)
    pl.semaphore_wait(bar, len(steps))


def axis_steps(pc, axis):
    if axis == "z":
        return [dict(dz=i) for i in range(1, pc.nz)]
    return [{"d" + axis: 1}]


def sends_of(nz, order):
    return sum(nz - 1 if axis == "z" else 1 for axis in order)


class Gather:
    def __init__(self, pc, copies, src, dst, send, recv, dims, order):
        self.pc, self.copies = pc, copies
        self.src, self.dst, self.send_sem, self.recv_sem = src, dst, send, recv
        self.dims, self.order = dims, order
        self.stages = []
        count = 0
        for axis in order:
            steps = axis_steps(pc, axis)
            self.stages.append([(count + i, step) for i, step in enumerate(steps)])
            count += len(steps)

    def index(self, stage, at=None):
        place = at or dict(z=self.pc.z, x=self.pc.x, y=self.pc.y, c=self.pc.c)
        done = self.order[:stage]
        return tuple(slice(None) if d in done else place[d] for d in self.dims)

    def keep(self, sem):
        self.local = pltpu.make_async_copy(self.src, self.dst.at[self.index(0)], sem)
        self.local.start()

    def send(self, k):
        if k == 1:
            self.local.wait()
        idx = self.index(k)
        src = self.src if k == 0 else self.dst.at[idx]
        for n, step in self.stages[k]:
            self.copies.start(
                src, self.dst.at[idx], self.send_sem.at[n], self.recv_sem.at[n], self.pc.rel(**step)
            )

    def wait(self, k):
        pc = self.pc
        for n, step in self.stages[k]:
            at = dict(z=pc.z, x=pc.x, y=pc.y, c=pc.c)
            if "dz" in step:
                at["z"] = lax.rem(pc.z + pc.nz - step["dz"], pc.nz)
            else:
                axis = self.order[k]
                at[axis] = 1 - at[axis]
            dst = self.dst.at[self.index(k, at)]
            wait_recv(dst, self.send_sem.at[n], self.recv_sem.at[n], pc.rel(**step))


def slots_of(lens_ref):
    lens = [lens_ref[0, p] for p in range(4)]
    starts = [0]
    for p in range(3):
        starts.append(starts[-1] + lens[p])
    big = 0
    for p in range(1, 4):
        big = jnp.where(lens[p] == BIG, p, big)
    sb = 0
    for p in range(1, 4):
        sb = jnp.where(big == p, starts[p], sb)
    out = [(sb, BIG)]
    for k in range(3):
        s = jnp.where(big <= k, starts[k + 1], starts[k])
        n = jnp.where(big <= k, lens[k + 1], lens[k])
        out.append((s, n))
    return out


def small_length(lens, k):
    slots = slots_of(lens)
    return jnp.where(k == 0, slots[1][1], jnp.where(k == 1, slots[2][1], slots[3][1]))


BASES = (0, BIG, BIG + SMALL, BIG + 2 * SMALL)


def shift_matrix(rows, cols, r):
    return jnp.where(iota((rows, cols), 1) == iota((rows, cols), 0) + r, 1.0, 0.0).astype(BF)


def load_rows(src, first, count):
    return jnp.concatenate([src[first + m] for m in range(count)], axis=0)


def pack_rows(src, dst, lens, masked=False):
    def big(j, carry):
        s = slots_of(lens)[0][0]
        r = lax.rem(s, 16)
        d = shift_matrix(128, 144, r)
        out = dot_nn(d, load_rows(src, s // 16 + j * 8, 9)).astype(BF)
        dst[pl.ds(pl.multiple_of(j * 128, 128), 128), :] = out
        return carry

    lax.fori_loop(0, BIG // 128, big, 0)

    for k in range(3):

        def small(j, carry, k=k):
            s, n = slots_of(lens)[1 + k]
            r = lax.rem(s, 16)
            d = shift_matrix(112, 128, r)
            out = dot_nn(d, load_rows(src, s // 16 + j * 7, 8))
            if masked:
                out = jnp.where(iota(out.shape, 0) + j * 112 < n, out, 0.0)
            out = out.astype(BF)
            dst[pl.ds(pl.multiple_of(BASES[1 + k] + j * 112, 16), 112), :] = out
            return carry

        lax.fori_loop(0, 4, small, 0)


def unpack_tile(src, i0, lens):
    wa, ea, wb, sb = 0, 0, 0, 4096
    for (s, n), base in zip(slots_of(lens), BASES):
        inside = (s <= i0) & (i0 < s + n)
        begins = (s > i0) & (s <= i0 + 127)
        w = base + i0 - s + MARGIN
        wa = jnp.where(inside, w, wa)
        ea = jnp.where(inside, s + n - i0, ea)
        wb = jnp.where(begins, w, wb)
        sb = jnp.where(begins, s - i0, sb)
    out = None
    row = iota((128, 144), 0)
    col = iota((128, 144), 1)
    for w, ok in ((wa, lambda: row < ea), (wb, lambda: row >= sb)):
        r = lax.rem(w, 16)
        d = jnp.where((col == row + r) & ok(), 1.0, 0.0).astype(BF)
        part = dot_nn(d, load_rows(src, w // 16, 9))
        out = part if out is None else out + part
    return out


def layer_norm_rows(x, g, b):
    mean = jnp.mean(x, axis=-1, keepdims=True)
    xc = x - mean
    var = jnp.mean(xc * xc, axis=-1, keepdims=True)
    inv = lax.rsqrt(var + EPS)
    n = xc * inv
    return n * g + b, n, inv


def own_heads(row, t, nt, width):
    out = row[:, :width]
    for k in range(1, nt):
        out = jnp.where(t == k, row[:, k * width : (k + 1) * width], out)
    return out


def build_gains(tiles, gains, per):
    chunks = len(tiles) * per // 128
    lane = iota((8, 128), 1)
    acc = [jnp.zeros((8, 128), F32) for _ in range(chunks)]
    for d, tile in enumerate(tiles):
        j, a = divmod(d * per, 128)
        if a:
            tile = pltpu.roll(tile, a, 1)
        acc[j] = jnp.where((lane >= a) & (lane < a + per), tile, acc[j])
        if a + per > 128:
            acc[j + 1] = jnp.where(lane < a + per - 128, tile, acc[j + 1])
    for j in range(chunks):
        gains[:, j * 128 : (j + 1) * 128] = acc[j]


def ka_kernel(
    nf, nt, orders,
    lens, tok, wq, wk, wv, wo_in, wu, wd, s0, s1, s2, s3, s4, s5,
    qkv_out, lse_out, ob_out, wqkv, gains, o_own, h1_out, wo_all, wu0_all, wu1_all, wd0_all, wd1_all,
    wa, wo, prm, qkv, lse, ob, tok_all, h1t, h1p, wa_all, prm_all, of, op, osend,
    prm_s, prm_r, tok_s, tok_r, wa_s, wa_r, wo_s, wo_r,
    u0_s, u0_r, u1_s, u1_r, d0_s, d0_r, d1_s, d1_r, o_s, o_r, loc,
):
    pc = Place(nf, nt)
    cps = Copies()
    rows, width = tok.shape
    hw = ob.shape[1]
    cut = width // 2
    wa[...] = jnp.concatenate([wq[...], wk[...], wv[...]], axis=1)
    wo[...] = wo_in[...].T
    prm[...] = jnp.zeros(prm.shape, F32)
    for i, small in enumerate((s0, s1, s2, s3, s4, s5)):
        prm[i : i + 1, : small.shape[1]] = small[...]
    gp = Gather(pc, cps, prm, prm_all, prm_s, prm_r, "zxyc", orders["prm"])
    ga = Gather(pc, cps, wa, wa_all, wa_s, wa_r, "zx", orders["wa"])
    go = Gather(pc, cps, wo, wo_all, wo_s, wo_r, "yczx", orders["wo"])
    gu0 = Gather(pc, cps, wu.at[:, :cut], wu0_all, u0_s, u0_r, "yzx", orders["u0"])
    gu1 = Gather(pc, cps, wu.at[:, cut:], wu1_all, u1_s, u1_r, "yzx", orders["u1"])
    gd0 = Gather(pc, cps, wd.at[:, :cut], wd0_all, d0_s, d0_r, "yzx", orders["d0"])
    gd1 = Gather(pc, cps, wd.at[:, cut:], wd1_all, d1_s, d1_r, "yzx", orders["d1"])
    for i, g in enumerate((gp, ga, go, gd1, gu0, gd0, gu1)):
        g.keep(loc.at[i])
    barrier_peers(pc)

    cps.start(tok, tok_all.at[pc.t], tok_s.at[1], tok_r.at[pc.t], pc.rel(dc=1))
    gp.send(0)
    ga.send(0)
    gd1.send(0)
    cps.start(tok, tok_all.at[pc.t], tok_s.at[0], tok_r.at[pc.t], pc.rel(dy=1))
    h1t[4 * rows // 16 :] = jnp.zeros((h1t.shape[0] - 4 * rows // 16, 16, width), BF)
    for k in range(4):
        gp.wait(k)
        if k < 3:
            gp.send(k + 1)
    gd1.wait(0)
    gd1.send(1)
    go.send(0)
    tiles = []
    for d in range(nf * nt):
        f, t = divmod(d, nt)
        tiles.append(prm_all[f // 2, f % 2, t // 2, t % 2])
    build_gains(tiles, gains, width // (nf * nt))
    gain_one, shift_one = gains[0:1, :], gains[1:2, :]

    def norm_block(t, block):
        def body(j, carry):
            at = pl.ds(pl.multiple_of(j * 128, 128), 128)
            out, _, _ = layer_norm_rows(block[at, :].astype(F32), gain_one, shift_one)
            h1t[pl.ds(t * (rows // 16) + j * 8, 8)] = out.astype(BF).reshape(8, 16, width)
            return carry

        lax.fori_loop(0, rows // 128, body, 0)

    def wait_tok(t):
        wait_recv(tok_all.at[t], tok_s.at[0], tok_r.at[t], pc.rel(dc=1))

    norm_block(pc.t, tok)
    t_core, t_y, t_diag = pc.rel(dc=1)[1], pc.rel(dy=1)[1], pc.rel(dy=1, dc=1)[1]
    wait_tok(t_core)
    norm_block(t_core, tok_all.at[t_core])
    ga.wait(0)
    ga.send(1)
    gu0.send(0)
    gd0.send(0)
    wait_tok(t_y)
    cps.start(tok_all.at[t_y], tok_all.at[t_y], tok_s.at[2], tok_r.at[t_y], pc.rel(dc=1))
    norm_block(t_y, tok_all.at[t_y])
    wait_tok(t_diag)
    norm_block(t_diag, tok_all.at[t_diag])
    h1_copy = pltpu.make_async_copy(h1t.at[: 4 * rows // 16], h1_out, loc.at[0])
    h1_copy.start()

    pack_rows(h1t, h1p, lens)
    go.wait(0)
    go.send(1)
    gu0.wait(0)
    gu0.send(1)
    gd0.wait(0)
    gd0.send(1)
    gu1.send(0)
    gd1.wait(1)
    ga.wait(1)
    seg = segment_matrix(hw)
    gq = own_heads(gains[4:5, :], pc.t, nt, hw)
    gk = own_heads(gains[5:6, :], pc.t, nt, hw)
    w_full = wa_all[...].reshape(width, 3 * hw)
    for i in range(3):
        wqkv[i] = w_full[:, i * hw : (i + 1) * hw]

    qt = LP // 4

    def project(j, carry):
        at = pl.ds(pl.multiple_of(j * qt, 16), qt)
        h = h1p[at, :]
        lane = iota((qt, 128), 1)
        kept = jnp.zeros((qt, 128), F32)
        for i, g in enumerate((gq, gk)):
            q = dot_nn(h, wqkv[i])
            qc = q - segment_mean(q, seg)
            inv = lax.rsqrt(segment_mean(qc * qc, seg) + EPS)
            qkv[at, i * 256 : i * 256 + hw] = (qc * inv * g).astype(BF)
            for k in range(hw // HD):
                kept = jnp.where(lane == 8 * (i + 1) + k, inv[:, k * HD : k * HD + 1], kept)
        lse[at, :] = kept
        qkv[at, 512 : 512 + hw] = dot_nn(h, wqkv[2]).astype(BF)
        return carry

    lax.fori_loop(0, 4, project, 0)
    qkv[:, 512 + hw :] = jnp.ones((LP, 256 - hw), BF)
    saves = [h1_copy, pltpu.make_async_copy(qkv, qkv_out, loc.at[2])]
    saves[-1].start()
    head, tail = MARGIN // 16, (MARGIN + LP) // 16
    op[:head] = jnp.zeros((head, 16, hw), BF)
    op[tail:] = jnp.zeros((op.shape[0] - tail, 16, hw), BF)

    gu0.wait(1)
    gu0.send(2)
    gu1.wait(0)
    gu1.send(1)
    gd0.wait(1)
    gd0.send(2)
    go.wait(1)
    go.send(2)
    gd1.send(2)

    def attend(at, keys, h, limit):
        nrow = at.size
        q = jnp.where(head_mask(nrow, hw, h), qkv[at, :hw], jnp.zeros((), BF))
        s = dot_nt(q, qkv[keys, 256 : 256 + hw])
        p = jnp.exp2(s * EXP_SCALE)
        if limit is not None:
            p = jnp.where(iota(p.shape, 1) < limit, p, 0.0)
        oa = dot_nn(p.astype(BF), qkv[keys, 512:768])
        total = oa[:, hw : hw + 1]
        o = oa[:, :hw] * (1.0 / total)
        l2 = jnp.log2(total)
        lane = iota((nrow, 128), 1)
        if h == 0:
            of[at, :] = o
        else:
            of[at, :] = jnp.where(head_mask(nrow, hw, h), o, of[at, :])
        lse[at, :] = jnp.where(lane == h, l2, lse[at, :])

    nh = hw // HD
    for h in range(nh):
        def big(j, carry, h=h):
            attend(pl.ds(pl.multiple_of(j * 512, 512), 512), pl.ds(0, BIG), h, None)
            return carry

        lax.fori_loop(0, BIG // 512, big, 0)

        def small(k, carry, h=h):
            at = pl.ds(pl.multiple_of(BIG + k * SMALL, 16), SMALL)
            attend(at, at, h, small_length(lens, k))
            return carry

        lax.fori_loop(0, 3, small, 0)
        if h == 1:
            gu1.wait(1)
            gu1.send(2)

    ob[...] = of[...].astype(BF)
    for i, (src, dst) in enumerate(((lse, lse_out), (ob, ob_out))):
        saves.append(pltpu.make_async_copy(src, dst, loc.at[3 + i]))
        saves[-1].start()
    op[head:tail] = ob[...].reshape(LP // 16, 16, hw)

    def unpack_block(t):
        def unpack(i, carry):
            out = unpack_tile(op, t * rows + i * 128, lens)
            osend[t, pl.ds(pl.multiple_of(i * 128, 128), 128), :] = out.astype(BF)
            return carry

        lax.fori_loop(0, rows // 128, unpack, 0)

    peers = [pc.rel(dy=1, dc=1), pc.rel(dy=1), pc.rel(dc=1)]
    for i, dev in enumerate(peers):
        unpack_block(dev[1])
        cps.start(osend.at[dev[1]], o_own.at[pc.t], o_s.at[i], o_r.at[pc.t], dev)
    unpack_block(pc.t)
    go.wait(2)
    go.send(3)
    cp = pltpu.make_async_copy(osend.at[pc.t], o_own.at[pc.t], loc.at[1])
    cp.start()
    cp.wait()
    for cp in saves:
        cp.wait()
    go.wait(3)
    for g in (gu0, gd0, gu1, gd1):
        g.wait(2)
    for dev in peers:
        wait_recv(o_own.at[dev[1]], o_s.at[0], o_r.at[dev[1]], dev)
    cps.finish()


def call_ka(nf, nt, lens, tok, wq, wk, wv, wo, wu, wd, smalls):
    nz = nf // 2
    rows, width = tok.shape
    r, hw = wq.shape
    cut = width // 2
    orders = dict(
        prm=("z", "x", "y", "c"), wa=("z", "x"), wo=("z", "y", "x", "c"),
        u0=("z", "y", "x"), d0=("z", "x", "y"), u1=("z", "y", "x"), d1=("y", "x", "z"),
    )
    S = jax.ShapeDtypeStruct
    V = pltpu.VMEM
    vm = pl.BlockSpec(memory_space=pltpu.VMEM)
    hb = pl.BlockSpec(memory_space=pl.ANY)
    half = (S((2, nz, 2, r, cut), BF), hb)
    outs = [
        (S((LP, 768), BF), hb), (S((LP, 128), F32), hb), (S((LP, hw), BF), hb), (S((3, width, hw), BF), vm),
        (S((8, width), F32), vm), (S((nt, rows, hw), BF), vm),
        (S((nt * rows // 16, 16, width), BF), hb), (S((2, 2, nz, 2, r, hw), BF), hb), half, half, half, half,
    ]
    dma = pltpu.SemaphoreType.DMA
    scratch = [
        V((r, 3 * hw), BF), V((r, hw), BF), V((8, 128), F32),
        V((LP, 768), BF), V((LP, 128), F32), V((LP, hw), BF),
        V((nt, rows, width), BF), V(((nt * rows + 192) // 16, 16, width), BF), V((LP, width), BF),
        V((nz, 2, r, 3 * hw), BF), V((nz, 2, 2, 2, 8, 128), F32),
        V((LP, hw), F32), V(((MARGIN + LP + 160) // 16, 16, hw), BF), V((nt, rows, hw), BF),
    ]
    p = sends_of(nz, orders["prm"])
    scratch += [dma((p,)), dma((p,)), dma((3,)), dma((nt,))]
    for name in ("wa", "wo", "u0", "u1", "d0", "d1"):
        p = sends_of(nz, orders[name])
        scratch += [dma((p,)), dma((p,))]
    scratch += [dma((3,)), dma((nt,)), dma((8,))]
    return pl.pallas_call(
        functools.partial(ka_kernel, nf, nt, orders),
        out_shape=[o[0] for o in outs],
        in_specs=[pl.BlockSpec(memory_space=pltpu.SMEM)] + [vm] * 5 + [hb] * 2 + [vm] * 6,
        out_specs=[o[1] for o in outs],
        scratch_shapes=scratch,
        compiler_params=pltpu.CompilerParams(
            collective_id=0, has_side_effects=True, vmem_limit_bytes=56 << 20
        ),
    )(lens, tok, wq, wk, wv, wo, wu, wd, *[v.reshape(1, -1) for v in smalls])


class Scatter:
    def __init__(self, pc, copies, own, land, send, recv, dims, order):
        self.pc, self.copies, self.own, self.land = pc, copies, own, land
        self.send_sem, self.recv_sem, self.dims, self.order = send, recv, dims, order
        self.place = dict(z=pc.z, x=pc.x, y=pc.y, c=pc.c)
        self.stage = 0
        self.count = 0
        self.waits = []

    def index(self, done, at):
        return tuple(at[d] if d in done else slice(None) for d in self.dims)

    def start(self):
        pc, axis = self.pc, self.order[self.stage]
        done = self.order[: self.stage + 1]
        self.waits = []
        for i, step in enumerate(axis_steps(pc, axis)):
            at = dict(self.place)
            at[axis] = lax.rem(pc.z + step["dz"], pc.nz) if axis == "z" else 1 - at[axis]
            dst = self.land[self.stage].at[i]
            n, dev = self.count, pc.rel(**step)
            self.copies.start(self.own.at[self.index(done, at)], dst, self.send_sem.at[n], self.recv_sem.at[n], dev)
            self.waits.append((dst, n, dev))
            self.count += 1

    def arrive(self):
        for dst, n, dev in self.waits:
            wait_recv(dst, self.send_sem.at[n], self.recv_sem.at[n], dev)
        land = self.land[self.stage]
        done = self.order[: self.stage + 1]
        rest = [d for d in self.dims if d not in done]
        sizes = [self.pc.nz if d == "z" else 2 for d in rest]
        count = 1
        for n in sizes:
            count *= n

        def body(i, carry):
            at, k = dict(self.place), i
            for d, n in reversed(list(zip(rest, sizes))):
                at[d] = lax.rem(k, n)
                k = k // n
            dst = self.own.at[tuple(at[d] for d in self.dims)]
            total = dst[...].astype(F32)
            for n in range(len(self.waits)):
                total = total + land[(n,) + tuple(at[d] for d in rest)].astype(F32)
            dst[...] = total.astype(BF)
            return carry

        lax.fori_loop(0, count, body, 0)
        self.stage += 1

    def next(self):
        self.arrive()
        self.start()

    def finish(self, out):
        for dst, n, dev in self.waits:
            wait_recv(dst, self.send_sem.at[n], self.recv_sem.at[n], dev)
        total = self.own[tuple(self.place[d] for d in self.dims)].astype(F32)
        for n in range(len(self.waits)):
            total = total + self.land[self.stage][n].astype(F32)
        out(total)


def landing(nz, dims, order, block):
    out = []
    for k, axis in enumerate(order):
        rest = [d for d in dims if d not in order[: k + 1]]
        n = nz - 1 if axis == "z" else 1
        out.append((n,) + tuple(nz if d == "z" else 2 for d in rest) + block)
    return out


def erf_parts(u):
    half = 0.5 * (1.0 + lax.erf(u * ROOT_HALF))
    return u * half, half + u * jnp.exp2(u * u * (-0.5 * 1.4426950408889634)) * DENSITY


def kc_kernel(
    nf, nt, orders,
    lens, tok, cot, o_own, wo, wqkv, gains, lse, ob, qkv, h1, wu0, wu1, wd0, wd1,
    out_ref, dx_out, gqk_out, gv_out, gwo_out, gwu_out, gwd_out, small_out,
    *rest,
):
    (sm, g1b, g2b, wb, inv2, h2a, dya, fs, hs, hr, dz, dos, dot_all, dop, delta, dhr, dhy, gq0_own, gq1_own, sm_src, sm_dst,
     o_part, u0_own, u1_own, d0_own, d1_own, h2_s, h2_r, dy_s, dy_r, f_s, f_r, hh_s, hh_r, do_s, do_r, dh_s, dh_r,
     st_s, st_r, loc) = rest[:41]
    rest = list(rest[41:])
    lands = {}
    for name in ("o", "u0", "u1", "d0", "d1", "q0", "q1"):
        k = len(orders[name])
        lands[name] = (rest[:k], rest[k], rest[k + 1])
        rest = rest[k + 2 :]
    pc = Place(nf, nt)
    cps = Copies()
    rows, width = tok.shape
    hw = ob.shape[1]
    nh = hw // HD
    groups = rows // 16
    r = width // nf
    c_me, c_other = pc.c, 1 - pc.c
    core = pc.rel(dc=1)

    local = []
    cut = width // 2
    for y in range(2):
        for base, lo, hi in ((y, wu0, wu1), (2 + y, wd0, wd1)):
            local.append((lo.at[y], wb.at[pl.ds(base * width, width), pl.ds(0, cut)]))
            local.append((hi.at[y], wb.at[pl.ds(base * width, width), pl.ds(cut, cut)]))
    weights = []
    for i, (src, dst) in enumerate(local):
        cp = pltpu.make_async_copy(src, dst, loc.at[i])
        cp.start()
        weights.append(cp)
    cot_copy = pltpu.make_async_copy(cot, dya.at[pc.c], loc.at[8])
    cot_copy.start()
    barrier_peers(pc)

    def slot_valid(t, first, count):
        row = iota((count, 1), 0) + (t * rows + first)
        total = lens[0, 0] + lens[0, 1] + lens[0, 2] + lens[0, 3]
        return jnp.where(row < total, 1.0, 0.0)

    half = rows // 2

    def own_dy(j, carry):
        at = pl.ds(pl.multiple_of(j * half, half), half)
        v = slot_valid(pc.t, j * half, half)
        dya[c_me, at, :] = (dya[c_me, at, :].astype(F32) * v).astype(BF)
        return carry

    cot_copy.wait()
    lax.fori_loop(0, 2, own_dy, 0)
    cps.start(dya.at[c_me], dya.at[c_me], dy_s.at[0], dy_r.at[0], core)
    gain, shift = gains[2:3, :], gains[3:4, :]
    none = jnp.zeros((1, width), F32)

    def colsum(x):
        return jnp.sum(x, axis=0, keepdims=True)

    def attn_out(j, carry):
        at = pl.ds(pl.multiple_of(j * half, half), half)
        v = slot_valid(pc.t, j * half, half)
        a = dot_nt(o_own[0, at, :], wo[0])
        for t in range(1, nt):
            a += dot_nt(o_own[t, at, :], wo[t])
        a = a * v
        x = tok[at, :].astype(F32)
        m = x + a
        h, n, inv = layer_norm_rows(m, gain, shift)
        sm[pl.ds(pl.multiple_of(j * half, half), half), :] = m
        sm[pl.ds(pl.multiple_of(rows + j * half, half), half), :] = n
        inv2[at, :] = jnp.broadcast_to(inv, (half, 128))
        h2a[c_me, at, :] = h.astype(BF)
        pltpu.make_async_remote_copy(
            src_ref=h2a.at[c_me, at], dst_ref=h2a.at[c_me, at], send_sem=h2_s.at[j], recv_sem=h2_r.at[j],
            device_id=core, device_id_type=MESH,
        ).start()
        return (carry[0] + colsum(x * x * v), carry[1] + colsum(a * a), carry[2] + colsum(m * m * v))

    sum_x, sum_a, sum_m = lax.fori_loop(0, 2, attn_out, (none, none, none))
    for cp in weights:
        cp.wait()

    def h2_copy(j, slot):
        at = pl.ds(pl.multiple_of(j * half, half), half)
        return pltpu.make_async_remote_copy(
            src_ref=h2a.at[slot, at], dst_ref=h2a.at[slot, at], send_sem=h2_s.at[j], recv_sem=h2_r.at[j],
            device_id=core, device_id_type=MESH,
        )

    def back_copy(j, src, dst, send, recv):
        at = pl.ds(pl.multiple_of(j * half, half), half)
        return pltpu.make_async_remote_copy(
            src_ref=src.at[at], dst_ref=dst.at[at], send_sem=send.at[j], recv_sem=recv.at[j],
            device_id=core, device_id_type=MESH,
        )

    def feed(i, carry):
        far = i // 2
        j = lax.rem(i, 2)
        slot = c_me + far * (1 - 2 * c_me)
        at = pl.ds(pl.multiple_of(j * half, half), half)

        @pl.when(far == 1)
        def _():
            h2_copy(j, c_other).wait_recv()

        @pl.when(i == 2)
        def _():
            wait_recv(dya.at[c_other], dy_s.at[0], dy_r.at[0], core)

        h = h2a[slot, at, :]
        g = dya[slot, at, :]
        f, dh = None, None
        for y in range(2):
            up = wb[y * width : (y + 1) * width, :]
            down = wb[(2 + y) * width : (3 + y) * width, :]
            act, slope = erf_parts(dot_nn(h, up))
            act = act.astype(BF)
            g1b[pl.ds(pl.multiple_of((y * 2 + slot) * rows + j * half, half), half), :] = act
            fy = dot_nt(act, down)
            du = (dot_nn(g, down) * slope).astype(BF)
            g2b[pl.ds((y * 2 + slot) * groups + j * (half // 16), half // 16)] = du.reshape(half // 16, 16, width)
            dy = dot_nt(du, up)
            f = fy if f is None else f + fy
            dh = dy if dh is None else dh + dy

        @pl.when(far == 0)
        def _():
            sm[pl.ds(pl.multiple_of(2 * rows + j * half, half), half), :] = f
            sm[pl.ds(pl.multiple_of(3 * rows + j * half, half), half), :] = dh

        @pl.when(far == 1)
        def _():
            fs[at, :] = f.astype(BF)
            hs[at, :] = dh.astype(BF)
            back_copy(j, hs, hr, hh_s, hh_r).start()
            back_copy(j, fs, fr_in, f_s, f_r).start()

        return carry

    fr_in = hr.at[pl.ds(rows, rows)]
    lax.fori_loop(0, 4, feed, 0)

    def rows_of(ref, y):
        return ref[pl.ds(y * 2 * rows, 2 * rows), :]

    dyall = dya[...].reshape(2 * rows, width)
    part_w = width // 2
    zblk = pc.nz // 2

    def weight_grad(left, get_right, lo, hi):
        for q in range(2):
            lq = left[:, q * part_w : (q + 1) * part_w]

            def body(y, carry, lq=lq, q=q):
                g = dot_tn(lq, get_right(y)).astype(BF)
                lo[y, q * zblk : (q + 1) * zblk] = g[:, :cut].reshape(zblk, 2, r, cut)
                hi[y, q * zblk : (q + 1) * zblk] = g[:, cut:].reshape(zblk, 2, r, cut)
                return carry

            lax.fori_loop(0, 2, body, 0)

    def scatter(name, own, dims):
        land, send, recv = lands[name]
        return Scatter(pc, cps, own, land, send, recv, dims, orders[name])

    weight_grad(dyall, lambda y: g1b[pl.ds(pl.multiple_of(y * 2 * rows, rows), 2 * rows), :], d0_own, d1_own)
    sc_d0 = scatter("d0", d0_own, "yzx")
    sc_d1 = scatter("d1", d1_own, "yzx")
    sc_d0.start()
    sc_d1.start()
    qkv_copy = pltpu.make_async_copy(qkv, g1b, loc.at[0])
    qkv_copy.start()

    def ln_back(j, carry):
        at = pl.ds(pl.multiple_of(j * half, half), half)
        back_copy(j, hs, hr, hh_s, hh_r).wait_recv()
        back_copy(j, fs, fr_in, f_s, f_r).wait_recv()
        v = slot_valid(pc.t, j * half, half)
        e = sm[pl.ds(pl.multiple_of(3 * rows + j * half, half), half), :] + hr[at, :].astype(F32)
        f = sm[pl.ds(pl.multiple_of(2 * rows + j * half, half), half), :]
        f = (f + hr[pl.ds(pl.multiple_of(rows + j * half, half), half), :].astype(F32)) * v
        m = sm[pl.ds(pl.multiple_of(j * half, half), half), :]
        n = sm[pl.ds(pl.multiple_of(rows + j * half, half), half), :]
        out_ref[at, :] = (m + f).astype(BF)
        c = e * gain
        dm = dya[c_me, at, :].astype(F32) + inv2[at, 0:1] * (
            c - jnp.mean(c, axis=-1, keepdims=True) - n * jnp.mean(c * n, axis=-1, keepdims=True)
        )
        dx_out[at, :] = dm
        z = (dm * v).astype(BF)
        dz[at, :] = z
        for t in range(nt):
            d = dot_nn(z, wo[t]).astype(BF)
            dos[t, pl.ds(j * (half // 16), half // 16)] = d.reshape(half // 16, 16, hw)
        return (carry[0] + colsum(e * n), carry[1] + colsum(e), carry[2] + colsum(f * f))

    sum_g2, sum_b2, sum_f = lax.fori_loop(0, 2, ln_back, (none, none, none))
    peers = [pc.rel(dy=1), pc.rel(dy=1, dc=1), core]
    own_groups = pl.ds(pc.t * groups, groups)
    for i, dev in enumerate(peers):
        cps.start(dos.at[dev[1]], dot_all.at[own_groups], do_s.at[i], do_r.at[pc.t], dev)
    cp = pltpu.make_async_copy(dos.at[pc.t], dot_all.at[own_groups], loc.at[2])
    cp.start()
    h1_copy = pltpu.make_async_copy(h1, wb.at[pl.ds(0, nt * rows)], loc.at[1])
    h1_copy.start()

    hall = h2a[...].reshape(2 * rows, width)
    weight_grad(
        hall,
        lambda y: g2b[pl.ds(y * 2 * groups, 2 * groups)].reshape(2 * rows, width),
        u0_own, u1_own,
    )
    sc_u0 = scatter("u0", u0_own, "yzx")
    sc_u1 = scatter("u1", u1_own, "yzx")
    sc_u0.start()
    for t in range(nt):
        o_part[t // 2, t % 2] = dot_tn(dz[...], o_own[t]).astype(BF).reshape(pc.nz, 2, r, hw)
    sc_o = scatter("o", o_part, "yczx")
    sc_o.start()

    small_out[...] = jnp.zeros(small_out.shape, F32)
    tail = 4 * groups
    dot_all[tail:] = jnp.zeros((dot_all.shape[0] - tail, 16, hw), BF)
    sm[...] = jnp.zeros(sm.shape, F32)
    head, mid = MARGIN // 16, (MARGIN + LP) // 16
    g2b[:head] = jnp.zeros((head, 16, width), BF)
    g2b[mid:] = jnp.zeros((g2b.shape[0] - mid, 16, width), BF)
    cp.wait()
    for dev in peers:
        wait_recv(dot_all.at[pl.ds(dev[1] * groups, groups)], do_s.at[0], do_r.at[dev[1]], dev)
    sc_u1.start()
    pack_rows(dot_all, dop, lens, True)

    dlt = LP // 4

    def deltas(j, carry):
        at = pl.ds(pl.multiple_of(j * dlt, 16), dlt)
        prod = dop[at, :].astype(F32) * ob[at, :].astype(F32)
        lane = iota((dlt, 128), 1)
        out = jnp.zeros((dlt, 128), F32)
        for h in range(nh):
            part_h = jnp.where(head_mask(dlt, hw, h), prod, 0.0)
            out = jnp.where(lane == h, jnp.sum(part_h, axis=-1, keepdims=True), out)
        delta[at, :] = out
        return carry

    lax.fori_loop(0, 4, deltas, 0)
    qkv_copy.wait()

    def back(at, keys, h, limit):
        nrow, nkey = at.size, keys.size
        zero = jnp.zeros((), BF)
        hm = head_mask(nrow, hw, h)
        q = jnp.where(hm, g1b[at, :hw], zero)
        s = dot_nt(q, g1b[keys, 256 : 256 + hw])
        p = jnp.exp2(s * EXP_SCALE - lse[at, h : h + 1])
        if limit is not None:
            p = jnp.where(iota(p.shape, 1) < limit, p, 0.0)
        g = jnp.where(hm, dop[at, :], zero)
        dp = dot_nt(g, g1b[keys, 512 : 512 + hw])
        ds = (p * (dp - delta[at, h : h + 1])).astype(BF)
        sm[keys, 512 : 512 + hw] += dot_tn(p.astype(BF), g)
        sm[keys, 256 : 256 + hw] += dot_tn(ds, q)
        km = jnp.where(head_mask(nkey, hw, h), g1b[keys, 256 : 256 + hw], zero)
        sm[at, :hw] += dot_nn(ds, km)

    for h in range(nh):
        def big(j, carry, h=h):
            back(pl.ds(pl.multiple_of(j * 256, 256), 256), pl.ds(0, BIG), h, None)
            return carry

        lax.fori_loop(0, BIG // 256, big, 0)
        def small(k, carry, h=h):
            at = pl.ds(pl.multiple_of(BIG + k * SMALL, 16), SMALL)
            back(at, at, h, small_length(lens, k))
            return carry

        lax.fori_loop(0, 3, small, 0)
        if h == 0:
            sc_d0.next()
            sc_o.next()
        elif h == 1:
            sc_u0.next()
            sc_d1.next()
        else:
            sc_u1.next()
            sc_d0.next()
            sc_o.next()

    seg = segment_matrix(hw)
    gq = own_heads(gains[4:5, :], pc.t, nt, hw)
    gk = own_heads(gains[5:6, :], pc.t, nt, hw)

    def norms(j, carry):
        at = pl.ds(pl.multiple_of(j * dlt, 16), dlt)
        kept = lse[at, :]
        sums, outs = [], []
        for i, g in enumerate((gq, gk)):
            inv = jnp.broadcast_to(kept[:, 8 * (i + 1) : 8 * (i + 1) + 1], (dlt, hw))
            for k in range(1, nh):
                inv = jnp.where(head_mask(dlt, hw, k), kept[:, 8 * (i + 1) + k : 8 * (i + 1) + k + 1], inv)
            n = g1b[at, i * 256 : i * 256 + hw].astype(F32) / g
            e = sm[at, i * 256 : i * 256 + hw] * 0.125
            c = e * g
            d = inv * (c - segment_mean(c, seg) - n * segment_mean(c * n, seg))
            outs.append(d.astype(BF))
            sums.append(colsum(e * n))
        outs.append(sm[at, 512 : 512 + hw].astype(BF))
        for i, d in enumerate(outs):
            g2b[pl.ds(head + j * (dlt // 16), dlt // 16), :, i * 256 : i * 256 + hw] = d.reshape(dlt // 16, 16, hw)
        return (carry[0] + sums[0], carry[1] + sums[1])

    nones = jnp.zeros((1, hw), F32)
    sum_q, sum_k = lax.fori_loop(0, 4, norms, (nones, nones))
    sc_u0.next()
    sc_d1.next()

    def unpack(i, carry):
        out = unpack_tile(g2b, i * 128, lens)
        g1b[pl.ds(pl.multiple_of(i * 128, 128), 128), :] = out.astype(BF)
        return carry

    lax.fori_loop(0, 16, unpack, 0)
    h1_copy.wait()
    sc_u1.next()
    sc_o.next()

    def project(t, sums):
        def body(j, carry):
            at = pl.ds(pl.multiple_of(t * rows + j * half, half), half)
            total = dot_nt(g1b[at, :hw], wqkv[0])
            total += dot_nt(g1b[at, 256 : 256 + hw], wqkv[1])
            total += dot_nt(g1b[at, 512 : 512 + hw], wqkv[2])
            low = total.astype(BF)
            g2b[pl.ds(t * groups + j * (half // 16), half // 16)] = low.reshape(half // 16, 16, width)
            return (carry[0] + colsum(total * wb[at, :].astype(F32)), carry[1] + colsum(total))

        return lax.fori_loop(0, 2, body, sums)

    def add_groups(t, src):
        def body(j, carry):
            at = pl.ds(t * groups + j * 4, 4)
            g2b[at] = (g2b[at].astype(F32) + src[pl.ds(j * 4, 4)].astype(F32)).astype(BF)
            return carry

        lax.fori_loop(0, groups // 4, body, 0)

    def block_of(t):
        return g2b.at[pl.ds(t * groups, groups)]

    t_fo, t_ff = (1 - pc.y) * 2 + c_other, (1 - pc.y) * 2 + c_me
    t_no = pc.y * 2 + c_other
    sc_q = [scatter("q0", gq0_own, "zx"), scatter("q1", gq1_own, "zx")]

    def attn_grad(piece):
        for q in range(2):
            hq = wb[: nt * rows, q * part_w : (q + 1) * part_w]
            if piece == 0:
                g = dot_tn(hq, g1b[: nt * rows, :512])
                g = jnp.concatenate([g[:, :hw], g[:, 256 : 256 + hw]], axis=1)
            else:
                g = dot_tn(hq, g1b[: nt * rows, 512 : 512 + hw])
            own = (gq0_own, gq1_own)[piece]
            own[q * zblk : (q + 1) * zblk] = g.astype(BF).reshape(zblk, 2, r, g.shape[1])
        sc_q[piece].start()

    sums = project(t_fo, (none, none))
    cps.start(block_of(t_fo), dhr.at[0], dh_s.at[0], dh_r.at[0], core)
    sums = project(t_ff, sums)
    wait_recv(dhr.at[0], dh_s.at[0], dh_r.at[0], core)
    add_groups(t_ff, dhr.at[0])
    cps.start(block_of(t_ff), dhy, dh_s.at[2], dh_r.at[2], pc.rel(dy=1))
    attn_grad(0)
    sums = project(t_no, sums)
    cps.start(block_of(t_no), dhr.at[1], dh_s.at[1], dh_r.at[1], core)
    sum_h, sum_d = project(pc.t, sums)
    attn_grad(1)

    gain_one, shift_one = gains[0:1, :], gains[1:2, :]
    small_out[4:5, :hw] = sum_q
    small_out[5:6, :hw] = sum_k
    placed = pltpu.roll(small_out[...], pc.t * hw, 1)
    small_out[...] = placed
    small_out[0:1, :] = (sum_h - shift_one * sum_d) / gain_one
    small_out[1:2, :] = sum_d
    small_out[2:3, :] = sum_g2
    small_out[3:4, :] = sum_b2
    lane = iota((1, width), 1)
    stat = jnp.zeros((1, width), F32)
    counted = jnp.sum(slot_valid(pc.t, 0, rows))
    for i, v in enumerate((sum_x, sum_a, sum_m, sum_f)):
        stat = jnp.where(lane == i, jnp.sum(v), stat)
    small_out[6:7, :] = jnp.where(lane == 4, counted, stat)
    small_stages = [[dict(dc=1)], [dict(dy=1)], [dict(dx=1)], axis_steps(pc, "z")]
    total = small_out[...]

    def small_send(k, total):
        sm_src[k] = total
        for i, step in enumerate(small_stages[k]):
            cps.start(sm_src.at[k], sm_dst.at[k + i], st_s.at[k + i], st_r.at[k + i], pc.rel(**step))

    def small_add(k, total):
        for i, step in enumerate(small_stages[k]):
            wait_recv(sm_dst.at[k + i], st_s.at[k + i], st_r.at[k + i], pc.rel(**step))
            total = total + sm_dst[k + i]
        return total

    small_send(0, total)
    total = small_add(0, total)
    small_send(1, total)
    for s in sc_q:
        s.next()
    total = small_add(1, total)
    small_send(2, total)
    total = small_add(2, total)
    small_send(3, total)

    wait_recv(dhr.at[1], dh_s.at[1], dh_r.at[1], core)
    add_groups(pc.t, dhr.at[1])
    wait_recv(dhy, dh_s.at[2], dh_r.at[2], pc.rel(dy=1))

    def last(j, carry):
        at = pl.ds(pl.multiple_of(j * 128, 128), 128)
        near = g2b[pl.ds(pc.t * groups + j * 8, 8)].astype(F32)
        e = (near + dhy[pl.ds(j * 8, 8)].astype(F32)).reshape(128, width)
        x = tok[at, :].astype(F32)
        _, n, inv = layer_norm_rows(x, gain_one, 0.0)
        c = e * gain_one
        grad = inv * (
            c - jnp.mean(c, axis=-1, keepdims=True) - n * jnp.mean(c * n, axis=-1, keepdims=True)
        )
        dx_out[at, :] = dx_out[at, :] + grad
        return carry

    lax.fori_loop(0, rows // 128, last, 0)
    small_out[...] = small_add(3, total)
    stat = small_out[6:7, :]
    counted = jnp.sum(jnp.where(lane == 4, stat, 0.0))
    small_out[7:8, :] = jnp.where(lane < 4, jnp.sqrt(stat / (counted * width)), 0.0)

    def store(ref, at=None):
        def put(total):
            if at is None:
                ref[...] = total
            else:
                ref[:, at : at + cut] = total

        return put

    sc_q[0].finish(store(gqk_out))
    sc_q[1].finish(store(gv_out))
    sc_o.finish(lambda v: store(gwo_out)(v.T))
    sc_d0.finish(store(gwd_out, 0))
    sc_d1.finish(store(gwd_out, cut))
    sc_u0.finish(store(gwu_out, 0))
    sc_u1.finish(store(gwu_out, cut))

    def sent(j, carry):
        h2_copy(j, c_me).wait_send()
        back_copy(j, hs, hr, hh_s, hh_r).wait_send()
        back_copy(j, fs, fr_in, f_s, f_r).wait_send()
        return carry

    lax.fori_loop(0, 2, sent, 0)
    cps.finish()


def call_kc(nf, nt, lens, tok, cot, o_own, wo, wqkv, gains, lse, ob, qkv, h1, wu0, wu1, wd0, wd1):
    nz = nf // 2
    rows, width = tok.shape
    hw = ob.shape[1]
    r = width // nf
    cut = width // 2
    orders = dict(
        o=("c", "x", "y", "z"), u0=("x", "y", "z"), u1=("y", "x", "z"),
        d0=("x", "y", "z"), d1=("z", "x", "y"), q0=("x", "z"), q1=("x", "z"),
    )
    S = jax.ShapeDtypeStruct
    V = pltpu.VMEM
    vm = pl.BlockSpec(memory_space=pltpu.VMEM)
    hb = pl.BlockSpec(memory_space=pl.ANY)
    dma = pltpu.SemaphoreType.DMA
    g3 = (MARGIN + LP + 160) // 16
    outs = [
        S((rows, width), BF), S((rows, width), F32), S((r, 2 * hw), F32), S((r, hw), F32), S((hw, r), F32),
        S((r, width), F32), S((r, width), F32), S((8, width), F32),
    ]
    own = (2, nz, 2, r, cut)
    scratch = [
        V((LP, width), F32), V((LP, width), BF), V((g3, 16, width), BF), V((4 * width, width), BF),
        V((rows, 128), F32), V((2, rows, width), BF), V((2, rows, width), BF),
        V((rows, width), BF), V((rows, width), BF), V((2 * rows, width), BF),
        V((rows, width), BF), V((nt, rows // 16, 16, hw), BF),
        V(((nt * rows + 192) // 16, 16, hw), BF), V((LP, hw), BF), V((LP, 128), F32),
        V((2, rows // 16, 16, width), BF), V((rows // 16, 16, width), BF),
        V((nz, 2, r, 2 * hw), BF), V((nz, 2, r, hw), BF), V((4, 8, width), F32), V((2 + nz, 8, width), F32),
        V((2, 2, nz, 2, r, hw), BF), V(own, BF), V(own, BF), V(own, BF), V(own, BF),
        dma((2,)), dma((2,)), dma((1,)), dma((1,)), dma((2,)), dma((2,)), dma((2,)), dma((2,)),
        dma((3,)), dma((nt,)), dma((3,)), dma((3,)), dma((2 + nz,)), dma((2 + nz,)), dma((9,)),
    ]
    for name in ("o", "u0", "u1", "d0", "d1", "q0", "q1"):
        dims = {"o": "yczx", "q0": "zx", "q1": "zx"}.get(name, "yzx")
        block = (r, {"o": hw, "q0": 2 * hw, "q1": hw}.get(name, cut))
        scratch += [V(shape, BF) for shape in landing(nz, dims, orders[name], block)]
        n = sends_of(nz, orders[name])
        scratch += [dma((n,)), dma((n,))]
    return pl.pallas_call(
        functools.partial(kc_kernel, nf, nt, orders),
        out_shape=outs,
        in_specs=[pl.BlockSpec(memory_space=pltpu.SMEM), vm, hb] + [vm] * 6 + [hb] * 6,
        out_specs=[vm] * 8,
        scratch_shapes=scratch,
        compiler_params=pltpu.CompilerParams(
            collective_id=1, has_side_effects=True, vmem_limit_bytes=64 << 20
        ),
    )(lens, tok, cot, o_own, wo, wqkv, gains, lse, ob, qkv, h1, wu0, wu1, wd0, wd1)


def local_fused(nf, nt, args):
    (tokens, lengths, pictures, w_query, w_key, w_value, w_out, w_up, w_down) = args[:9]
    smalls, cotangent = args[9:15], args[15]
    rows, width = tokens.shape[1:]
    hw = w_query.shape[1]
    per = smalls[0].shape[0]
    place = lax.axis_index("fsdp") * nt + lax.axis_index("tp")
    qkv, lse, ob, wqkv, gains, o_own, h1, wo, *halves = call_ka(
        nf, nt, lengths, tokens[0], w_query, w_key, w_value, w_out, w_up, w_down.T, smalls
    )
    result, grad_in, gqk, gv, gwo, gwu, gwd, small = call_kc(
        nf, nt, lengths, tokens[0], cotangent[0], o_own, wo.reshape(nt, width, hw), wqkv, gains, lse, ob,
        qkv, h1.reshape(nt * rows, width),
        *[w.reshape(2, width, width // 2) for w in halves],
    )
    own = lax.dynamic_slice_in_dim(small, place * per, per, 1)
    statistics = small[7, :4]
    return (
        result[None], grad_in[None],
        gqk[:, :hw], gqk[:, hw:], gv, gwo, gwu, gwd.T,
        own[0], own[1], own[2], own[3], own[4], own[5], statistics,
    )


def solution(mesh):
    nf, nt = mesh.shape["fsdp"], mesh.shape["tp"]

    def local(*args):
        tokens, w_query = args[0], args[3]
        if nt == 4 and tokens.shape[0] == 1 and tokens.shape[1] == 512 and w_query.shape[0] % 32 == 0:
            return local_fused(nf, nt, args)
        return local_plain(*args)

    in_specs = (
        P("fsdp", "tp", None),
        P("fsdp", None),
        P("fsdp", None),
        P("fsdp", "tp"),
        P("fsdp", "tp"),
        P("fsdp", "tp"),
        P("tp", "fsdp"),
        P("fsdp", "tp"),
        P("tp", "fsdp"),
        P(("fsdp", "tp")),
        P(("fsdp", "tp")),
        P(("fsdp", "tp")),
        P(("fsdp", "tp")),
        P(("fsdp", "tp")),
        P(("fsdp", "tp")),
        P("fsdp", "tp", None),
    )
    out_specs = (
        P("fsdp", "tp", None),
        P("fsdp", "tp", None),
        P("fsdp", "tp"),
        P("fsdp", "tp"),
        P("fsdp", "tp"),
        P("tp", "fsdp"),
        P("fsdp", "tp"),
        P("tp", "fsdp"),
        P(("fsdp", "tp")),
        P(("fsdp", "tp")),
        P(("fsdp", "tp")),
        P(("fsdp", "tp")),
        P(("fsdp", "tp")),
        P(("fsdp", "tp")),
        P(),
    )
    return jax.shard_map(local, mesh=mesh, in_specs=in_specs, out_specs=out_specs, check_vma=False)
```
